512 devices in a mesh: grp: 16 (over z), seq: 32 (over y, x, core).
Axes of the slice: x: 4, y: 4, z: 16, core: 2. Of those that a mesh axis runs over, the one named last changes fastest.
Arguments:
- queries: bfloat16 [32, 1024, 128], P('seq'), may hold values from -8 to 8
- scene_keys: bfloat16 [65536, 2048], P(('grp', 'seq')), may hold values from -8 to 8
- scene_values: bfloat16 [65536, 2048], P(('grp', 'seq')), may hold values from -6 to 6
- grad_output: bfloat16 [32, 1024, 128], P('seq'), may hold values from -6 to 6
- tile_list: int32 [16, 32, 9, 2], P('grp', 'seq'), may hold values from 0 to 7, as said below
- tile_counts: int32 [16, 32], P('grp', 'seq'), may hold values from 2 to 9, as said below
Outputs:
- attended: bfloat16 [32, 1024, 128], P('seq')
- grad_queries: bfloat16 [32, 1024, 128], P('seq')
- grad_keys: bfloat16 [65536, 2048], P(('grp', 'seq'))
- grad_values: bfloat16 [65536, 2048], P(('grp', 'seq'))
The draws below stay inside these ranges and needn't reach their ends.
Inputs may be any that keep to these rules, and one draw needn't show every extreme that they name: For each group g and item i: every one of the 2 query blocks appears in at least one of the first tile_counts[g, i] entries; some group and item list 9 tiles and some list 2. The first tile_counts[g, i] entries of tile_list[g, i] are distinct pairs (query block below 2, key block below 8) in no particular order; the later entries are unused.
All inputs are finite; a program needn't handle non-finite values.
Results may differ from the reference program's by a relative error of at most 0.024.
Values may be sent and summed in bfloat16 or wider, within the bound.
A program may use at most 64 MiB of HBM per device.

```python
import jax
import jax.numpy as jnp
from jax import lax

HEADS = 16
HEAD_DIM = 128
QPARTS = 2
QBLK = 512
KBLK = 512
QPART = 1024
ITEMS = 32
GROUPS = 16
SCENE = 65536
QBLOCKS = 2
KBLOCKS = 8
LIST = 9


def tile_plan(key):
    base_key = jax.random.fold_in(key, 11)
    pieces = jax.random.split(base_key, 7)
    total_slots = GROUPS * ITEMS
    load_first = jax.random.randint(pieces[0], (GROUPS, ITEMS), 0, 1024)
    load_second = jax.random.randint(pieces[1], (GROUPS, 1), 0, 1024)
    extra_tiles = (LIST - QBLOCKS) * load_first * load_second // (1023 * 1023)
    flat_counts = (QBLOCKS + extra_tiles).reshape(total_slots)
    heavy_slot = jax.random.randint(pieces[2], (), 0, total_slots)
    light_slot = (heavy_slot + 1 + jax.random.randint(pieces[3], (), 0, max(total_slots - 1, 1))) % total_slots
    slot_index = jnp.arange(total_slots)
    flat_counts = jnp.where(slot_index == heavy_slot, LIST, flat_counts)
    flat_counts = jnp.where(slot_index == light_slot, QBLOCKS, flat_counts)
    tile_counts = flat_counts.reshape(GROUPS, ITEMS)
    every_tile = QBLOCKS * KBLOCKS
    anchors = jax.random.randint(pieces[4], (GROUPS, ITEMS, QBLOCKS), 0, KBLOCKS)
    cells = jnp.arange(every_tile)
    cell_query = cells // KBLOCKS
    cell_key = cells % KBLOCKS
    anchor_cell = anchors[:, :, cell_query]
    is_anchor = anchor_cell == cell_key[None, None, :]
    noise = jax.random.randint(pieces[5], (GROUPS, ITEMS, every_tile), 0, 1 << 20)
    ranking = noise * every_tile + cells + jnp.where(is_anchor, 1 << 28, 0)
    order = jnp.argsort(-ranking, axis=-1)[..., :LIST]
    positions = jnp.arange(LIST)
    live_slot = positions[None, None, :] < tile_counts[..., None]
    mixer = jax.random.randint(pieces[6], (GROUPS, ITEMS, LIST), 0, 1 << 20) * LIST + positions
    mixer = jnp.where(live_slot, mixer, (1 << 30) + positions)
    shuffle = jnp.argsort(mixer, axis=-1)
    chosen = jnp.take_along_axis(order, shuffle, axis=-1)
    paired = jnp.stack([chosen // KBLOCKS, chosen % KBLOCKS], axis=-1)
    paired = jnp.where(live_slot[..., None], paired, 0)
    return (tile_counts.astype(jnp.int32), paired.astype(jnp.int32))


def draw_tile_list(key, part):
    return tile_plan(key)[1]


def draw_tile_counts(key, part):
    return tile_plan(key)[0]


def draw_queries(key, part):
    shape_full = (ITEMS, QPART, HEAD_DIM)
    values_drawn = jnp.clip(3.0 * jax.random.normal(jax.random.fold_in(key, 31), shape_full, jnp.float32), -8.0, 8.0)
    return values_drawn.astype(jnp.bfloat16)


def draw_scene_keys(key, part):
    shape_full = (SCENE, HEADS * HEAD_DIM)
    values_drawn = jnp.clip(jax.random.normal(jax.random.fold_in(key, 41), shape_full, jnp.float32), -6.0, 6.0)
    return values_drawn.astype(jnp.bfloat16)


def block_scale(own_key, dims, cuts, least, largest):
    def one(axis_at, shards_of):
        steps = jax.random.uniform(jax.random.fold_in(jax.random.fold_in(own_key, 6), axis_at), (shards_of,), jnp.float32, least / len(cuts), largest / len(cuts))
        return jnp.repeat(jnp.exp(steps), dims[axis_at] // shards_of).reshape((-1,) + (1,) * (len(dims) - axis_at - 1))

    factor_of = one(*cuts[0])
    for cut in cuts[1:]:
        factor_of = factor_of * one(*cut)
    return factor_of


def scatter_about(rng, shape, width, limit, cuts=(), held_as=jnp.bfloat16):
    level = block_scale(rng, shape, cuts, -0.22, 0.18) if cuts else 1.0
    entries = jax.random.normal(rng, shape, jnp.float32) * width * level
    return jnp.minimum(jnp.maximum(entries, -limit), limit).astype(held_as)


def setup_inputs(seed: int = 0) -> dict:
    keys = jax.random.split(jax.random.key(seed), 7)
    queries = draw_queries(jax.random.fold_in(keys[6], 71), 0)
    scene_keys = draw_scene_keys(jax.random.fold_in(keys[6], 71), 0)
    scene_values = scatter_about(keys[2], (SCENE, HEADS * HEAD_DIM), 1.0, 6.0, ((0, 512),))
    grad_output = scatter_about(keys[3], (ITEMS, QPART, HEAD_DIM), 1.0, 6.0, ((0, 32),))
    tile_list = draw_tile_list(jax.random.fold_in(keys[6], 71), 0)
    tile_counts = draw_tile_counts(jax.random.fold_in(keys[6], 71), 0)
    return dict(queries=queries, scene_keys=scene_keys, scene_values=scene_values, grad_output=grad_output, tile_list=tile_list, tile_counts=tile_counts)


def tile_allowed(tile_list, tile_counts):
    every_tile = QBLOCKS * KBLOCKS
    cell_index = tile_list[..., 0] * KBLOCKS + tile_list[..., 1]
    live_slot = jnp.arange(LIST, dtype=jnp.int32)[None, None, :] < tile_counts[..., None]
    matched = (cell_index[..., None] == jnp.arange(every_tile, dtype=jnp.int32)) & live_slot[..., None]
    return jnp.any(matched, axis=2).reshape(GROUPS, ITEMS, QBLOCKS, KBLOCKS)


def reference(queries, scene_keys, scene_values, grad_output, tile_list, tile_counts):
    softmax_scale = HEAD_DIM ** -0.5
    allowed = tile_allowed(tile_list, tile_counts)
    allowed = allowed.reshape(GROUPS, HEADS, QPARTS, QBLOCKS, KBLOCKS).transpose(1, 2, 3, 0, 4)
    key_heads = scene_keys.reshape(SCENE, HEADS, HEAD_DIM).transpose(1, 0, 2)
    value_heads = scene_values.reshape(SCENE, HEADS, HEAD_DIM).transpose(1, 0, 2)
    query_heads = queries.reshape(HEADS, QPARTS, QPART, HEAD_DIM)
    grad_heads = grad_output.reshape(HEADS, QPARTS, QPART, HEAD_DIM)

    def per_head(inputs):
        query_all, grad_all, allow_all, key_head, value_head = inputs
        outputs = []
        query_grads = []
        key_total = jnp.zeros((SCENE, HEAD_DIM), jnp.float32)
        value_total = jnp.zeros((SCENE, HEAD_DIM), jnp.float32)
        for half_index in range(QPARTS):
            query_item = query_all[half_index]
            grad_item = grad_all[half_index]
            block_mask = allow_all[half_index]
            full_mask = jnp.repeat(jnp.repeat(block_mask, QBLK, axis=0), KBLK, axis=2).reshape(QPART, SCENE)
            scores = jnp.dot(query_item, key_head.T, preferred_element_type=jnp.float32) * softmax_scale
            row_max = jnp.max(jnp.where(full_mask, scores, -jnp.inf), axis=1, keepdims=True)
            weights = jnp.where(full_mask, jnp.exp(scores - row_max), 0.0)
            row_total = jnp.sum(weights, axis=1, keepdims=True)
            attended = (jnp.dot(weights.astype(jnp.bfloat16), value_head, preferred_element_type=jnp.float32) / row_total).astype(jnp.bfloat16)
            log_total = row_max + jnp.log(row_total)
            deltas = jnp.sum(attended.astype(jnp.float32) * grad_item.astype(jnp.float32), axis=1, keepdims=True)
            probs = jnp.where(full_mask, jnp.exp(scores - log_total), 0.0)
            prob_grad = jnp.dot(grad_item, value_head.T, preferred_element_type=jnp.float32)
            score_grad = (probs * (prob_grad - deltas)).astype(jnp.bfloat16)
            query_grad = (jnp.dot(score_grad, key_head, preferred_element_type=jnp.float32) * softmax_scale).astype(jnp.bfloat16)
            key_part = (jnp.dot(score_grad.T, query_item, preferred_element_type=jnp.float32) * softmax_scale).astype(jnp.bfloat16)
            value_part = jnp.dot(probs.astype(jnp.bfloat16).T, grad_item, preferred_element_type=jnp.float32).astype(jnp.bfloat16)
            key_total = key_total + key_part.astype(jnp.float32)
            value_total = value_total + value_part.astype(jnp.float32)
            outputs.append(attended)
            query_grads.append(query_grad)
        return jnp.stack(outputs), jnp.stack(query_grads), key_total.astype(jnp.bfloat16), value_total.astype(jnp.bfloat16)

    attended, grad_queries, key_grads, value_grads = lax.map(per_head, (query_heads, grad_heads, allowed, key_heads, value_heads))
    attended = attended.reshape(ITEMS, QPART, HEAD_DIM)
    grad_queries = grad_queries.reshape(ITEMS, QPART, HEAD_DIM)
    grad_keys = key_grads.transpose(1, 0, 2).reshape(SCENE, HEADS * HEAD_DIM)
    grad_values = value_grads.transpose(1, 0, 2).reshape(SCENE, HEADS * HEAD_DIM)
    return (attended, grad_queries, grad_keys, grad_values)
```

```python
import jax
import jax.numpy as jnp
from jax import lax
from jax.sharding import PartitionSpec as P

QPARTS = 2
QBLK = 512
KBLK = 512


NEG_START = -1e30


def tile_scores(query_block, key_block, softmax_scale):
    return (
        lax.dot_general(
            query_block, key_block, (((1,), (1,)), ((), ())), preferred_element_type=jnp.float32
        )
        * softmax_scale
    )


def forward_item(query_item, key_head, value_head, listing, live_tiles, softmax_scale):
    query_rows = query_item.shape[0]
    head_width = query_item.shape[1]

    def forward_visit_tile(position, running):
        run_max, run_total, run_accum = running
        query_start = listing[position, 0] * QBLK
        key_start = listing[position, 1] * KBLK
        query_block = lax.dynamic_slice_in_dim(query_item, query_start, QBLK, 0)
        key_block = lax.dynamic_slice_in_dim(key_head, key_start, KBLK, 0)
        value_block = lax.dynamic_slice_in_dim(value_head, key_start, KBLK, 0)
        scores = tile_scores(query_block, key_block, softmax_scale)
        old_max = lax.dynamic_slice_in_dim(run_max, query_start, QBLK, 0)
        old_total = lax.dynamic_slice_in_dim(run_total, query_start, QBLK, 0)
        old_accum = lax.dynamic_slice_in_dim(run_accum, query_start, QBLK, 0)
        new_max = jnp.maximum(old_max, jnp.max(scores, axis=1))
        weights = jnp.exp(scores - new_max[:, None])
        shrink = jnp.exp(old_max - new_max)
        new_total = old_total * shrink + jnp.sum(weights, axis=1)
        new_accum = old_accum * shrink[:, None] + jnp.dot(
            weights.astype(jnp.bfloat16), value_block, preferred_element_type=jnp.float32
        )
        run_max = lax.dynamic_update_slice_in_dim(run_max, new_max, query_start, 0)
        run_total = lax.dynamic_update_slice_in_dim(run_total, new_total, query_start, 0)
        run_accum = lax.dynamic_update_slice_in_dim(run_accum, new_accum, query_start, 0)
        return (run_max, run_total, run_accum)

    initial = (
        jnp.full((query_rows,), NEG_START, jnp.float32),
        jnp.zeros((query_rows,), jnp.float32),
        jnp.zeros((query_rows, head_width), jnp.float32),
    )
    return lax.fori_loop(0, live_tiles, forward_visit_tile, initial)


def backward_item(
    query_item,
    key_head,
    value_head,
    grad_item,
    log_total,
    deltas,
    listing,
    live_tiles,
    softmax_scale,
):
    query_rows = query_item.shape[0]
    head_width = query_item.shape[1]
    key_rows = key_head.shape[0]

    def backward_visit_tile(position, running):
        query_grad, key_grad, value_grad = running
        query_start = listing[position, 0] * QBLK
        key_start = listing[position, 1] * KBLK
        query_block = lax.dynamic_slice_in_dim(query_item, query_start, QBLK, 0)
        grad_block = lax.dynamic_slice_in_dim(grad_item, query_start, QBLK, 0)
        key_block = lax.dynamic_slice_in_dim(key_head, key_start, KBLK, 0)
        value_block = lax.dynamic_slice_in_dim(value_head, key_start, KBLK, 0)
        log_block = lax.dynamic_slice_in_dim(log_total, query_start, QBLK, 0)
        delta_block = lax.dynamic_slice_in_dim(deltas, query_start, QBLK, 0)
        scores = tile_scores(query_block, key_block, softmax_scale)
        probs = jnp.exp(scores - log_block[:, None])
        probs_half = probs.astype(jnp.bfloat16)
        value_term = lax.dot_general(
            probs_half, grad_block, (((0,), (0,)), ((), ())), preferred_element_type=jnp.float32
        )
        prob_grad = lax.dot_general(
            grad_block, value_block, (((1,), (1,)), ((), ())), preferred_element_type=jnp.float32
        )
        score_grad = (probs * (prob_grad - delta_block[:, None])).astype(jnp.bfloat16)
        query_term = (
            jnp.dot(score_grad, key_block, preferred_element_type=jnp.float32) * softmax_scale
        )
        key_term = (
            lax.dot_general(
                score_grad,
                query_block,
                (((0,), (0,)), ((), ())),
                preferred_element_type=jnp.float32,
            )
            * softmax_scale
        )
        query_grad = lax.dynamic_update_slice_in_dim(
            query_grad,
            lax.dynamic_slice_in_dim(query_grad, query_start, QBLK, 0) + query_term,
            query_start,
            0,
        )
        key_grad = lax.dynamic_update_slice_in_dim(
            key_grad,
            lax.dynamic_slice_in_dim(key_grad, key_start, KBLK, 0) + key_term,
            key_start,
            0,
        )
        value_grad = lax.dynamic_update_slice_in_dim(
            value_grad,
            lax.dynamic_slice_in_dim(value_grad, key_start, KBLK, 0) + value_term,
            key_start,
            0,
        )
        return (query_grad, key_grad, value_grad)

    initial = (
        jnp.zeros((query_rows, head_width), jnp.float32),
        jnp.zeros((key_rows, head_width), jnp.float32),
        jnp.zeros((key_rows, head_width), jnp.float32),
    )
    return lax.fori_loop(0, live_tiles, backward_visit_tile, initial)


def scatter_rows(rows, parts):
    return lax.all_to_all(
        rows.reshape(parts, rows.shape[0] // parts, rows.shape[1]),
        "grp",
        split_axis=0,
        concat_axis=0,
        tiled=True,
    )


def broadcast_rows(chunk, parts):
    spread = jnp.broadcast_to(chunk[None], (parts,) + chunk.shape)
    gathered = lax.all_to_all(spread, "grp", split_axis=0, concat_axis=0, tiled=True)
    return gathered.reshape(parts * chunk.shape[0], chunk.shape[1])


def per_device(queries, scene_keys, scene_values, grad_output, tile_list, tile_counts):
    items_here = queries.shape[0]
    head_width = queries.shape[2]
    query_rows = queries.shape[1]
    scene_here = scene_keys.shape[0]
    heads_total = scene_keys.shape[1] // head_width
    seq_devices = lax.axis_size("seq")
    groups = lax.axis_size("grp")
    chunk_rows = query_rows // groups
    group_keys = scene_here * seq_devices
    copies = max(1, QPARTS // items_here)
    heads_here = max(1, items_here // QPARTS)
    softmax_scale = head_width ** (-0.5)
    key_wide = jnp.repeat(
        scene_keys.reshape(scene_here, heads_total, head_width), copies, axis=1
    ).reshape(scene_here, -1)
    value_wide = jnp.repeat(
        scene_values.reshape(scene_here, heads_total, head_width), copies, axis=1
    ).reshape(scene_here, -1)
    key_group, value_group = (
        lax.all_to_all(key_wide, "seq", split_axis=1, concat_axis=0, tiled=True),
        lax.all_to_all(value_wide, "seq", split_axis=1, concat_axis=0, tiled=True),
    )
    key_group = key_group.reshape(group_keys, heads_here, head_width)
    value_group = value_group.reshape(group_keys, heads_here, head_width)
    part_max, part_total, part_accum = forward_item(
        queries[0],
        key_group[:, 0, :],
        value_group[:, 0, :],
        tile_list[0, 0],
        tile_counts[0, 0],
        softmax_scale,
    )
    stats = jnp.concatenate(
        [part_max.reshape(groups, 1, chunk_rows), part_total.reshape(groups, 1, chunk_rows)],
        axis=2,
    )
    packed = jnp.concatenate([part_accum.reshape(groups, chunk_rows, head_width), stats], axis=1)
    arrived = scatter_rows(packed.reshape(groups * (chunk_rows + 1), head_width), groups)
    arrived = arrived.reshape(groups, chunk_rows + 1, head_width)
    got_accum = arrived[:, :chunk_rows, :]
    got_max = arrived[:, chunk_rows, :chunk_rows]
    got_total = arrived[:, chunk_rows, chunk_rows:]
    top = jnp.max(got_max, axis=0)
    shrink = jnp.exp(got_max - top[None, :])
    chunk_total = jnp.sum(got_total * shrink, axis=0)
    chunk_accum = jnp.sum(got_accum * shrink[:, :, None], axis=0)
    chunk_out = (chunk_accum / chunk_total[:, None]).astype(jnp.bfloat16)
    chunk_log = top + jnp.log(chunk_total)
    log_row = jnp.concatenate([chunk_log, jnp.zeros((chunk_rows,), jnp.float32)])
    back = broadcast_rows(
        jnp.concatenate([chunk_out.astype(jnp.float32), log_row[None, :]], axis=0), groups
    ).reshape(groups, chunk_rows + 1, head_width)
    attended = back[:, :chunk_rows, :].reshape(1, query_rows, head_width).astype(jnp.bfloat16)
    log_total = back[:, chunk_rows, :chunk_rows].reshape(1, query_rows)
    deltas = jnp.sum(attended.astype(jnp.float32) * grad_output.astype(jnp.float32), axis=2)
    query_grad, key_grad, value_grad = backward_item(
        queries[0],
        key_group[:, 0, :],
        value_group[:, 0, :],
        grad_output[0],
        log_total[0],
        deltas[0],
        tile_list[0, 0],
        tile_counts[0, 0],
        softmax_scale,
    )
    key_stack = key_grad.astype(jnp.bfloat16)[:, None, :]
    value_stack = value_grad.astype(jnp.bfloat16)[:, None, :]
    key_back, value_back = (
        lax.all_to_all(
            key_stack.reshape(group_keys, -1), "seq", split_axis=0, concat_axis=1, tiled=True
        ),
        lax.all_to_all(
            value_stack.reshape(group_keys, -1), "seq", split_axis=0, concat_axis=1, tiled=True
        ),
    )
    grad_keys = (
        jnp.sum(
            key_back.reshape(scene_here, heads_total, copies, head_width).astype(jnp.float32),
            axis=2,
        )
        .astype(jnp.bfloat16)
        .reshape(scene_here, -1)
    )
    grad_values = (
        jnp.sum(
            value_back.reshape(scene_here, heads_total, copies, head_width).astype(jnp.float32),
            axis=2,
        )
        .astype(jnp.bfloat16)
        .reshape(scene_here, -1)
    )
    query_parts = scatter_rows(query_grad, groups)
    query_chunk = jnp.sum(query_parts, axis=0).astype(jnp.bfloat16)
    grad_queries = broadcast_rows(query_chunk, groups).reshape(1, query_rows, head_width)
    return (attended, grad_queries, grad_keys, grad_values)


def solution(mesh):
    in_specs = (
        P("seq", None, None),
        P(("grp", "seq"), None),
        P(("grp", "seq"), None),
        P("seq", None, None),
        P("grp", "seq", None, None),
        P("grp", "seq"),
    )
    out_specs = (
        P("seq", None, None),
        P("seq", None, None),
        P(("grp", "seq"), None),
        P(("grp", "seq"), None),
    )
    return jax.shard_map(
        per_device, mesh=mesh, in_specs=in_specs, out_specs=out_specs, check_vma=False
    )
```

```python
import jax
import jax.numpy as jnp
from jax import lax
from jax.sharding import PartitionSpec as P

QPARTS = 2
QBLK = 512
KBLK = 512


NEG_START = -1e30


def tile_scores(query_block, key_block, softmax_scale):
    return (
        lax.dot_general(
            query_block, key_block, (((1,), (1,)), ((), ())), preferred_element_type=jnp.float32
        )
        * softmax_scale
    )


def forward_item(query_item, key_head, value_head, listing, live_tiles, softmax_scale):
    query_rows = query_item.shape[0]
    head_width = query_item.shape[1]

    def forward_visit_tile(position, running):
        run_max, run_total, run_accum = running
        query_start = listing[position, 0] * QBLK
        key_start = listing[position, 1] * KBLK
        query_block = lax.dynamic_slice_in_dim(query_item, query_start, QBLK, 0)
        key_block = lax.dynamic_slice_in_dim(key_head, key_start, KBLK, 0)
        value_block = lax.dynamic_slice_in_dim(value_head, key_start, KBLK, 0)
        scores = tile_scores(query_block, key_block, softmax_scale)
        old_max = lax.dynamic_slice_in_dim(run_max, query_start, QBLK, 0)
        old_total = lax.dynamic_slice_in_dim(run_total, query_start, QBLK, 0)
        old_accum = lax.dynamic_slice_in_dim(run_accum, query_start, QBLK, 0)
        new_max = jnp.maximum(old_max, jnp.max(scores, axis=1))
        new_max = new_max.astype(jnp.bfloat16).astype(jnp.float32)
        weights = jnp.exp(scores - new_max[:, None])
        shrink = jnp.exp(old_max - new_max)
        new_total = old_total * shrink + jnp.sum(weights, axis=1)
        new_accum = old_accum * shrink[:, None] + jnp.dot(
            weights.astype(jnp.bfloat16), value_block, preferred_element_type=jnp.float32
        )
        run_max = lax.dynamic_update_slice_in_dim(run_max, new_max, query_start, 0)
        run_total = lax.dynamic_update_slice_in_dim(run_total, new_total, query_start, 0)
        run_accum = lax.dynamic_update_slice_in_dim(run_accum, new_accum, query_start, 0)
        return (run_max, run_total, run_accum)

    initial = (
        jnp.full((query_rows,), NEG_START, jnp.float32),
        jnp.zeros((query_rows,), jnp.float32),
        jnp.zeros((query_rows, head_width), jnp.float32),
    )
    return lax.fori_loop(0, live_tiles, forward_visit_tile, initial)


def backward_item(
    query_item,
    key_head,
    value_head,
    grad_item,
    log_total,
    deltas,
    listing,
    live_tiles,
    softmax_scale,
):
    query_rows = query_item.shape[0]
    head_width = query_item.shape[1]
    key_rows = key_head.shape[0]

    def backward_visit_tile(position, running):
        query_grad, key_grad, value_grad = running
        query_start = listing[position, 0] * QBLK
        key_start = listing[position, 1] * KBLK
        query_block = lax.dynamic_slice_in_dim(query_item, query_start, QBLK, 0)
        grad_block = lax.dynamic_slice_in_dim(grad_item, query_start, QBLK, 0)
        key_block = lax.dynamic_slice_in_dim(key_head, key_start, KBLK, 0)
        value_block = lax.dynamic_slice_in_dim(value_head, key_start, KBLK, 0)
        log_block = lax.dynamic_slice_in_dim(log_total, query_start, QBLK, 0)
        delta_block = lax.dynamic_slice_in_dim(deltas, query_start, QBLK, 0)
        scores = tile_scores(query_block, key_block, softmax_scale)
        probs = jnp.exp(scores - log_block[:, None])
        probs_half = probs.astype(jnp.bfloat16)
        value_term = lax.dot_general(
            probs_half, grad_block, (((0,), (0,)), ((), ())), preferred_element_type=jnp.float32
        )
        prob_grad = lax.dot_general(
            grad_block, value_block, (((1,), (1,)), ((), ())), preferred_element_type=jnp.float32
        )
        score_grad = (probs * (prob_grad - delta_block[:, None])).astype(jnp.bfloat16)
        query_term = (
            jnp.dot(score_grad, key_block, preferred_element_type=jnp.float32) * softmax_scale
        )
        key_term = (
            lax.dot_general(
                score_grad,
                query_block,
                (((0,), (0,)), ((), ())),
                preferred_element_type=jnp.float32,
            )
            * softmax_scale
        )
        query_grad = lax.dynamic_update_slice_in_dim(
            query_grad,
            lax.dynamic_slice_in_dim(query_grad, query_start, QBLK, 0) + query_term,
            query_start,
            0,
        )
        key_grad = lax.dynamic_update_slice_in_dim(
            key_grad,
            lax.dynamic_slice_in_dim(key_grad, key_start, KBLK, 0) + key_term,
            key_start,
            0,
        )
        value_grad = lax.dynamic_update_slice_in_dim(
            value_grad,
            lax.dynamic_slice_in_dim(value_grad, key_start, KBLK, 0) + value_term,
            key_start,
            0,
        )
        return (query_grad, key_grad, value_grad)

    initial = (
        jnp.zeros((query_rows, head_width), jnp.float32),
        jnp.zeros((key_rows, head_width), jnp.float32),
        jnp.zeros((key_rows, head_width), jnp.float32),
    )
    return lax.fori_loop(0, live_tiles, backward_visit_tile, initial)


def scatter_rows(rows, parts):
    return lax.all_to_all(
        rows.reshape(parts, rows.shape[0] // parts, rows.shape[1]),
        "grp",
        split_axis=0,
        concat_axis=0,
        tiled=True,
    )


def broadcast_rows(chunk, parts):
    spread = jnp.broadcast_to(chunk[None], (parts,) + chunk.shape)
    gathered = lax.all_to_all(spread, "grp", split_axis=0, concat_axis=0, tiled=True)
    return gathered.reshape(parts * chunk.shape[0], chunk.shape[1])


def per_device(queries, scene_keys, scene_values, grad_output, tile_list, tile_counts):
    items_here = queries.shape[0]
    head_width = queries.shape[2]
    query_rows = queries.shape[1]
    scene_here = scene_keys.shape[0]
    heads_total = scene_keys.shape[1] // head_width
    seq_devices = lax.axis_size("seq")
    groups = lax.axis_size("grp")
    chunk_rows = query_rows // groups
    group_keys = scene_here * seq_devices
    copies = max(1, QPARTS // items_here)
    heads_here = max(1, items_here // QPARTS)
    softmax_scale = head_width ** (-0.5)
    key_wide = jnp.repeat(
        scene_keys.reshape(scene_here, heads_total, head_width), copies, axis=1
    ).reshape(scene_here, -1)
    value_wide = jnp.repeat(
        scene_values.reshape(scene_here, heads_total, head_width), copies, axis=1
    ).reshape(scene_here, -1)
    key_group, value_group = (
        lax.all_to_all(key_wide, "seq", split_axis=1, concat_axis=0, tiled=True),
        lax.all_to_all(value_wide, "seq", split_axis=1, concat_axis=0, tiled=True),
    )
    key_group = key_group.reshape(group_keys, heads_here, head_width)
    value_group = value_group.reshape(group_keys, heads_here, head_width)
    part_max, part_total, part_accum = forward_item(
        queries[0],
        key_group[:, 0, :],
        value_group[:, 0, :],
        tile_list[0, 0],
        tile_counts[0, 0],
        softmax_scale,
    )
    total_hi = part_total.astype(jnp.bfloat16)
    total_lo = (part_total - total_hi.astype(jnp.float32)).astype(jnp.bfloat16)
    stats = jnp.stack(
        [
            jnp.concatenate(
                [part_max.astype(jnp.bfloat16).reshape(groups, chunk_rows), total_hi.reshape(groups, chunk_rows)],
                axis=1,
            ),
            jnp.concatenate(
                [total_lo.reshape(groups, chunk_rows), jnp.zeros((groups, chunk_rows), jnp.bfloat16)],
                axis=1,
            ),
        ],
        axis=1,
    )
    packed = jnp.concatenate(
        [part_accum.astype(jnp.bfloat16).reshape(groups, chunk_rows, head_width), stats], axis=1
    )
    arrived = scatter_rows(packed.reshape(groups * (chunk_rows + 2), head_width), groups)
    arrived = arrived.reshape(groups, chunk_rows + 2, head_width).astype(jnp.float32)
    got_accum = arrived[:, :chunk_rows, :]
    got_max = arrived[:, chunk_rows, :chunk_rows]
    got_total = arrived[:, chunk_rows, chunk_rows:] + arrived[:, chunk_rows + 1, :chunk_rows]
    top = jnp.max(got_max, axis=0)
    shrink = jnp.exp(got_max - top[None, :])
    chunk_total = jnp.sum(got_total * shrink, axis=0)
    chunk_accum = jnp.sum(got_accum * shrink[:, :, None], axis=0)
    chunk_out = (chunk_accum / chunk_total[:, None]).astype(jnp.bfloat16)
    chunk_hi = chunk_total.astype(jnp.bfloat16)
    chunk_lo = (chunk_total - chunk_hi.astype(jnp.float32)).astype(jnp.bfloat16)
    chunk_stats = jnp.stack(
        [
            jnp.concatenate([top.astype(jnp.bfloat16), chunk_hi]),
            jnp.concatenate([chunk_lo, jnp.zeros((chunk_rows,), jnp.bfloat16)]),
        ]
    )
    back = broadcast_rows(jnp.concatenate([chunk_out, chunk_stats], axis=0), groups)
    back = back.reshape(groups, chunk_rows + 2, head_width)
    attended = back[:, :chunk_rows, :].reshape(1, query_rows, head_width)
    back_stats = back[:, chunk_rows:, :].astype(jnp.float32)
    row_top = back_stats[:, 0, :chunk_rows].reshape(1, query_rows)
    row_total = (back_stats[:, 0, chunk_rows:] + back_stats[:, 1, :chunk_rows]).reshape(1, query_rows)
    log_total = row_top + jnp.log(row_total)
    deltas = jnp.sum(attended.astype(jnp.float32) * grad_output.astype(jnp.float32), axis=2)
    query_grad, key_grad, value_grad = backward_item(
        queries[0],
        key_group[:, 0, :],
        value_group[:, 0, :],
        grad_output[0],
        log_total[0],
        deltas[0],
        tile_list[0, 0],
        tile_counts[0, 0],
        softmax_scale,
    )
    key_stack = key_grad.astype(jnp.bfloat16)[:, None, :]
    value_stack = value_grad.astype(jnp.bfloat16)[:, None, :]
    key_back, value_back = (
        lax.all_to_all(
            key_stack.reshape(group_keys, -1), "seq", split_axis=0, concat_axis=1, tiled=True
        ),
        lax.all_to_all(
            value_stack.reshape(group_keys, -1), "seq", split_axis=0, concat_axis=1, tiled=True
        ),
    )
    grad_keys = (
        jnp.sum(
            key_back.reshape(scene_here, heads_total, copies, head_width).astype(jnp.float32),
            axis=2,
        )
        .astype(jnp.bfloat16)
        .reshape(scene_here, -1)
    )
    grad_values = (
        jnp.sum(
            value_back.reshape(scene_here, heads_total, copies, head_width).astype(jnp.float32),
            axis=2,
        )
        .astype(jnp.bfloat16)
        .reshape(scene_here, -1)
    )
    query_parts = scatter_rows(query_grad.astype(jnp.bfloat16), groups)
    query_chunk = jnp.sum(query_parts.astype(jnp.float32), axis=0).astype(jnp.bfloat16)
    grad_queries = broadcast_rows(query_chunk, groups).reshape(1, query_rows, head_width)
    return (attended, grad_queries, grad_keys, grad_values)


def solution(mesh):
    in_specs = (
        P("seq", None, None),
        P(("grp", "seq"), None),
        P(("grp", "seq"), None),
        P("seq", None, None),
        P("grp", "seq", None, None),
        P("grp", "seq"),
    )
    out_specs = (
        P("seq", None, None),
        P("seq", None, None),
        P(("grp", "seq"), None),
        P(("grp", "seq"), None),
    )
    return jax.shard_map(
        per_device, mesh=mesh, in_specs=in_specs, out_specs=out_specs, check_vma=False
    )
```

```python
import jax
import jax.numpy as jnp
from jax import lax
from jax.experimental import pallas as pl
from jax.experimental.pallas import tpu as pltpu
from jax.sharding import PartitionSpec as P

QPARTS = 2
QBLK = 512
KBLK = 512


NEG_START = -1e30


LIST_SLOTS = 9


def tile_starts(list_ref, position):
    query_block = jnp.clip(list_ref[position, 0], 0, QPARTS - 1)
    key_block = jnp.clip(list_ref[position, 1], 0, 7)
    return (
        pl.multiple_of(query_block * QBLK, QBLK),
        pl.multiple_of(key_block * KBLK, KBLK),
    )


def forward_kernel(softmax_scale, list_ref, count_ref, q_ref, k_ref, v_ref, max_ref, total_ref, accum_ref):
    max_ref[...] = jnp.full(max_ref.shape, NEG_START, jnp.float32)
    total_ref[...] = jnp.zeros(total_ref.shape, jnp.float32)
    accum_ref[...] = jnp.zeros(accum_ref.shape, jnp.float32)
    live_tiles = jnp.clip(count_ref[0], 0, LIST_SLOTS)

    def visit(position, carry):
        query_start, key_start = tile_starts(list_ref, position)
        rows = pl.ds(query_start, QBLK)
        keys = pl.ds(key_start, KBLK)
        scores = (
            lax.dot_general(
                q_ref[rows, :], k_ref[keys, :], (((1,), (1,)), ((), ())),
                preferred_element_type=jnp.float32,
            )
            * softmax_scale
        )
        old_max = max_ref[rows, :]
        new_max = jnp.maximum(old_max, jnp.max(scores, axis=1, keepdims=True))
        new_max = new_max.astype(jnp.bfloat16).astype(jnp.float32)
        weights = jnp.exp(scores - new_max[:, :1])
        shrink = jnp.exp(old_max - new_max)
        total_ref[rows, :] = total_ref[rows, :] * shrink + jnp.sum(weights, axis=1, keepdims=True)
        accum_ref[rows, :] = accum_ref[rows, :] * shrink[:, :1] + jnp.dot(
            weights.astype(jnp.bfloat16), v_ref[keys, :], preferred_element_type=jnp.float32
        )
        max_ref[rows, :] = new_max
        return carry

    lax.fori_loop(0, live_tiles, visit, 0)


def forward_item(query_item, key_head, value_head, listing, live_tiles, softmax_scale):
    query_rows, head_width = query_item.shape
    smem = pl.BlockSpec(memory_space=pltpu.SMEM)
    vmem = pl.BlockSpec(memory_space=pltpu.VMEM)
    row_shape = jax.ShapeDtypeStruct((query_rows, head_width), jnp.float32)
    run_max, run_total, run_accum = pl.pallas_call(
        lambda *refs: forward_kernel(softmax_scale, *refs),
        out_shape=(row_shape, row_shape, row_shape),
        in_specs=[smem, smem, vmem, vmem, vmem],
        out_specs=(vmem, vmem, vmem),
    )(listing, live_tiles.reshape(1), query_item, key_head, value_head)
    return run_max[:, 0], run_total[:, 0], run_accum


def backward_kernel(
    softmax_scale, list_ref, count_ref, q_ref, k_ref, v_ref, do_ref, log_ref, delta_ref,
    dq_ref, dk_ref, dv_ref, dq_acc, dk_acc, dv_acc,
):
    dq_acc[...] = jnp.zeros(dq_acc.shape, jnp.float32)
    dk_acc[...] = jnp.zeros(dk_acc.shape, jnp.float32)
    dv_acc[...] = jnp.zeros(dv_acc.shape, jnp.float32)
    live_tiles = jnp.clip(count_ref[0], 0, LIST_SLOTS)

    def visit(position, carry):
        query_start, key_start = tile_starts(list_ref, position)
        rows = pl.ds(query_start, QBLK)
        keys = pl.ds(key_start, KBLK)
        query_block = q_ref[rows, :]
        grad_block = do_ref[rows, :]
        key_block = k_ref[keys, :]
        value_block = v_ref[keys, :]
        scores = (
            lax.dot_general(
                query_block, key_block, (((1,), (1,)), ((), ())),
                preferred_element_type=jnp.float32,
            )
            * softmax_scale
        )
        probs = jnp.exp(scores - log_ref[rows, :])
        probs_half = probs.astype(jnp.bfloat16)
        dv_acc[keys, :] += lax.dot_general(
            probs_half, grad_block, (((0,), (0,)), ((), ())), preferred_element_type=jnp.float32
        )
        prob_grad = lax.dot_general(
            grad_block, value_block, (((1,), (1,)), ((), ())), preferred_element_type=jnp.float32
        )
        score_grad = (probs * (prob_grad - delta_ref[rows, :])).astype(jnp.bfloat16)
        dq_acc[rows, :] += (
            jnp.dot(score_grad, key_block, preferred_element_type=jnp.float32) * softmax_scale
        )
        dk_acc[keys, :] += (
            lax.dot_general(
                score_grad, query_block, (((0,), (0,)), ((), ())),
                preferred_element_type=jnp.float32,
            )
            * softmax_scale
        )
        return carry

    lax.fori_loop(0, live_tiles, visit, 0)
    dq_ref[...] = dq_acc[...].astype(dq_ref.dtype)
    dk_ref[...] = dk_acc[...].astype(dk_ref.dtype)
    dv_ref[...] = dv_acc[...].astype(dv_ref.dtype)


def backward_item(
    query_item, key_head, value_head, grad_item, log_total, deltas, listing, live_tiles, softmax_scale,
):
    query_rows, head_width = query_item.shape
    key_rows = key_head.shape[0]
    smem = pl.BlockSpec(memory_space=pltpu.SMEM)
    vmem = pl.BlockSpec(memory_space=pltpu.VMEM)
    return pl.pallas_call(
        lambda *refs: backward_kernel(softmax_scale, *refs),
        out_shape=(
            jax.ShapeDtypeStruct((query_rows, head_width), jnp.bfloat16),
            jax.ShapeDtypeStruct((key_rows, head_width), jnp.bfloat16),
            jax.ShapeDtypeStruct((key_rows, head_width), jnp.bfloat16),
        ),
        in_specs=[smem, smem] + [vmem] * 6,
        out_specs=(vmem, vmem, vmem),
        scratch_shapes=[
            pltpu.VMEM((query_rows, head_width), jnp.float32),
            pltpu.VMEM((key_rows, head_width), jnp.float32),
            pltpu.VMEM((key_rows, head_width), jnp.float32),
        ],
    )(
        listing,
        live_tiles.reshape(1),
        query_item,
        key_head,
        value_head,
        grad_item,
        log_total.reshape(query_rows, 1),
        deltas.reshape(query_rows, 1),
    )


def scatter_rows(rows, parts):
    return lax.all_to_all(
        rows.reshape(parts, rows.shape[0] // parts, rows.shape[1]),
        "grp",
        split_axis=0,
        concat_axis=0,
        tiled=True,
    )


def broadcast_rows(chunk, parts):
    spread = jnp.broadcast_to(chunk[None], (parts,) + chunk.shape)
    gathered = lax.all_to_all(spread, "grp", split_axis=0, concat_axis=0, tiled=True)
    return gathered.reshape(parts * chunk.shape[0], chunk.shape[1])


def per_device(queries, scene_keys, scene_values, grad_output, tile_list, tile_counts):
    items_here = queries.shape[0]
    head_width = queries.shape[2]
    query_rows = queries.shape[1]
    scene_here = scene_keys.shape[0]
    heads_total = scene_keys.shape[1] // head_width
    seq_devices = lax.axis_size("seq")
    groups = lax.axis_size("grp")
    chunk_rows = query_rows // groups
    group_keys = scene_here * seq_devices
    copies = max(1, QPARTS // items_here)
    heads_here = max(1, items_here // QPARTS)
    softmax_scale = head_width ** (-0.5)
    key_wide = jnp.repeat(
        scene_keys.reshape(scene_here, heads_total, head_width), copies, axis=1
    ).reshape(scene_here, -1)
    value_wide = jnp.repeat(
        scene_values.reshape(scene_here, heads_total, head_width), copies, axis=1
    ).reshape(scene_here, -1)
    key_group, value_group = (
        lax.all_to_all(key_wide, "seq", split_axis=1, concat_axis=0, tiled=True),
        lax.all_to_all(value_wide, "seq", split_axis=1, concat_axis=0, tiled=True),
    )
    key_group = key_group.reshape(group_keys, heads_here, head_width)
    value_group = value_group.reshape(group_keys, heads_here, head_width)
    part_max, part_total, part_accum = forward_item(
        queries[0],
        key_group[:, 0, :],
        value_group[:, 0, :],
        tile_list[0, 0],
        tile_counts[0, 0],
        softmax_scale,
    )
    total_hi = part_total.astype(jnp.bfloat16)
    total_lo = (part_total - total_hi.astype(jnp.float32)).astype(jnp.bfloat16)
    stats = jnp.stack(
        [
            jnp.concatenate(
                [part_max.astype(jnp.bfloat16).reshape(groups, chunk_rows), total_hi.reshape(groups, chunk_rows)],
                axis=1,
            ),
            jnp.concatenate(
                [total_lo.reshape(groups, chunk_rows), jnp.zeros((groups, chunk_rows), jnp.bfloat16)],
                axis=1,
            ),
        ],
        axis=1,
    )
    packed = jnp.concatenate(
        [part_accum.astype(jnp.bfloat16).reshape(groups, chunk_rows, head_width), stats], axis=1
    )
    arrived = scatter_rows(packed.reshape(groups * (chunk_rows + 2), head_width), groups)
    arrived = arrived.reshape(groups, chunk_rows + 2, head_width).astype(jnp.float32)
    got_accum = arrived[:, :chunk_rows, :]
    got_max = arrived[:, chunk_rows, :chunk_rows]
    got_total = arrived[:, chunk_rows, chunk_rows:] + arrived[:, chunk_rows + 1, :chunk_rows]
    top = jnp.max(got_max, axis=0)
    shrink = jnp.exp(got_max - top[None, :])
    chunk_total = jnp.sum(got_total * shrink, axis=0)
    chunk_accum = jnp.sum(got_accum * shrink[:, :, None], axis=0)
    chunk_out = (chunk_accum / chunk_total[:, None]).astype(jnp.bfloat16)
    chunk_hi = chunk_total.astype(jnp.bfloat16)
    chunk_lo = (chunk_total - chunk_hi.astype(jnp.float32)).astype(jnp.bfloat16)
    chunk_stats = jnp.stack(
        [
            jnp.concatenate([top.astype(jnp.bfloat16), chunk_hi]),
            jnp.concatenate([chunk_lo, jnp.zeros((chunk_rows,), jnp.bfloat16)]),
        ]
    )
    back = broadcast_rows(jnp.concatenate([chunk_out, chunk_stats], axis=0), groups)
    back = back.reshape(groups, chunk_rows + 2, head_width)
    attended = back[:, :chunk_rows, :].reshape(1, query_rows, head_width)
    back_stats = back[:, chunk_rows:, :].astype(jnp.float32)
    row_top = back_stats[:, 0, :chunk_rows].reshape(1, query_rows)
    row_total = (back_stats[:, 0, chunk_rows:] + back_stats[:, 1, :chunk_rows]).reshape(1, query_rows)
    log_total = row_top + jnp.log(row_total)
    deltas = jnp.sum(attended.astype(jnp.float32) * grad_output.astype(jnp.float32), axis=2)
    query_grad, key_grad, value_grad = backward_item(
        queries[0],
        key_group[:, 0, :],
        value_group[:, 0, :],
        grad_output[0],
        log_total[0],
        deltas[0],
        tile_list[0, 0],
        tile_counts[0, 0],
        softmax_scale,
    )
    key_stack = key_grad[:, None, :]
    value_stack = value_grad[:, None, :]
    key_back, value_back = (
        lax.all_to_all(
            key_stack.reshape(group_keys, -1), "seq", split_axis=0, concat_axis=1, tiled=True
        ),
        lax.all_to_all(
            value_stack.reshape(group_keys, -1), "seq", split_axis=0, concat_axis=1, tiled=True
        ),
    )
    grad_keys = (
        jnp.sum(
            key_back.reshape(scene_here, heads_total, copies, head_width).astype(jnp.float32),
            axis=2,
        )
        .astype(jnp.bfloat16)
        .reshape(scene_here, -1)
    )
    grad_values = (
        jnp.sum(
            value_back.reshape(scene_here, heads_total, copies, head_width).astype(jnp.float32),
            axis=2,
        )
        .astype(jnp.bfloat16)
        .reshape(scene_here, -1)
    )
    query_parts = scatter_rows(query_grad, groups)
    query_chunk = jnp.sum(query_parts.astype(jnp.float32), axis=0).astype(jnp.bfloat16)
    grad_queries = broadcast_rows(query_chunk, groups).reshape(1, query_rows, head_width)
    return (attended, grad_queries, grad_keys, grad_values)


def solution(mesh):
    in_specs = (
        P("seq", None, None),
        P(("grp", "seq"), None),
        P(("grp", "seq"), None),
        P("seq", None, None),
        P("grp", "seq", None, None),
        P("grp", "seq"),
    )
    out_specs = (
        P("seq", None, None),
        P("seq", None, None),
        P(("grp", "seq"), None),
        P(("grp", "seq"), None),
    )
    return jax.shard_map(
        per_device, mesh=mesh, in_specs=in_specs, out_specs=out_specs, check_vma=False
    )
```

```python
import jax
import jax.numpy as jnp
from jax import lax
from jax.experimental import pallas as pl
from jax.experimental.pallas import tpu as pltpu
from jax.sharding import PartitionSpec as P

QPARTS = 2
QBLK = 512
KBLK = 512


NEG_START = -1e30


LIST_SLOTS = 9


def tile_starts(list_ref, position):
    query_block = jnp.clip(list_ref[position, 0], 0, QPARTS - 1)
    key_block = jnp.clip(list_ref[position, 1], 0, 7)
    return (
        pl.multiple_of(query_block * QBLK, QBLK),
        pl.multiple_of(key_block * KBLK, KBLK),
    )


def forward_kernel(softmax_scale, list_ref, count_ref, q_ref, k_ref, v_ref, max_ref, total_ref, accum_ref):
    max_ref[...] = jnp.full(max_ref.shape, NEG_START, jnp.float32)
    total_ref[...] = jnp.zeros(total_ref.shape, jnp.float32)
    accum_ref[...] = jnp.zeros(accum_ref.shape, jnp.float32)
    live_tiles = jnp.clip(count_ref[0], 0, LIST_SLOTS)

    def visit(position, carry):
        query_start, key_start = tile_starts(list_ref, position)
        rows = pl.ds(query_start, QBLK)
        keys = pl.ds(key_start, KBLK)
        scores = (
            lax.dot_general(
                q_ref[rows, :], k_ref[keys, :], (((1,), (1,)), ((), ())),
                preferred_element_type=jnp.float32,
            )
            * softmax_scale
        )
        old_max = max_ref[rows, :]
        new_max = jnp.maximum(old_max, jnp.max(scores, axis=1, keepdims=True))
        new_max = new_max.astype(jnp.bfloat16).astype(jnp.float32)
        weights = jnp.exp(scores - new_max[:, :1])
        shrink = jnp.exp(old_max - new_max)
        total_ref[rows, :] = total_ref[rows, :] * shrink + jnp.sum(weights, axis=1, keepdims=True)
        accum_ref[rows, :] = accum_ref[rows, :] * shrink[:, :1] + jnp.dot(
            weights.astype(jnp.bfloat16), v_ref[keys, :], preferred_element_type=jnp.float32
        )
        max_ref[rows, :] = new_max
        return carry

    lax.fori_loop(0, live_tiles, visit, 0)


def forward_item(query_item, key_head, value_head, listing, live_tiles, softmax_scale):
    query_rows, head_width = query_item.shape
    smem = pl.BlockSpec(memory_space=pltpu.SMEM)
    vmem = pl.BlockSpec(memory_space=pltpu.VMEM)
    row_shape = jax.ShapeDtypeStruct((query_rows, head_width), jnp.float32)
    run_max, run_total, run_accum = pl.pallas_call(
        lambda *refs: forward_kernel(softmax_scale, *refs),
        out_shape=(row_shape, row_shape, row_shape),
        in_specs=[smem, smem, vmem, vmem, vmem],
        out_specs=(vmem, vmem, vmem),
    )(listing, live_tiles.reshape(1), query_item, key_head, value_head)
    return run_max[:, 0], run_total[:, 0], run_accum


def backward_kernel(
    softmax_scale, list_ref, count_ref, q_ref, k_ref, v_ref, do_ref, log_ref, delta_ref,
    dq_ref, dk_ref, dv_ref, dq_acc, dk_acc, dv_acc,
):
    dq_acc[...] = jnp.zeros(dq_acc.shape, jnp.float32)
    dk_acc[...] = jnp.zeros(dk_acc.shape, jnp.float32)
    dv_acc[...] = jnp.zeros(dv_acc.shape, jnp.float32)
    live_tiles = jnp.clip(count_ref[0], 0, LIST_SLOTS)

    def visit(position, carry):
        query_start, key_start = tile_starts(list_ref, position)
        rows = pl.ds(query_start, QBLK)
        keys = pl.ds(key_start, KBLK)
        query_block = q_ref[rows, :]
        grad_block = do_ref[rows, :]
        key_block = k_ref[keys, :]
        value_block = v_ref[keys, :]
        scores = (
            lax.dot_general(
                query_block, key_block, (((1,), (1,)), ((), ())),
                preferred_element_type=jnp.float32,
            )
            * softmax_scale
        )
        probs = jnp.exp(scores - log_ref[rows, :])
        probs_half = probs.astype(jnp.bfloat16)
        dv_acc[keys, :] += lax.dot_general(
            probs_half, grad_block, (((0,), (0,)), ((), ())), preferred_element_type=jnp.float32
        )
        prob_grad = lax.dot_general(
            grad_block, value_block, (((1,), (1,)), ((), ())), preferred_element_type=jnp.float32
        )
        score_grad = (probs * (prob_grad - delta_ref[rows, :])).astype(jnp.bfloat16)
        dq_acc[rows, :] += (
            jnp.dot(score_grad, key_block, preferred_element_type=jnp.float32) * softmax_scale
        )
        dk_acc[keys, :] += (
            lax.dot_general(
                score_grad, query_block, (((0,), (0,)), ((), ())),
                preferred_element_type=jnp.float32,
            )
            * softmax_scale
        )
        return carry

    lax.fori_loop(0, live_tiles, visit, 0)
    dq_ref[...] = dq_acc[...].astype(dq_ref.dtype)
    dk_ref[...] = dk_acc[...].astype(dk_ref.dtype)
    dv_ref[...] = dv_acc[...].astype(dv_ref.dtype)


def backward_item(
    query_item, key_head, value_head, grad_item, log_total, deltas, listing, live_tiles, softmax_scale,
):
    query_rows, head_width = query_item.shape
    key_rows = key_head.shape[0]
    smem = pl.BlockSpec(memory_space=pltpu.SMEM)
    vmem = pl.BlockSpec(memory_space=pltpu.VMEM)
    return pl.pallas_call(
        lambda *refs: backward_kernel(softmax_scale, *refs),
        out_shape=(
            jax.ShapeDtypeStruct((query_rows, head_width), jnp.bfloat16),
            jax.ShapeDtypeStruct((key_rows, head_width), jnp.bfloat16),
            jax.ShapeDtypeStruct((key_rows, head_width), jnp.bfloat16),
        ),
        in_specs=[smem, smem] + [vmem] * 6,
        out_specs=(vmem, vmem, vmem),
        scratch_shapes=[
            pltpu.VMEM((query_rows, head_width), jnp.float32),
            pltpu.VMEM((key_rows, head_width), jnp.float32),
            pltpu.VMEM((key_rows, head_width), jnp.float32),
        ],
    )(
        listing,
        live_tiles.reshape(1),
        query_item,
        key_head,
        value_head,
        grad_item,
        log_total.reshape(query_rows, 1),
        deltas.reshape(query_rows, 1),
    )


def scatter_rows(rows, parts):
    return lax.all_to_all(
        rows.reshape(parts, rows.shape[0] // parts, rows.shape[1]),
        "grp",
        split_axis=0,
        concat_axis=0,
        tiled=True,
    )


def broadcast_rows(chunk, parts):
    spread = jnp.broadcast_to(chunk[None], (parts,) + chunk.shape)
    gathered = lax.all_to_all(spread, "grp", split_axis=0, concat_axis=0, tiled=True)
    return gathered.reshape(parts * chunk.shape[0], chunk.shape[1])


def per_device(queries, scene_keys, scene_values, grad_output, tile_list, tile_counts):
    items_here = queries.shape[0]
    head_width = queries.shape[2]
    query_rows = queries.shape[1]
    scene_here = scene_keys.shape[0]
    heads_total = scene_keys.shape[1] // head_width
    seq_devices = lax.axis_size("seq")
    groups = lax.axis_size("grp")
    chunk_rows = query_rows // groups
    group_keys = scene_here * seq_devices
    copies = max(1, QPARTS // items_here)
    heads_here = max(1, items_here // QPARTS)
    softmax_scale = head_width ** (-0.5)
    both_wide = jnp.repeat(
        jnp.stack(
            [
                scene_keys.reshape(scene_here, heads_total, head_width),
                scene_values.reshape(scene_here, heads_total, head_width),
            ],
            axis=2,
        ),
        copies,
        axis=1,
    ).reshape(scene_here, -1)
    both_group = lax.all_to_all(both_wide, "seq", split_axis=1, concat_axis=0, tiled=True)
    key_group = both_group[:, None, :head_width]
    value_group = both_group[:, None, head_width:]
    part_max, part_total, part_accum = forward_item(
        queries[0],
        key_group[:, 0, :],
        value_group[:, 0, :],
        tile_list[0, 0],
        tile_counts[0, 0],
        softmax_scale,
    )
    total_hi = part_total.astype(jnp.bfloat16)
    total_lo = (part_total - total_hi.astype(jnp.float32)).astype(jnp.bfloat16)
    stats = jnp.stack(
        [
            jnp.concatenate(
                [part_max.astype(jnp.bfloat16).reshape(groups, chunk_rows), total_hi.reshape(groups, chunk_rows)],
                axis=1,
            ),
            jnp.concatenate(
                [total_lo.reshape(groups, chunk_rows), jnp.zeros((groups, chunk_rows), jnp.bfloat16)],
                axis=1,
            ),
        ],
        axis=1,
    )
    packed = jnp.concatenate(
        [part_accum.astype(jnp.bfloat16).reshape(groups, chunk_rows, head_width), stats], axis=1
    )
    arrived = scatter_rows(packed.reshape(groups * (chunk_rows + 2), head_width), groups)
    arrived = arrived.reshape(groups, chunk_rows + 2, head_width).astype(jnp.float32)
    got_accum = arrived[:, :chunk_rows, :]
    got_max = arrived[:, chunk_rows, :chunk_rows]
    got_total = arrived[:, chunk_rows, chunk_rows:] + arrived[:, chunk_rows + 1, :chunk_rows]
    top = jnp.max(got_max, axis=0)
    shrink = jnp.exp(got_max - top[None, :])
    chunk_total = jnp.sum(got_total * shrink, axis=0)
    chunk_accum = jnp.sum(got_accum * shrink[:, :, None], axis=0)
    chunk_out = (chunk_accum / chunk_total[:, None]).astype(jnp.bfloat16)
    chunk_hi = chunk_total.astype(jnp.bfloat16)
    chunk_lo = (chunk_total - chunk_hi.astype(jnp.float32)).astype(jnp.bfloat16)
    chunk_stats = jnp.stack(
        [
            jnp.concatenate([top.astype(jnp.bfloat16), chunk_hi]),
            jnp.concatenate([chunk_lo, jnp.zeros((chunk_rows,), jnp.bfloat16)]),
        ]
    )
    back = broadcast_rows(jnp.concatenate([chunk_out, chunk_stats], axis=0), groups)
    back = back.reshape(groups, chunk_rows + 2, head_width)
    attended = back[:, :chunk_rows, :].reshape(1, query_rows, head_width)
    back_stats = back[:, chunk_rows:, :].astype(jnp.float32)
    row_top = back_stats[:, 0, :chunk_rows].reshape(1, query_rows)
    row_total = (back_stats[:, 0, chunk_rows:] + back_stats[:, 1, :chunk_rows]).reshape(1, query_rows)
    log_total = row_top + jnp.log(row_total)
    deltas = jnp.sum(attended.astype(jnp.float32) * grad_output.astype(jnp.float32), axis=2)
    query_grad, key_grad, value_grad = backward_item(
        queries[0],
        key_group[:, 0, :],
        value_group[:, 0, :],
        grad_output[0],
        log_total[0],
        deltas[0],
        tile_list[0, 0],
        tile_counts[0, 0],
        softmax_scale,
    )
    both_back = lax.all_to_all(
        jnp.concatenate([key_grad, value_grad], axis=1), "seq", split_axis=0, concat_axis=1, tiled=True
    ).reshape(scene_here, heads_total, copies, 2, head_width)
    both_sum = jnp.sum(both_back.astype(jnp.float32), axis=2).astype(jnp.bfloat16)
    grad_keys = both_sum[:, :, 0, :].reshape(scene_here, -1)
    grad_values = both_sum[:, :, 1, :].reshape(scene_here, -1)
    query_parts = scatter_rows(query_grad, groups)
    query_chunk = jnp.sum(query_parts.astype(jnp.float32), axis=0).astype(jnp.bfloat16)
    grad_queries = broadcast_rows(query_chunk, groups).reshape(1, query_rows, head_width)
    return (attended, grad_queries, grad_keys, grad_values)


def solution(mesh):
    in_specs = (
        P("seq", None, None),
        P(("grp", "seq"), None),
        P(("grp", "seq"), None),
        P("seq", None, None),
        P("grp", "seq", None, None),
        P("grp", "seq"),
    )
    out_specs = (
        P("seq", None, None),
        P("seq", None, None),
        P(("grp", "seq"), None),
        P(("grp", "seq"), None),
    )
    return jax.shard_map(
        per_device, mesh=mesh, in_specs=in_specs, out_specs=out_specs, check_vma=False
    )
```

```python
import jax
import jax.numpy as jnp
from jax import lax
from jax.experimental import pallas as pl
from jax.experimental.pallas import tpu as pltpu
from jax.sharding import PartitionSpec as P

QPARTS = 2
QBLK = 512
KBLK = 512


NEG_START = -1e30


LIST_SLOTS = 9


def tile_starts(list_ref, position):
    query_block = jnp.clip(list_ref[position, 0], 0, QPARTS - 1)
    key_block = jnp.clip(list_ref[position, 1], 0, 7)
    return (
        pl.multiple_of(query_block * QBLK, QBLK),
        pl.multiple_of(key_block * KBLK, KBLK),
    )


def forward_kernel(softmax_scale, list_ref, count_ref, q_ref, k_ref, v_ref, max_ref, total_ref, accum_ref):
    max_ref[...] = jnp.full(max_ref.shape, NEG_START, jnp.float32)
    total_ref[...] = jnp.zeros(total_ref.shape, jnp.float32)
    accum_ref[...] = jnp.zeros(accum_ref.shape, jnp.float32)
    live_tiles = jnp.clip(count_ref[0], 0, LIST_SLOTS)

    def visit(position, carry):
        query_start, key_start = tile_starts(list_ref, position)
        rows = pl.ds(query_start, QBLK)
        keys = pl.ds(key_start, KBLK)
        scores = (
            lax.dot_general(
                q_ref[rows, :], k_ref[keys, :], (((1,), (1,)), ((), ())),
                preferred_element_type=jnp.float32,
            )
            * softmax_scale
        )
        old_max = max_ref[rows, :]
        new_max = jnp.maximum(old_max, jnp.max(scores, axis=1, keepdims=True))
        new_max = new_max.astype(jnp.bfloat16).astype(jnp.float32)
        weights = jnp.exp(scores - new_max[:, :1])
        shrink = jnp.exp(old_max - new_max)
        total_ref[rows, :] = total_ref[rows, :] * shrink + jnp.sum(weights, axis=1, keepdims=True)
        accum_ref[rows, :] = accum_ref[rows, :] * shrink[:, :1] + jnp.dot(
            weights.astype(jnp.bfloat16), v_ref[keys, :], preferred_element_type=jnp.float32
        )
        max_ref[rows, :] = new_max
        return carry

    lax.fori_loop(0, live_tiles, visit, 0)


def forward_item(query_item, key_head, value_head, listing, live_tiles, softmax_scale):
    query_rows, head_width = query_item.shape
    smem = pl.BlockSpec(memory_space=pltpu.SMEM)
    vmem = pl.BlockSpec(memory_space=pltpu.VMEM)
    row_shape = jax.ShapeDtypeStruct((query_rows, head_width), jnp.float32)
    run_max, run_total, run_accum = pl.pallas_call(
        lambda *refs: forward_kernel(softmax_scale, *refs),
        out_shape=(row_shape, row_shape, row_shape),
        in_specs=[smem, smem, vmem, vmem, vmem],
        out_specs=(vmem, vmem, vmem),
    )(listing, live_tiles.reshape(1), query_item, key_head, value_head)
    return run_max[:, 0], run_total[:, 0], run_accum


def backward_kernel(
    softmax_scale, list_ref, count_ref, q_ref, k_ref, v_ref, do_ref, log_ref, delta_ref,
    dq_ref, dk_ref, dv_ref, dq_acc, dk_acc, dv_acc,
):
    dq_acc[...] = jnp.zeros(dq_acc.shape, jnp.float32)
    dk_acc[...] = jnp.zeros(dk_acc.shape, jnp.float32)
    dv_acc[...] = jnp.zeros(dv_acc.shape, jnp.float32)
    live_tiles = jnp.clip(count_ref[0], 0, LIST_SLOTS)

    def visit(position, carry):
        query_start, key_start = tile_starts(list_ref, position)
        rows = pl.ds(query_start, QBLK)
        keys = pl.ds(key_start, KBLK)
        query_block = q_ref[rows, :]
        grad_block = do_ref[rows, :]
        key_block = k_ref[keys, :]
        value_block = v_ref[keys, :]
        scores = (
            lax.dot_general(
                query_block, key_block, (((1,), (1,)), ((), ())),
                preferred_element_type=jnp.float32,
            )
            * softmax_scale
        )
        probs = jnp.exp(scores - log_ref[rows, :])
        probs_half = probs.astype(jnp.bfloat16)
        dv_acc[keys, :] += lax.dot_general(
            probs_half, grad_block, (((0,), (0,)), ((), ())), preferred_element_type=jnp.float32
        )
        prob_grad = lax.dot_general(
            grad_block, value_block, (((1,), (1,)), ((), ())), preferred_element_type=jnp.float32
        )
        score_grad = (probs * (prob_grad - delta_ref[rows, :])).astype(jnp.bfloat16)
        dq_acc[rows, :] += (
            jnp.dot(score_grad, key_block, preferred_element_type=jnp.float32) * softmax_scale
        )
        dk_acc[keys, :] += (
            lax.dot_general(
                score_grad, query_block, (((0,), (0,)), ((), ())),
                preferred_element_type=jnp.float32,
            )
            * softmax_scale
        )
        return carry

    lax.fori_loop(0, live_tiles, visit, 0)
    dq_ref[...] = dq_acc[...].astype(dq_ref.dtype)
    dk_ref[...] = dk_acc[...].astype(dk_ref.dtype)
    dv_ref[...] = dv_acc[...].astype(dv_ref.dtype)


def backward_item(
    query_item, key_head, value_head, grad_item, log_total, deltas, listing, live_tiles, softmax_scale,
):
    query_rows, head_width = query_item.shape
    key_rows = key_head.shape[0]
    smem = pl.BlockSpec(memory_space=pltpu.SMEM)
    vmem = pl.BlockSpec(memory_space=pltpu.VMEM)
    return pl.pallas_call(
        lambda *refs: backward_kernel(softmax_scale, *refs),
        out_shape=(
            jax.ShapeDtypeStruct((query_rows, head_width), jnp.bfloat16),
            jax.ShapeDtypeStruct((key_rows, head_width), jnp.bfloat16),
            jax.ShapeDtypeStruct((key_rows, head_width), jnp.bfloat16),
        ),
        in_specs=[smem, smem] + [vmem] * 6,
        out_specs=(vmem, vmem, vmem),
        scratch_shapes=[
            pltpu.VMEM((query_rows, head_width), jnp.float32),
            pltpu.VMEM((key_rows, head_width), jnp.float32),
            pltpu.VMEM((key_rows, head_width), jnp.float32),
        ],
    )(
        listing,
        live_tiles.reshape(1),
        query_item,
        key_head,
        value_head,
        grad_item,
        log_total.reshape(query_rows, 1),
        deltas.reshape(query_rows, 1),
    )


def exchange_kernel(broadcast, x_ref, y_ref, send_sem, recv_sem):
    groups = y_ref.shape[0]
    me = lax.axis_index("grp")
    lane = lax.axis_index("seq")
    mesh_ids = pl.DeviceIdType.MESH
    barrier = pltpu.get_barrier_semaphore()
    for step in range(1, groups):
        pl.semaphore_signal(
            barrier, inc=1, device_id=(lax.rem(me + step, groups), lane), device_id_type=mesh_ids
        )
    pl.semaphore_wait(barrier, groups - 1)
    copies = []
    for step in range(1, groups):
        target = lax.rem(me + step, groups)
        copy = pltpu.make_async_remote_copy(
            src_ref=x_ref if broadcast else x_ref.at[target],
            dst_ref=y_ref.at[me],
            send_sem=send_sem.at[step],
            recv_sem=recv_sem.at[step],
            device_id=(target, lane),
            device_id_type=mesh_ids,
        )
        copy.start()
        copies.append(copy)
    y_ref[me] = x_ref[...] if broadcast else x_ref[me]
    for copy in copies:
        copy.wait()


def grp_exchange(x, groups, broadcast, collective):
    out_shape = (groups,) + (x.shape if broadcast else x.shape[1:])
    vmem = pl.BlockSpec(memory_space=pltpu.VMEM)
    return pl.pallas_call(
        lambda *refs: exchange_kernel(broadcast, *refs),
        out_shape=jax.ShapeDtypeStruct(out_shape, x.dtype),
        in_specs=[vmem],
        out_specs=vmem,
        scratch_shapes=[pltpu.SemaphoreType.DMA((groups,)), pltpu.SemaphoreType.DMA((groups,))],
        compiler_params=pltpu.CompilerParams(collective_id=collective, has_side_effects=True),
    )(x)


def scatter_rows(rows, parts, collective):
    return grp_exchange(
        rows.reshape(parts, rows.shape[0] // parts, rows.shape[1]), parts, False, collective
    )


def broadcast_rows(chunk, parts, collective):
    gathered = grp_exchange(chunk, parts, True, collective)
    return gathered.reshape(parts * chunk.shape[0], chunk.shape[1])


def per_device(queries, scene_keys, scene_values, grad_output, tile_list, tile_counts):
    items_here = queries.shape[0]
    head_width = queries.shape[2]
    query_rows = queries.shape[1]
    scene_here = scene_keys.shape[0]
    heads_total = scene_keys.shape[1] // head_width
    seq_devices = lax.axis_size("seq")
    groups = lax.axis_size("grp")
    chunk_rows = query_rows // groups
    group_keys = scene_here * seq_devices
    copies = max(1, QPARTS // items_here)
    heads_here = max(1, items_here // QPARTS)
    softmax_scale = head_width ** (-0.5)
    both_wide = jnp.repeat(
        jnp.stack(
            [
                scene_keys.reshape(scene_here, heads_total, head_width),
                scene_values.reshape(scene_here, heads_total, head_width),
            ],
            axis=2,
        ),
        copies,
        axis=1,
    ).reshape(scene_here, -1)
    both_group = lax.all_to_all(both_wide, "seq", split_axis=1, concat_axis=0, tiled=True)
    key_group = both_group[:, None, :head_width]
    value_group = both_group[:, None, head_width:]
    part_max, part_total, part_accum = forward_item(
        queries[0],
        key_group[:, 0, :],
        value_group[:, 0, :],
        tile_list[0, 0],
        tile_counts[0, 0],
        softmax_scale,
    )
    total_hi = part_total.astype(jnp.bfloat16)
    total_lo = (part_total - total_hi.astype(jnp.float32)).astype(jnp.bfloat16)
    stats = jnp.stack(
        [
            jnp.concatenate(
                [part_max.astype(jnp.bfloat16).reshape(groups, chunk_rows), total_hi.reshape(groups, chunk_rows)],
                axis=1,
            ),
            jnp.concatenate(
                [total_lo.reshape(groups, chunk_rows), jnp.zeros((groups, chunk_rows), jnp.bfloat16)],
                axis=1,
            ),
        ],
        axis=1,
    )
    packed = jnp.concatenate(
        [part_accum.astype(jnp.bfloat16).reshape(groups, chunk_rows, head_width), stats], axis=1
    )
    arrived = scatter_rows(packed.reshape(groups * (chunk_rows + 2), head_width), groups, 0)
    arrived = arrived.reshape(groups, chunk_rows + 2, head_width).astype(jnp.float32)
    got_accum = arrived[:, :chunk_rows, :]
    got_max = arrived[:, chunk_rows, :chunk_rows]
    got_total = arrived[:, chunk_rows, chunk_rows:] + arrived[:, chunk_rows + 1, :chunk_rows]
    top = jnp.max(got_max, axis=0)
    shrink = jnp.exp(got_max - top[None, :])
    chunk_total = jnp.sum(got_total * shrink, axis=0)
    chunk_accum = jnp.sum(got_accum * shrink[:, :, None], axis=0)
    chunk_out = (chunk_accum / chunk_total[:, None]).astype(jnp.bfloat16)
    chunk_hi = chunk_total.astype(jnp.bfloat16)
    chunk_lo = (chunk_total - chunk_hi.astype(jnp.float32)).astype(jnp.bfloat16)
    chunk_stats = jnp.stack(
        [
            jnp.concatenate([top.astype(jnp.bfloat16), chunk_hi]),
            jnp.concatenate([chunk_lo, jnp.zeros((chunk_rows,), jnp.bfloat16)]),
        ]
    )
    back = broadcast_rows(jnp.concatenate([chunk_out, chunk_stats], axis=0), groups, 1)
    back = back.reshape(groups, chunk_rows + 2, head_width)
    attended = back[:, :chunk_rows, :].reshape(1, query_rows, head_width)
    back_stats = back[:, chunk_rows:, :].astype(jnp.float32)
    row_top = back_stats[:, 0, :chunk_rows].reshape(1, query_rows)
    row_total = (back_stats[:, 0, chunk_rows:] + back_stats[:, 1, :chunk_rows]).reshape(1, query_rows)
    log_total = row_top + jnp.log(row_total)
    deltas = jnp.sum(attended.astype(jnp.float32) * grad_output.astype(jnp.float32), axis=2)
    query_grad, key_grad, value_grad = backward_item(
        queries[0],
        key_group[:, 0, :],
        value_group[:, 0, :],
        grad_output[0],
        log_total[0],
        deltas[0],
        tile_list[0, 0],
        tile_counts[0, 0],
        softmax_scale,
    )
    both_back = lax.all_to_all(
        jnp.concatenate([key_grad, value_grad], axis=1), "seq", split_axis=0, concat_axis=1, tiled=True
    ).reshape(scene_here, heads_total, copies, 2, head_width)
    both_sum = jnp.sum(both_back.astype(jnp.float32), axis=2).astype(jnp.bfloat16)
    grad_keys = both_sum[:, :, 0, :].reshape(scene_here, -1)
    grad_values = both_sum[:, :, 1, :].reshape(scene_here, -1)
    query_parts = scatter_rows(query_grad, groups, 2)
    query_chunk = jnp.sum(query_parts.astype(jnp.float32), axis=0).astype(jnp.bfloat16)
    grad_queries = broadcast_rows(query_chunk, groups, 3).reshape(1, query_rows, head_width)
    return (attended, grad_queries, grad_keys, grad_values)


def solution(mesh):
    in_specs = (
        P("seq", None, None),
        P(("grp", "seq"), None),
        P(("grp", "seq"), None),
        P("seq", None, None),
        P("grp", "seq", None, None),
        P("grp", "seq"),
    )
    out_specs = (
        P("seq", None, None),
        P("seq", None, None),
        P(("grp", "seq"), None),
        P(("grp", "seq"), None),
    )
    return jax.shard_map(
        per_device, mesh=mesh, in_specs=in_specs, out_specs=out_specs, check_vma=False
    )
```

```python
import jax
import jax.numpy as jnp
from jax import lax
from jax.experimental import pallas as pl
from jax.experimental.pallas import tpu as pltpu
from jax.sharding import PartitionSpec as P

QPARTS = 2
QBLK = 512
KBLK = 512


NEG_START = -1e30


LIST_SLOTS = 9


def tile_starts(list_ref, position):
    query_block = jnp.clip(list_ref[position, 0], 0, QPARTS - 1)
    key_block = jnp.clip(list_ref[position, 1], 0, 7)
    return (
        pl.multiple_of(query_block * QBLK, QBLK),
        pl.multiple_of(key_block * KBLK, KBLK),
    )


def forward_kernel(softmax_scale, list_ref, count_ref, q_ref, k_ref, v_ref, max_ref, total_ref, accum_ref):
    max_ref[...] = jnp.full(max_ref.shape, NEG_START, jnp.float32)
    total_ref[...] = jnp.zeros(total_ref.shape, jnp.float32)
    accum_ref[...] = jnp.zeros(accum_ref.shape, jnp.float32)
    live_tiles = jnp.clip(count_ref[0], 0, LIST_SLOTS)

    def visit(position, carry):
        query_start, key_start = tile_starts(list_ref, position)
        rows = pl.ds(query_start, QBLK)
        keys = pl.ds(key_start, KBLK)
        scores = (
            lax.dot_general(
                q_ref[rows, :], k_ref[keys, :], (((1,), (1,)), ((), ())),
                preferred_element_type=jnp.float32,
            )
            * softmax_scale
        )
        old_max = max_ref[rows, :]
        new_max = jnp.maximum(old_max, jnp.max(scores, axis=1, keepdims=True))
        new_max = new_max.astype(jnp.bfloat16).astype(jnp.float32)
        weights = jnp.exp(scores - new_max[:, :1])
        shrink = jnp.exp(old_max - new_max)
        total_ref[rows, :] = total_ref[rows, :] * shrink + jnp.sum(weights, axis=1, keepdims=True)
        accum_ref[rows, :] = accum_ref[rows, :] * shrink[:, :1] + jnp.dot(
            weights.astype(jnp.bfloat16), v_ref[keys, :], preferred_element_type=jnp.float32
        )
        max_ref[rows, :] = new_max
        return carry

    lax.fori_loop(0, live_tiles, visit, 0)


def forward_item(query_item, key_head, value_head, listing, live_tiles, softmax_scale):
    query_rows, head_width = query_item.shape
    smem = pl.BlockSpec(memory_space=pltpu.SMEM)
    vmem = pl.BlockSpec(memory_space=pltpu.VMEM)
    row_shape = jax.ShapeDtypeStruct((query_rows, head_width), jnp.float32)
    run_max, run_total, run_accum = pl.pallas_call(
        lambda *refs: forward_kernel(softmax_scale, *refs),
        out_shape=(row_shape, row_shape, row_shape),
        in_specs=[smem, smem, vmem, vmem, vmem],
        out_specs=(vmem, vmem, vmem),
    )(listing, live_tiles.reshape(1), query_item, key_head, value_head)
    return run_max[:, 0], run_total[:, 0], run_accum


def backward_kernel(
    softmax_scale, list_ref, count_ref, q_ref, k_ref, v_ref, do_ref, log_ref, delta_ref,
    dq_ref, dk_ref, dv_ref, dq_acc, dk_acc, dv_acc,
):
    dq_acc[...] = jnp.zeros(dq_acc.shape, jnp.float32)
    dk_acc[...] = jnp.zeros(dk_acc.shape, jnp.float32)
    dv_acc[...] = jnp.zeros(dv_acc.shape, jnp.float32)
    live_tiles = jnp.clip(count_ref[0], 0, LIST_SLOTS)

    def visit(position, carry):
        query_start, key_start = tile_starts(list_ref, position)
        rows = pl.ds(query_start, QBLK)
        keys = pl.ds(key_start, KBLK)
        query_block = q_ref[rows, :]
        grad_block = do_ref[rows, :]
        key_block = k_ref[keys, :]
        value_block = v_ref[keys, :]
        scores = (
            lax.dot_general(
                query_block, key_block, (((1,), (1,)), ((), ())),
                preferred_element_type=jnp.float32,
            )
            * softmax_scale
        )
        probs = jnp.exp(scores - log_ref[rows, :])
        probs_half = probs.astype(jnp.bfloat16)
        dv_acc[keys, :] += lax.dot_general(
            probs_half, grad_block, (((0,), (0,)), ((), ())), preferred_element_type=jnp.float32
        )
        prob_grad = lax.dot_general(
            grad_block, value_block, (((1,), (1,)), ((), ())), preferred_element_type=jnp.float32
        )
        score_grad = (probs * (prob_grad - delta_ref[rows, :])).astype(jnp.bfloat16)
        dq_acc[rows, :] += (
            jnp.dot(score_grad, key_block, preferred_element_type=jnp.float32) * softmax_scale
        )
        dk_acc[keys, :] += (
            lax.dot_general(
                score_grad, query_block, (((0,), (0,)), ((), ())),
                preferred_element_type=jnp.float32,
            )
            * softmax_scale
        )
        return carry

    lax.fori_loop(0, live_tiles, visit, 0)
    dq_ref[...] = dq_acc[...].astype(dq_ref.dtype)
    dk_ref[...] = dk_acc[...].astype(dk_ref.dtype)
    dv_ref[...] = dv_acc[...].astype(dv_ref.dtype)


def backward_item(
    query_item, key_head, value_head, grad_item, log_total, deltas, listing, live_tiles, softmax_scale,
):
    query_rows, head_width = query_item.shape
    key_rows = key_head.shape[0]
    smem = pl.BlockSpec(memory_space=pltpu.SMEM)
    vmem = pl.BlockSpec(memory_space=pltpu.VMEM)
    return pl.pallas_call(
        lambda *refs: backward_kernel(softmax_scale, *refs),
        out_shape=(
            jax.ShapeDtypeStruct((query_rows, head_width), jnp.bfloat16),
            jax.ShapeDtypeStruct((key_rows, head_width), jnp.bfloat16),
            jax.ShapeDtypeStruct((key_rows, head_width), jnp.bfloat16),
        ),
        in_specs=[smem, smem] + [vmem] * 6,
        out_specs=(vmem, vmem, vmem),
        scratch_shapes=[
            pltpu.VMEM((query_rows, head_width), jnp.float32),
            pltpu.VMEM((key_rows, head_width), jnp.float32),
            pltpu.VMEM((key_rows, head_width), jnp.float32),
        ],
    )(
        listing,
        live_tiles.reshape(1),
        query_item,
        key_head,
        value_head,
        grad_item,
        log_total.reshape(query_rows, 1),
        deltas.reshape(query_rows, 1),
    )


def exchange_kernel(broadcast, x_ref, y_ref, send_sem, recv_sem):
    groups = y_ref.shape[0]
    me = lax.axis_index("grp")
    lane = lax.axis_index("seq")
    mesh_ids = pl.DeviceIdType.MESH
    barrier = pltpu.get_barrier_semaphore()
    for step in range(1, groups):
        pl.semaphore_signal(
            barrier, inc=1, device_id=(lax.rem(me + step, groups), lane), device_id_type=mesh_ids
        )
    pl.semaphore_wait(barrier, groups - 1)
    copies = []
    for step in range(1, groups):
        target = lax.rem(me + step, groups)
        copy = pltpu.make_async_remote_copy(
            src_ref=x_ref if broadcast else x_ref.at[target],
            dst_ref=y_ref.at[me],
            send_sem=send_sem.at[step],
            recv_sem=recv_sem.at[step],
            device_id=(target, lane),
            device_id_type=mesh_ids,
        )
        copy.start()
        copies.append(copy)
    y_ref[me] = x_ref[...] if broadcast else x_ref[me]
    for copy in copies:
        copy.wait()


def grp_exchange(x, groups, broadcast, collective):
    out_shape = (groups,) + (x.shape if broadcast else x.shape[1:])
    vmem = pl.BlockSpec(memory_space=pltpu.VMEM)
    return pl.pallas_call(
        lambda *refs: exchange_kernel(broadcast, *refs),
        out_shape=jax.ShapeDtypeStruct(out_shape, x.dtype),
        in_specs=[vmem],
        out_specs=vmem,
        scratch_shapes=[pltpu.SemaphoreType.DMA((groups,)), pltpu.SemaphoreType.DMA((groups,))],
        compiler_params=pltpu.CompilerParams(collective_id=collective, has_side_effects=True),
    )(x)


def scatter_rows(rows, parts, collective):
    return grp_exchange(
        rows.reshape(parts, rows.shape[0] // parts, rows.shape[1]), parts, False, collective
    )


def broadcast_rows(chunk, parts, collective):
    gathered = grp_exchange(chunk, parts, True, collective)
    return gathered.reshape(parts * chunk.shape[0], chunk.shape[1])


def per_device(queries, scene_keys, scene_values, grad_output, tile_list, tile_counts):
    items_here = queries.shape[0]
    head_width = queries.shape[2]
    query_rows = queries.shape[1]
    scene_here = scene_keys.shape[0]
    heads_total = scene_keys.shape[1] // head_width
    seq_devices = lax.axis_size("seq")
    groups = lax.axis_size("grp")
    chunk_rows = query_rows // groups
    group_keys = scene_here * seq_devices
    copies = max(1, QPARTS // items_here)
    heads_here = max(1, items_here // QPARTS)
    softmax_scale = head_width ** (-0.5)
    half_keys = scene_here // QPARTS
    both_here = jnp.stack(
        [
            scene_keys.reshape(QPARTS, half_keys, heads_total, head_width),
            scene_values.reshape(QPARTS, half_keys, heads_total, head_width),
        ],
        axis=3,
    ).transpose(2, 0, 1, 3, 4)
    mine = lax.all_to_all(
        both_here.reshape(seq_devices, half_keys, 2 * head_width), "seq", 0, 0, tiled=True
    )
    pairs = [(2 * h + c, 2 * h + 1 - c) for h in range(seq_devices // 2) for c in range(2)]
    other = lax.ppermute(mine, "seq", pairs)
    core = lax.rem(lax.axis_index("seq"), 2)
    both_group = jnp.where(
        core == 0, jnp.stack([mine, other], axis=1), jnp.stack([other, mine], axis=1)
    ).reshape(group_keys, 2 * head_width)
    key_group = both_group[:, None, :head_width]
    value_group = both_group[:, None, head_width:]
    part_max, part_total, part_accum = forward_item(
        queries[0],
        key_group[:, 0, :],
        value_group[:, 0, :],
        tile_list[0, 0],
        tile_counts[0, 0],
        softmax_scale,
    )
    total_hi = part_total.astype(jnp.bfloat16)
    total_lo = (part_total - total_hi.astype(jnp.float32)).astype(jnp.bfloat16)
    stats = jnp.stack(
        [
            jnp.concatenate(
                [part_max.astype(jnp.bfloat16).reshape(groups, chunk_rows), total_hi.reshape(groups, chunk_rows)],
                axis=1,
            ),
            jnp.concatenate(
                [total_lo.reshape(groups, chunk_rows), jnp.zeros((groups, chunk_rows), jnp.bfloat16)],
                axis=1,
            ),
        ],
        axis=1,
    )
    packed = jnp.concatenate(
        [part_accum.astype(jnp.bfloat16).reshape(groups, chunk_rows, head_width), stats], axis=1
    )
    arrived = scatter_rows(packed.reshape(groups * (chunk_rows + 2), head_width), groups, 0)
    arrived = arrived.reshape(groups, chunk_rows + 2, head_width).astype(jnp.float32)
    got_accum = arrived[:, :chunk_rows, :]
    got_max = arrived[:, chunk_rows, :chunk_rows]
    got_total = arrived[:, chunk_rows, chunk_rows:] + arrived[:, chunk_rows + 1, :chunk_rows]
    top = jnp.max(got_max, axis=0)
    shrink = jnp.exp(got_max - top[None, :])
    chunk_total = jnp.sum(got_total * shrink, axis=0)
    chunk_accum = jnp.sum(got_accum * shrink[:, :, None], axis=0)
    chunk_out = (chunk_accum / chunk_total[:, None]).astype(jnp.bfloat16)
    chunk_hi = chunk_total.astype(jnp.bfloat16)
    chunk_lo = (chunk_total - chunk_hi.astype(jnp.float32)).astype(jnp.bfloat16)
    chunk_stats = jnp.stack(
        [
            jnp.concatenate([top.astype(jnp.bfloat16), chunk_hi]),
            jnp.concatenate([chunk_lo, jnp.zeros((chunk_rows,), jnp.bfloat16)]),
        ]
    )
    back = broadcast_rows(jnp.concatenate([chunk_out, chunk_stats], axis=0), groups, 1)
    back = back.reshape(groups, chunk_rows + 2, head_width)
    attended = back[:, :chunk_rows, :].reshape(1, query_rows, head_width)
    back_stats = back[:, chunk_rows:, :].astype(jnp.float32)
    row_top = back_stats[:, 0, :chunk_rows].reshape(1, query_rows)
    row_total = (back_stats[:, 0, chunk_rows:] + back_stats[:, 1, :chunk_rows]).reshape(1, query_rows)
    log_total = row_top + jnp.log(row_total)
    deltas = jnp.sum(attended.astype(jnp.float32) * grad_output.astype(jnp.float32), axis=2)
    query_grad, key_grad, value_grad = backward_item(
        queries[0],
        key_group[:, 0, :],
        value_group[:, 0, :],
        grad_output[0],
        log_total[0],
        deltas[0],
        tile_list[0, 0],
        tile_counts[0, 0],
        softmax_scale,
    )
    both_parts = jnp.concatenate([key_grad, value_grad], axis=1).reshape(
        seq_devices, QPARTS, half_keys, 2 * head_width
    )
    kept = lax.dynamic_index_in_dim(both_parts, core, axis=1, keepdims=False)
    given = lax.dynamic_index_in_dim(both_parts, 1 - core, axis=1, keepdims=False)
    summed = (kept.astype(jnp.float32) + lax.ppermute(given, "seq", pairs).astype(jnp.float32)).astype(
        jnp.bfloat16
    )
    both_back = lax.all_to_all(summed, "seq", 0, 0, tiled=True)
    both_back = both_back.reshape(heads_total, QPARTS, half_keys, 2, head_width).transpose(1, 2, 0, 3, 4)
    both_back = both_back.reshape(scene_here, heads_total, 2, head_width)
    grad_keys = both_back[:, :, 0, :].reshape(scene_here, -1)
    grad_values = both_back[:, :, 1, :].reshape(scene_here, -1)
    query_parts = scatter_rows(query_grad, groups, 2)
    query_chunk = jnp.sum(query_parts.astype(jnp.float32), axis=0).astype(jnp.bfloat16)
    grad_queries = broadcast_rows(query_chunk, groups, 3).reshape(1, query_rows, head_width)
    return (attended, grad_queries, grad_keys, grad_values)


def solution(mesh):
    in_specs = (
        P("seq", None, None),
        P(("grp", "seq"), None),
        P(("grp", "seq"), None),
        P("seq", None, None),
        P("grp", "seq", None, None),
        P("grp", "seq"),
    )
    out_specs = (
        P("seq", None, None),
        P("seq", None, None),
        P(("grp", "seq"), None),
        P(("grp", "seq"), None),
    )
    return jax.shard_map(
        per_device, mesh=mesh, in_specs=in_specs, out_specs=out_specs, check_vma=False
    )
```

```python
import jax
import jax.numpy as jnp
from jax import lax
from jax.experimental import pallas as pl
from jax.experimental.pallas import tpu as pltpu
from jax.sharding import PartitionSpec as P

QPARTS = 2
QBLK = 512
KBLK = 512


NEG_START = -1e30


LIST_SLOTS = 9


def tile_starts(list_ref, position):
    query_block = jnp.clip(list_ref[position, 0], 0, QPARTS - 1)
    key_block = jnp.clip(list_ref[position, 1], 0, 7)
    return (
        pl.multiple_of(query_block * QBLK, QBLK),
        pl.multiple_of(key_block * KBLK, KBLK),
    )


def forward_kernel(softmax_scale, list_ref, count_ref, q_ref, k_ref, v_ref, max_ref, total_ref, accum_ref):
    max_ref[...] = jnp.full(max_ref.shape, NEG_START, jnp.float32)
    total_ref[...] = jnp.zeros(total_ref.shape, jnp.float32)
    accum_ref[...] = jnp.zeros(accum_ref.shape, jnp.float32)
    live_tiles = jnp.clip(count_ref[0], 0, LIST_SLOTS)

    def visit(position, carry):
        query_start, key_start = tile_starts(list_ref, position)
        rows = pl.ds(query_start, QBLK)
        keys = pl.ds(key_start, KBLK)
        scores = (
            lax.dot_general(
                q_ref[rows, :], k_ref[keys, :], (((1,), (1,)), ((), ())),
                preferred_element_type=jnp.float32,
            )
            * softmax_scale
        )
        old_max = max_ref[rows, :]
        new_max = jnp.maximum(old_max, jnp.max(scores, axis=1, keepdims=True))
        new_max = new_max.astype(jnp.bfloat16).astype(jnp.float32)
        weights = jnp.exp(scores - new_max[:, :1])
        shrink = jnp.exp(old_max - new_max)
        total_ref[rows, :] = total_ref[rows, :] * shrink + jnp.sum(weights, axis=1, keepdims=True)
        accum_ref[rows, :] = accum_ref[rows, :] * shrink[:, :1] + jnp.dot(
            weights.astype(jnp.bfloat16), v_ref[keys, :], preferred_element_type=jnp.float32
        )
        max_ref[rows, :] = new_max
        return carry

    lax.fori_loop(0, live_tiles, visit, 0)


def forward_item(query_item, key_head, value_head, listing, live_tiles, softmax_scale):
    query_rows, head_width = query_item.shape
    smem = pl.BlockSpec(memory_space=pltpu.SMEM)
    vmem = pl.BlockSpec(memory_space=pltpu.VMEM)
    row_shape = jax.ShapeDtypeStruct((query_rows, head_width), jnp.float32)
    run_max, run_total, run_accum = pl.pallas_call(
        lambda *refs: forward_kernel(softmax_scale, *refs),
        out_shape=(row_shape, row_shape, row_shape),
        in_specs=[smem, smem, vmem, vmem, vmem],
        out_specs=(vmem, vmem, vmem),
    )(listing, live_tiles.reshape(1), query_item, key_head, value_head)
    return run_max[:, 0], run_total[:, 0], run_accum


def backward_kernel(
    softmax_scale, list_ref, count_ref, q_ref, k_ref, v_ref, do_ref, log_ref, delta_ref,
    dq_ref, dk_ref, dv_ref, dq_acc, dk_acc, dv_acc,
):
    dq_acc[...] = jnp.zeros(dq_acc.shape, jnp.float32)
    dk_acc[...] = jnp.zeros(dk_acc.shape, jnp.float32)
    dv_acc[...] = jnp.zeros(dv_acc.shape, jnp.float32)
    live_tiles = jnp.clip(count_ref[0], 0, LIST_SLOTS)

    def visit(position, carry):
        query_start, key_start = tile_starts(list_ref, position)
        rows = pl.ds(query_start, QBLK)
        keys = pl.ds(key_start, KBLK)
        query_block = q_ref[rows, :]
        grad_block = do_ref[rows, :]
        key_block = k_ref[keys, :]
        value_block = v_ref[keys, :]
        scores = (
            lax.dot_general(
                query_block, key_block, (((1,), (1,)), ((), ())),
                preferred_element_type=jnp.float32,
            )
            * softmax_scale
        )
        probs = jnp.exp(scores - log_ref[rows, :])
        probs_half = probs.astype(jnp.bfloat16)
        dv_acc[keys, :] += lax.dot_general(
            probs_half, grad_block, (((0,), (0,)), ((), ())), preferred_element_type=jnp.float32
        )
        prob_grad = lax.dot_general(
            grad_block, value_block, (((1,), (1,)), ((), ())), preferred_element_type=jnp.float32
        )
        score_grad = (probs * (prob_grad - delta_ref[rows, :])).astype(jnp.bfloat16)
        dq_acc[rows, :] += (
            jnp.dot(score_grad, key_block, preferred_element_type=jnp.float32) * softmax_scale
        )
        dk_acc[keys, :] += (
            lax.dot_general(
                score_grad, query_block, (((0,), (0,)), ((), ())),
                preferred_element_type=jnp.float32,
            )
            * softmax_scale
        )
        return carry

    lax.fori_loop(0, live_tiles, visit, 0)
    dq_ref[...] = dq_acc[...].astype(dq_ref.dtype)
    dk_ref[...] = dk_acc[...].astype(dk_ref.dtype)
    dv_ref[...] = dv_acc[...].astype(dv_ref.dtype)


def backward_item(
    query_item, key_head, value_head, grad_item, log_total, deltas, listing, live_tiles, softmax_scale,
):
    query_rows, head_width = query_item.shape
    key_rows = key_head.shape[0]
    smem = pl.BlockSpec(memory_space=pltpu.SMEM)
    vmem = pl.BlockSpec(memory_space=pltpu.VMEM)
    return pl.pallas_call(
        lambda *refs: backward_kernel(softmax_scale, *refs),
        out_shape=(
            jax.ShapeDtypeStruct((query_rows, head_width), jnp.bfloat16),
            jax.ShapeDtypeStruct((key_rows, head_width), jnp.bfloat16),
            jax.ShapeDtypeStruct((key_rows, head_width), jnp.bfloat16),
        ),
        in_specs=[smem, smem] + [vmem] * 6,
        out_specs=(vmem, vmem, vmem),
        scratch_shapes=[
            pltpu.VMEM((query_rows, head_width), jnp.float32),
            pltpu.VMEM((key_rows, head_width), jnp.float32),
            pltpu.VMEM((key_rows, head_width), jnp.float32),
        ],
    )(
        listing,
        live_tiles.reshape(1),
        query_item,
        key_head,
        value_head,
        grad_item,
        log_total.reshape(query_rows, 1),
        deltas.reshape(query_rows, 1),
    )


def exchange_kernel(broadcast, x_ref, y_ref, send_sem, recv_sem):
    groups = y_ref.shape[0]
    me = lax.axis_index("grp")
    lane = lax.axis_index("seq")
    mesh_ids = pl.DeviceIdType.MESH
    barrier = pltpu.get_barrier_semaphore()
    for step in range(1, groups):
        pl.semaphore_signal(
            barrier, inc=1, device_id=(lax.rem(me + step, groups), lane), device_id_type=mesh_ids
        )
    pl.semaphore_wait(barrier, groups - 1)
    copies = []
    for step in range(1, groups):
        target = lax.rem(me + step, groups)
        copy = pltpu.make_async_remote_copy(
            src_ref=x_ref if broadcast else x_ref.at[target],
            dst_ref=y_ref.at[me],
            send_sem=send_sem.at[step],
            recv_sem=recv_sem.at[step],
            device_id=(target, lane),
            device_id_type=mesh_ids,
        )
        copy.start()
        copies.append(copy)
    y_ref[me] = x_ref[...] if broadcast else x_ref[me]
    for copy in copies:
        copy.wait()


def grp_exchange(x, groups, broadcast, collective):
    out_shape = (groups,) + (x.shape if broadcast else x.shape[1:])
    vmem = pl.BlockSpec(memory_space=pltpu.VMEM)
    return pl.pallas_call(
        lambda *refs: exchange_kernel(broadcast, *refs),
        out_shape=jax.ShapeDtypeStruct(out_shape, x.dtype),
        in_specs=[vmem],
        out_specs=vmem,
        scratch_shapes=[pltpu.SemaphoreType.DMA((groups,)), pltpu.SemaphoreType.DMA((groups,))],
        compiler_params=pltpu.CompilerParams(collective_id=collective, has_side_effects=True),
    )(x)


def reduce_kernel(x_ref, y_ref, part_ref, send_sem, recv_sem, back_send, back_recv):
    groups = y_ref.shape[0]
    me = lax.axis_index("grp")
    lane = lax.axis_index("seq")
    mesh_ids = pl.DeviceIdType.MESH
    barrier = pltpu.get_barrier_semaphore()
    for step in range(1, groups):
        pl.semaphore_signal(
            barrier, inc=1, device_id=(lax.rem(me + step, groups), lane), device_id_type=mesh_ids
        )
    pl.semaphore_wait(barrier, groups - 1)
    copies = []
    for step in range(1, groups):
        target = lax.rem(me + step, groups)
        copy = pltpu.make_async_remote_copy(
            src_ref=x_ref.at[target],
            dst_ref=part_ref.at[me],
            send_sem=send_sem.at[step],
            recv_sem=recv_sem.at[step],
            device_id=(target, lane),
            device_id_type=mesh_ids,
        )
        copy.start()
        copies.append(copy)
    part_ref[me] = x_ref[me]
    for copy in copies:
        copy.wait()
    y_ref[me] = jnp.sum(part_ref[...].astype(jnp.float32), axis=0).astype(y_ref.dtype)
    copies = []
    for step in range(1, groups):
        target = lax.rem(me + step, groups)
        copy = pltpu.make_async_remote_copy(
            src_ref=y_ref.at[me],
            dst_ref=y_ref.at[me],
            send_sem=back_send.at[step],
            recv_sem=back_recv.at[step],
            device_id=(target, lane),
            device_id_type=mesh_ids,
        )
        copy.start()
        copies.append(copy)
    for copy in copies:
        copy.wait()


def grp_reduce(x, groups, collective):
    vmem = pl.BlockSpec(memory_space=pltpu.VMEM)
    sems = pltpu.SemaphoreType.DMA((groups,))
    return pl.pallas_call(
        reduce_kernel,
        out_shape=jax.ShapeDtypeStruct(x.shape, x.dtype),
        in_specs=[vmem],
        out_specs=vmem,
        scratch_shapes=[pltpu.VMEM(x.shape, x.dtype), sems, sems, sems, sems],
        compiler_params=pltpu.CompilerParams(collective_id=collective, has_side_effects=True),
    )(x)


def scatter_rows(rows, parts, collective):
    return grp_exchange(
        rows.reshape(parts, rows.shape[0] // parts, rows.shape[1]), parts, False, collective
    )


def broadcast_rows(chunk, parts, collective):
    gathered = grp_exchange(chunk, parts, True, collective)
    return gathered.reshape(parts * chunk.shape[0], chunk.shape[1])


def per_device(queries, scene_keys, scene_values, grad_output, tile_list, tile_counts):
    items_here = queries.shape[0]
    head_width = queries.shape[2]
    query_rows = queries.shape[1]
    scene_here = scene_keys.shape[0]
    heads_total = scene_keys.shape[1] // head_width
    seq_devices = lax.axis_size("seq")
    groups = lax.axis_size("grp")
    chunk_rows = query_rows // groups
    group_keys = scene_here * seq_devices
    copies = max(1, QPARTS // items_here)
    heads_here = max(1, items_here // QPARTS)
    softmax_scale = head_width ** (-0.5)
    half_keys = scene_here // QPARTS
    both_here = jnp.stack(
        [
            scene_keys.reshape(QPARTS, half_keys, heads_total, head_width),
            scene_values.reshape(QPARTS, half_keys, heads_total, head_width),
        ],
        axis=3,
    ).transpose(2, 0, 1, 3, 4)
    mine = lax.all_to_all(
        both_here.reshape(seq_devices, half_keys, 2 * head_width), "seq", 0, 0, tiled=True
    )
    pairs = [(2 * h + c, 2 * h + 1 - c) for h in range(seq_devices // 2) for c in range(2)]
    other = lax.ppermute(mine, "seq", pairs)
    core = lax.rem(lax.axis_index("seq"), 2)
    both_group = jnp.where(
        core == 0, jnp.stack([mine, other], axis=1), jnp.stack([other, mine], axis=1)
    ).reshape(group_keys, 2 * head_width)
    key_group = both_group[:, None, :head_width]
    value_group = both_group[:, None, head_width:]
    part_max, part_total, part_accum = forward_item(
        queries[0],
        key_group[:, 0, :],
        value_group[:, 0, :],
        tile_list[0, 0],
        tile_counts[0, 0],
        softmax_scale,
    )
    total_hi = part_total.astype(jnp.bfloat16)
    total_lo = (part_total - total_hi.astype(jnp.float32)).astype(jnp.bfloat16)
    stats = jnp.stack(
        [
            jnp.concatenate(
                [part_max.astype(jnp.bfloat16).reshape(groups, chunk_rows), total_hi.reshape(groups, chunk_rows)],
                axis=1,
            ),
            jnp.concatenate(
                [total_lo.reshape(groups, chunk_rows), jnp.zeros((groups, chunk_rows), jnp.bfloat16)],
                axis=1,
            ),
        ],
        axis=1,
    )
    packed = jnp.concatenate(
        [part_accum.astype(jnp.bfloat16).reshape(groups, chunk_rows, head_width), stats], axis=1
    )
    arrived = scatter_rows(packed.reshape(groups * (chunk_rows + 2), head_width), groups, 0)
    arrived = arrived.reshape(groups, chunk_rows + 2, head_width).astype(jnp.float32)
    got_accum = arrived[:, :chunk_rows, :]
    got_max = arrived[:, chunk_rows, :chunk_rows]
    got_total = arrived[:, chunk_rows, chunk_rows:] + arrived[:, chunk_rows + 1, :chunk_rows]
    top = jnp.max(got_max, axis=0)
    shrink = jnp.exp(got_max - top[None, :])
    chunk_total = jnp.sum(got_total * shrink, axis=0)
    chunk_accum = jnp.sum(got_accum * shrink[:, :, None], axis=0)
    chunk_out = (chunk_accum / chunk_total[:, None]).astype(jnp.bfloat16)
    chunk_hi = chunk_total.astype(jnp.bfloat16)
    chunk_lo = (chunk_total - chunk_hi.astype(jnp.float32)).astype(jnp.bfloat16)
    chunk_stats = jnp.stack(
        [
            jnp.concatenate([top.astype(jnp.bfloat16), chunk_hi]),
            jnp.concatenate([chunk_lo, jnp.zeros((chunk_rows,), jnp.bfloat16)]),
        ]
    )
    back = broadcast_rows(jnp.concatenate([chunk_out, chunk_stats], axis=0), groups, 1)
    back = back.reshape(groups, chunk_rows + 2, head_width)
    attended = back[:, :chunk_rows, :].reshape(1, query_rows, head_width)
    back_stats = back[:, chunk_rows:, :].astype(jnp.float32)
    row_top = back_stats[:, 0, :chunk_rows].reshape(1, query_rows)
    row_total = (back_stats[:, 0, chunk_rows:] + back_stats[:, 1, :chunk_rows]).reshape(1, query_rows)
    log_total = row_top + jnp.log(row_total)
    deltas = jnp.sum(attended.astype(jnp.float32) * grad_output.astype(jnp.float32), axis=2)
    query_grad, key_grad, value_grad = backward_item(
        queries[0],
        key_group[:, 0, :],
        value_group[:, 0, :],
        grad_output[0],
        log_total[0],
        deltas[0],
        tile_list[0, 0],
        tile_counts[0, 0],
        softmax_scale,
    )
    both_parts = jnp.concatenate([key_grad, value_grad], axis=1).reshape(
        seq_devices, QPARTS, half_keys, 2 * head_width
    )
    kept = lax.dynamic_index_in_dim(both_parts, core, axis=1, keepdims=False)
    given = lax.dynamic_index_in_dim(both_parts, 1 - core, axis=1, keepdims=False)
    summed = (kept.astype(jnp.float32) + lax.ppermute(given, "seq", pairs).astype(jnp.float32)).astype(
        jnp.bfloat16
    )
    both_back = lax.all_to_all(summed, "seq", 0, 0, tiled=True)
    both_back = both_back.reshape(heads_total, QPARTS, half_keys, 2, head_width).transpose(1, 2, 0, 3, 4)
    both_back = both_back.reshape(scene_here, heads_total, 2, head_width)
    grad_keys = both_back[:, :, 0, :].reshape(scene_here, -1)
    grad_values = both_back[:, :, 1, :].reshape(scene_here, -1)
    grad_queries = grp_reduce(
        query_grad.reshape(groups, chunk_rows, head_width), groups, 2
    ).reshape(1, query_rows, head_width)
    return (attended, grad_queries, grad_keys, grad_values)


def solution(mesh):
    in_specs = (
        P("seq", None, None),
        P(("grp", "seq"), None),
        P(("grp", "seq"), None),
        P("seq", None, None),
        P("grp", "seq", None, None),
        P("grp", "seq"),
    )
    out_specs = (
        P("seq", None, None),
        P("seq", None, None),
        P(("grp", "seq"), None),
        P(("grp", "seq"), None),
    )
    return jax.shard_map(
        per_device, mesh=mesh, in_specs=in_specs, out_specs=out_specs, check_vma=False
    )
```

```python
import jax
import jax.numpy as jnp
from jax import lax
from jax.experimental import pallas as pl
from jax.experimental.pallas import tpu as pltpu
from jax.sharding import PartitionSpec as P

QPARTS = 2
QBLK = 512
KBLK = 512


NEG_START = -1e30


LIST_SLOTS = 9


def tile_starts(list_ref, position):
    query_block = jnp.clip(list_ref[position, 0], 0, QPARTS - 1)
    key_block = jnp.clip(list_ref[position, 1], 0, 7)
    return (
        pl.multiple_of(query_block * QBLK, QBLK),
        pl.multiple_of(key_block * KBLK, KBLK),
    )


def forward_kernel(softmax_scale, list_ref, count_ref, q_ref, k_ref, v_ref, max_ref, total_ref, accum_ref):
    max_ref[...] = jnp.full(max_ref.shape, NEG_START, jnp.float32)
    total_ref[...] = jnp.zeros(total_ref.shape, jnp.float32)
    accum_ref[...] = jnp.zeros(accum_ref.shape, jnp.float32)
    live_tiles = jnp.clip(count_ref[0], 0, LIST_SLOTS)

    def visit(position, carry):
        query_start, key_start = tile_starts(list_ref, position)
        rows = pl.ds(query_start, QBLK)
        keys = pl.ds(key_start, KBLK)
        scores = (
            lax.dot_general(
                q_ref[rows, :], k_ref[keys, :], (((1,), (1,)), ((), ())),
                preferred_element_type=jnp.float32,
            )
            * softmax_scale
        )
        old_max = max_ref[rows, :]
        new_max = jnp.maximum(old_max, jnp.max(scores, axis=1, keepdims=True))
        new_max = new_max.astype(jnp.bfloat16).astype(jnp.float32)
        weights = jnp.exp(scores - new_max[:, :1])
        shrink = jnp.exp(old_max - new_max)
        total_ref[rows, :] = total_ref[rows, :] * shrink + jnp.sum(weights, axis=1, keepdims=True)
        accum_ref[rows, :] = accum_ref[rows, :] * shrink[:, :1] + jnp.dot(
            weights.astype(jnp.bfloat16), v_ref[keys, :], preferred_element_type=jnp.float32
        )
        max_ref[rows, :] = new_max
        return carry

    lax.fori_loop(0, live_tiles, visit, 0)


def forward_item(query_item, key_head, value_head, listing, live_tiles, softmax_scale):
    query_rows, head_width = query_item.shape
    smem = pl.BlockSpec(memory_space=pltpu.SMEM)
    vmem = pl.BlockSpec(memory_space=pltpu.VMEM)
    row_shape = jax.ShapeDtypeStruct((query_rows, head_width), jnp.float32)
    run_max, run_total, run_accum = pl.pallas_call(
        lambda *refs: forward_kernel(softmax_scale, *refs),
        out_shape=(row_shape, row_shape, row_shape),
        in_specs=[smem, smem, vmem, vmem, vmem],
        out_specs=(vmem, vmem, vmem),
    )(listing, live_tiles.reshape(1), query_item, key_head, value_head)
    return run_max[:, 0], run_total[:, 0], run_accum


def backward_kernel(
    softmax_scale, list_ref, count_ref, q_ref, k_ref, v_ref, do_ref, log_ref, delta_ref,
    dq_ref, dk_ref, dv_ref, dq_acc, dk_acc, dv_acc,
):
    dq_acc[...] = jnp.zeros(dq_acc.shape, jnp.float32)
    dk_acc[...] = jnp.zeros(dk_acc.shape, jnp.float32)
    dv_acc[...] = jnp.zeros(dv_acc.shape, jnp.float32)
    live_tiles = jnp.clip(count_ref[0], 0, LIST_SLOTS)

    def visit(position, carry):
        query_start, key_start = tile_starts(list_ref, position)
        rows = pl.ds(query_start, QBLK)
        keys = pl.ds(key_start, KBLK)
        query_block = q_ref[rows, :]
        grad_block = do_ref[rows, :]
        key_block = k_ref[keys, :]
        value_block = v_ref[keys, :]
        scores = (
            lax.dot_general(
                query_block, key_block, (((1,), (1,)), ((), ())),
                preferred_element_type=jnp.float32,
            )
            * softmax_scale
        )
        probs = jnp.exp(scores - log_ref[rows, :])
        probs_half = probs.astype(jnp.bfloat16)
        dv_acc[keys, :] += lax.dot_general(
            probs_half, grad_block, (((0,), (0,)), ((), ())), preferred_element_type=jnp.float32
        )
        prob_grad = lax.dot_general(
            grad_block, value_block, (((1,), (1,)), ((), ())), preferred_element_type=jnp.float32
        )
        score_grad = (probs * (prob_grad - delta_ref[rows, :])).astype(jnp.bfloat16)
        dq_acc[rows, :] += (
            jnp.dot(score_grad, key_block, preferred_element_type=jnp.float32) * softmax_scale
        )
        dk_acc[keys, :] += (
            lax.dot_general(
                score_grad, query_block, (((0,), (0,)), ((), ())),
                preferred_element_type=jnp.float32,
            )
            * softmax_scale
        )
        return carry

    lax.fori_loop(0, live_tiles, visit, 0)
    dq_ref[...] = dq_acc[...].astype(dq_ref.dtype)
    dk_ref[...] = dk_acc[...].astype(dk_ref.dtype)
    dv_ref[...] = dv_acc[...].astype(dv_ref.dtype)


def backward_item(
    query_item, key_head, value_head, grad_item, log_total, deltas, listing, live_tiles, softmax_scale,
):
    query_rows, head_width = query_item.shape
    key_rows = key_head.shape[0]
    smem = pl.BlockSpec(memory_space=pltpu.SMEM)
    vmem = pl.BlockSpec(memory_space=pltpu.VMEM)
    return pl.pallas_call(
        lambda *refs: backward_kernel(softmax_scale, *refs),
        out_shape=(
            jax.ShapeDtypeStruct((query_rows, head_width), jnp.bfloat16),
            jax.ShapeDtypeStruct((key_rows, head_width), jnp.bfloat16),
            jax.ShapeDtypeStruct((key_rows, head_width), jnp.bfloat16),
        ),
        in_specs=[smem, smem] + [vmem] * 6,
        out_specs=(vmem, vmem, vmem),
        scratch_shapes=[
            pltpu.VMEM((query_rows, head_width), jnp.float32),
            pltpu.VMEM((key_rows, head_width), jnp.float32),
            pltpu.VMEM((key_rows, head_width), jnp.float32),
        ],
    )(
        listing,
        live_tiles.reshape(1),
        query_item,
        key_head,
        value_head,
        grad_item,
        log_total.reshape(query_rows, 1),
        deltas.reshape(query_rows, 1),
    )


def exchange_kernel(broadcast, x_ref, y_ref, send_sem, recv_sem):
    groups = y_ref.shape[0]
    me = lax.axis_index("grp")
    lane = lax.axis_index("seq")
    mesh_ids = pl.DeviceIdType.MESH
    barrier = pltpu.get_barrier_semaphore()
    for step in range(1, groups):
        pl.semaphore_signal(
            barrier, inc=1, device_id=(lax.rem(me + step, groups), lane), device_id_type=mesh_ids
        )
    pl.semaphore_wait(barrier, groups - 1)
    copies = []
    for step in range(1, groups):
        target = lax.rem(me + step, groups)
        copy = pltpu.make_async_remote_copy(
            src_ref=x_ref if broadcast else x_ref.at[target],
            dst_ref=y_ref.at[me],
            send_sem=send_sem.at[step],
            recv_sem=recv_sem.at[step],
            device_id=(target, lane),
            device_id_type=mesh_ids,
        )
        copy.start()
        copies.append(copy)
    y_ref[me] = x_ref[...] if broadcast else x_ref[me]
    for copy in copies:
        copy.wait()


def grp_exchange(x, groups, broadcast, collective):
    out_shape = (groups,) + (x.shape if broadcast else x.shape[1:])
    vmem = pl.BlockSpec(memory_space=pltpu.VMEM)
    return pl.pallas_call(
        lambda *refs: exchange_kernel(broadcast, *refs),
        out_shape=jax.ShapeDtypeStruct(out_shape, x.dtype),
        in_specs=[vmem],
        out_specs=vmem,
        scratch_shapes=[pltpu.SemaphoreType.DMA((groups,)), pltpu.SemaphoreType.DMA((groups,))],
        compiler_params=pltpu.CompilerParams(collective_id=collective, has_side_effects=True),
    )(x)


def reduce_kernel(x_ref, y_ref, part_ref, send_sem, recv_sem, back_send, back_recv):
    groups = y_ref.shape[0]
    me = lax.axis_index("grp")
    lane = lax.axis_index("seq")
    mesh_ids = pl.DeviceIdType.MESH
    barrier = pltpu.get_barrier_semaphore()
    for step in range(1, groups):
        pl.semaphore_signal(
            barrier, inc=1, device_id=(lax.rem(me + step, groups), lane), device_id_type=mesh_ids
        )
    pl.semaphore_wait(barrier, groups - 1)
    copies = []
    for step in range(1, groups):
        target = lax.rem(me + step, groups)
        copy = pltpu.make_async_remote_copy(
            src_ref=x_ref.at[target],
            dst_ref=part_ref.at[me],
            send_sem=send_sem.at[step],
            recv_sem=recv_sem.at[step],
            device_id=(target, lane),
            device_id_type=mesh_ids,
        )
        copy.start()
        copies.append(copy)
    part_ref[me] = x_ref[me]
    for copy in copies:
        copy.wait()
    y_ref[me] = jnp.sum(part_ref[...].astype(jnp.float32), axis=0).astype(y_ref.dtype)
    copies = []
    for step in range(1, groups):
        target = lax.rem(me + step, groups)
        copy = pltpu.make_async_remote_copy(
            src_ref=y_ref.at[me],
            dst_ref=y_ref.at[me],
            send_sem=back_send.at[step],
            recv_sem=back_recv.at[step],
            device_id=(target, lane),
            device_id_type=mesh_ids,
        )
        copy.start()
        copies.append(copy)
    for copy in copies:
        copy.wait()


def grp_reduce(x, groups, collective):
    vmem = pl.BlockSpec(memory_space=pltpu.VMEM)
    sems = pltpu.SemaphoreType.DMA((groups,))
    return pl.pallas_call(
        reduce_kernel,
        out_shape=jax.ShapeDtypeStruct(x.shape, x.dtype),
        in_specs=[vmem],
        out_specs=vmem,
        scratch_shapes=[pltpu.VMEM(x.shape, x.dtype), sems, sems, sems, sems],
        compiler_params=pltpu.CompilerParams(collective_id=collective, has_side_effects=True),
    )(x)


def combine_kernel(
    acc_in, stats_in, out_ref, stats_out, acc_part, stats_part,
    send_acc, recv_acc, send_stats, recv_stats, back_send, back_recv, stat_send, stat_recv,
):
    groups, chunk_rows, head_width = out_ref.shape
    me = lax.axis_index("grp")
    lane = lax.axis_index("seq")
    mesh_ids = pl.DeviceIdType.MESH
    barrier = pltpu.get_barrier_semaphore()
    for step in range(1, groups):
        pl.semaphore_signal(
            barrier, inc=1, device_id=(lax.rem(me + step, groups), lane), device_id_type=mesh_ids
        )
    pl.semaphore_wait(barrier, groups - 1)
    copies = []
    for step in range(1, groups):
        target = lax.rem(me + step, groups)
        for source, landing, sent, got in (
            (acc_in, acc_part, send_acc, recv_acc),
            (stats_in, stats_part, send_stats, recv_stats),
        ):
            copy = pltpu.make_async_remote_copy(
                src_ref=source.at[target],
                dst_ref=landing.at[me],
                send_sem=sent.at[step],
                recv_sem=got.at[step],
                device_id=(target, lane),
                device_id_type=mesh_ids,
            )
            copy.start()
            copies.append(copy)
    acc_part[me] = acc_in[me]
    stats_part[me] = stats_in[me]
    for copy in copies:
        copy.wait()
    columns = jnp.transpose(stats_part[...].reshape(groups * 8, 128))
    maxima = [columns[:chunk_rows, 8 * g : 8 * g + 1] for g in range(groups)]
    totals = [columns[chunk_rows:, 8 * g : 8 * g + 1] for g in range(groups)]
    top = maxima[0]
    for g in range(1, groups):
        top = jnp.maximum(top, maxima[g])
    row_total = jnp.zeros_like(top)
    row_accum = jnp.zeros((chunk_rows, head_width), jnp.float32)
    for g in range(groups):
        shrink = jnp.exp(maxima[g] - top)
        row_total = row_total + totals[g] * shrink
        row_accum = row_accum + acc_part[g].astype(jnp.float32) * shrink
    out_ref[me] = (row_accum / row_total).astype(out_ref.dtype)
    spread = jnp.concatenate(
        [jnp.broadcast_to(top, (chunk_rows, 128)), jnp.broadcast_to(row_total, (chunk_rows, 128))], axis=0
    )
    stats_out[me] = jnp.transpose(spread)[:8, :]
    copies = []
    for step in range(1, groups):
        target = lax.rem(me + step, groups)
        for source, sent, got in ((out_ref, back_send, back_recv), (stats_out, stat_send, stat_recv)):
            copy = pltpu.make_async_remote_copy(
                src_ref=source.at[me],
                dst_ref=source.at[me],
                send_sem=sent.at[step],
                recv_sem=got.at[step],
                device_id=(target, lane),
                device_id_type=mesh_ids,
            )
            copy.start()
            copies.append(copy)
    for copy in copies:
        copy.wait()


def grp_combine(accum, stats, collective):
    groups = accum.shape[0]
    vmem = pl.BlockSpec(memory_space=pltpu.VMEM)
    sems = pltpu.SemaphoreType.DMA((groups,))
    return pl.pallas_call(
        combine_kernel,
        out_shape=(
            jax.ShapeDtypeStruct(accum.shape, accum.dtype),
            jax.ShapeDtypeStruct(stats.shape, stats.dtype),
        ),
        in_specs=[vmem, vmem],
        out_specs=(vmem, vmem),
        scratch_shapes=[pltpu.VMEM(accum.shape, accum.dtype), pltpu.VMEM(stats.shape, stats.dtype)]
        + [sems] * 8,
        compiler_params=pltpu.CompilerParams(collective_id=collective, has_side_effects=True),
    )(accum, stats)


def scatter_rows(rows, parts, collective):
    return grp_exchange(
        rows.reshape(parts, rows.shape[0] // parts, rows.shape[1]), parts, False, collective
    )


def broadcast_rows(chunk, parts, collective):
    gathered = grp_exchange(chunk, parts, True, collective)
    return gathered.reshape(parts * chunk.shape[0], chunk.shape[1])


def per_device(queries, scene_keys, scene_values, grad_output, tile_list, tile_counts):
    items_here = queries.shape[0]
    head_width = queries.shape[2]
    query_rows = queries.shape[1]
    scene_here = scene_keys.shape[0]
    heads_total = scene_keys.shape[1] // head_width
    seq_devices = lax.axis_size("seq")
    groups = lax.axis_size("grp")
    chunk_rows = query_rows // groups
    group_keys = scene_here * seq_devices
    copies = max(1, QPARTS // items_here)
    heads_here = max(1, items_here // QPARTS)
    softmax_scale = head_width ** (-0.5)
    half_keys = scene_here // QPARTS
    both_here = jnp.stack(
        [
            scene_keys.reshape(QPARTS, half_keys, heads_total, head_width),
            scene_values.reshape(QPARTS, half_keys, heads_total, head_width),
        ],
        axis=3,
    ).transpose(2, 0, 1, 3, 4)
    mine = lax.all_to_all(
        both_here.reshape(seq_devices, half_keys, 2 * head_width), "seq", 0, 0, tiled=True
    )
    pairs = [(2 * h + c, 2 * h + 1 - c) for h in range(seq_devices // 2) for c in range(2)]
    other = lax.ppermute(mine, "seq", pairs)
    core = lax.rem(lax.axis_index("seq"), 2)
    both_group = jnp.where(
        core == 0, jnp.stack([mine, other], axis=1), jnp.stack([other, mine], axis=1)
    ).reshape(group_keys, 2 * head_width)
    key_group = both_group[:, None, :head_width]
    value_group = both_group[:, None, head_width:]
    part_max, part_total, part_accum = forward_item(
        queries[0],
        key_group[:, 0, :],
        value_group[:, 0, :],
        tile_list[0, 0],
        tile_counts[0, 0],
        softmax_scale,
    )
    stats = jnp.concatenate(
        [part_max.reshape(groups, 1, chunk_rows), part_total.reshape(groups, 1, chunk_rows)], axis=2
    )
    stats = jnp.concatenate([stats, jnp.zeros((groups, 7, 2 * chunk_rows), jnp.float32)], axis=1)
    out_rows, out_stats = grp_combine(
        part_accum.astype(jnp.bfloat16).reshape(groups, chunk_rows, head_width), stats, 0
    )
    attended = out_rows.reshape(1, query_rows, head_width)
    row_top = out_stats[:, 0, :chunk_rows].reshape(1, query_rows)
    row_total = out_stats[:, 0, chunk_rows:].reshape(1, query_rows)
    log_total = row_top + jnp.log(row_total)
    deltas = jnp.sum(attended.astype(jnp.float32) * grad_output.astype(jnp.float32), axis=2)
    query_grad, key_grad, value_grad = backward_item(
        queries[0],
        key_group[:, 0, :],
        value_group[:, 0, :],
        grad_output[0],
        log_total[0],
        deltas[0],
        tile_list[0, 0],
        tile_counts[0, 0],
        softmax_scale,
    )
    both_parts = jnp.concatenate([key_grad, value_grad], axis=1).reshape(
        seq_devices, QPARTS, half_keys, 2 * head_width
    )
    kept = lax.dynamic_index_in_dim(both_parts, core, axis=1, keepdims=False)
    given = lax.dynamic_index_in_dim(both_parts, 1 - core, axis=1, keepdims=False)
    summed = (kept.astype(jnp.float32) + lax.ppermute(given, "seq", pairs).astype(jnp.float32)).astype(
        jnp.bfloat16
    )
    both_back = lax.all_to_all(summed, "seq", 0, 0, tiled=True)
    both_back = both_back.reshape(heads_total, QPARTS, half_keys, 2, head_width).transpose(1, 2, 0, 3, 4)
    both_back = both_back.reshape(scene_here, heads_total, 2, head_width)
    grad_keys = both_back[:, :, 0, :].reshape(scene_here, -1)
    grad_values = both_back[:, :, 1, :].reshape(scene_here, -1)
    grad_queries = grp_reduce(
        query_grad.reshape(groups, chunk_rows, head_width), groups, 2
    ).reshape(1, query_rows, head_width)
    return (attended, grad_queries, grad_keys, grad_values)


def solution(mesh):
    in_specs = (
        P("seq", None, None),
        P(("grp", "seq"), None),
        P(("grp", "seq"), None),
        P("seq", None, None),
        P("grp", "seq", None, None),
        P("grp", "seq"),
    )
    out_specs = (
        P("seq", None, None),
        P("seq", None, None),
        P(("grp", "seq"), None),
        P(("grp", "seq"), None),
    )
    return jax.shard_map(
        per_device, mesh=mesh, in_specs=in_specs, out_specs=out_specs, check_vma=False
    )
```

```python
import jax
import jax.numpy as jnp
from jax import lax
from jax.experimental import pallas as pl
from jax.experimental.pallas import tpu as pltpu
from jax.sharding import PartitionSpec as P

QPARTS = 2
QBLK = 512
KBLK = 512


NEG_START = -1e30


LIST_SLOTS = 9


def tile_starts(list_ref, position):
    query_block = jnp.clip(list_ref[position, 0], 0, QPARTS - 1)
    key_block = jnp.clip(list_ref[position, 1], 0, 7)
    return (
        pl.multiple_of(query_block * QBLK, QBLK),
        pl.multiple_of(key_block * KBLK, KBLK),
    )


def forward_kernel(
    softmax_scale, list_ref, count_ref, q_ref, k_ref, v_ref, acc_out, stats_out, max_ref, total_ref, accum_ref
):
    max_ref[...] = jnp.full(max_ref.shape, NEG_START, jnp.float32)
    total_ref[...] = jnp.zeros(total_ref.shape, jnp.float32)
    accum_ref[...] = jnp.zeros(accum_ref.shape, jnp.float32)
    live_tiles = jnp.clip(count_ref[0], 0, LIST_SLOTS)

    def visit(position, carry):
        query_start, key_start = tile_starts(list_ref, position)
        rows = pl.ds(query_start, QBLK)
        keys = pl.ds(key_start, KBLK)
        scores = (
            lax.dot_general(
                q_ref[rows, :], k_ref[keys, :], (((1,), (1,)), ((), ())),
                preferred_element_type=jnp.float32,
            )
            * softmax_scale
        )
        old_max = max_ref[rows, :]
        new_max = jnp.maximum(old_max, jnp.max(scores, axis=1, keepdims=True))
        new_max = new_max.astype(jnp.bfloat16).astype(jnp.float32)
        weights = jnp.exp(scores - new_max[:, :1])
        shrink = jnp.exp(old_max - new_max)
        total_ref[rows, :] = total_ref[rows, :] * shrink + jnp.sum(weights, axis=1, keepdims=True)
        accum_ref[rows, :] = accum_ref[rows, :] * shrink[:, :1] + jnp.dot(
            weights.astype(jnp.bfloat16), v_ref[keys, :], preferred_element_type=jnp.float32
        )
        max_ref[rows, :] = new_max
        return carry

    lax.fori_loop(0, live_tiles, visit, 0)
    groups, chunk_rows = acc_out.shape[0], acc_out.shape[1]
    for g in range(groups):
        rows = pl.ds(g * chunk_rows, chunk_rows)
        acc_out[g] = accum_ref[rows, :].astype(acc_out.dtype)
        stacked = jnp.concatenate([max_ref[rows, :], total_ref[rows, :]], axis=0)
        stats_out[g] = jnp.transpose(stacked)[:8, :]


def forward_item(query_item, key_head, value_head, listing, live_tiles, softmax_scale, groups):
    query_rows, head_width = query_item.shape
    chunk_rows = query_rows // groups
    smem = pl.BlockSpec(memory_space=pltpu.SMEM)
    vmem = pl.BlockSpec(memory_space=pltpu.VMEM)
    rows_f32 = pltpu.VMEM((query_rows, head_width), jnp.float32)
    return pl.pallas_call(
        lambda *refs: forward_kernel(softmax_scale, *refs),
        out_shape=(
            jax.ShapeDtypeStruct((groups, chunk_rows, head_width), jnp.bfloat16),
            jax.ShapeDtypeStruct((groups, 8, 2 * chunk_rows), jnp.float32),
        ),
        in_specs=[smem, smem, vmem, vmem, vmem],
        out_specs=(vmem, vmem),
        scratch_shapes=[rows_f32, rows_f32, rows_f32],
    )(listing, live_tiles.reshape(1), query_item, key_head, value_head)


def backward_kernel(
    softmax_scale, list_ref, count_ref, q_ref, k_ref, v_ref, do_ref, att_ref, stats_ref,
    dq_ref, dk_ref, dv_ref, dq_acc, dk_acc, dv_acc, log_ref, delta_ref,
):
    groups = stats_ref.shape[0]
    chunk_rows = stats_ref.shape[2] // 2
    for g in range(groups):
        rows = pl.ds(g * chunk_rows, chunk_rows)
        columns = jnp.transpose(jnp.broadcast_to(stats_ref[g][0:1, :], (2 * chunk_rows, 2 * chunk_rows)))
        log_ref[rows, :] = columns[:chunk_rows, 0:1] + jnp.log(columns[chunk_rows:, 0:1])
        delta_ref[rows, :] = jnp.sum(
            att_ref[rows, :].astype(jnp.float32) * do_ref[rows, :].astype(jnp.float32),
            axis=1,
            keepdims=True,
        )
    dq_acc[...] = jnp.zeros(dq_acc.shape, jnp.float32)
    dk_acc[...] = jnp.zeros(dk_acc.shape, jnp.float32)
    dv_acc[...] = jnp.zeros(dv_acc.shape, jnp.float32)
    live_tiles = jnp.clip(count_ref[0], 0, LIST_SLOTS)

    def visit(position, carry):
        query_start, key_start = tile_starts(list_ref, position)
        rows = pl.ds(query_start, QBLK)
        keys = pl.ds(key_start, KBLK)
        query_block = q_ref[rows, :]
        grad_block = do_ref[rows, :]
        key_block = k_ref[keys, :]
        value_block = v_ref[keys, :]
        scores = (
            lax.dot_general(
                query_block, key_block, (((1,), (1,)), ((), ())),
                preferred_element_type=jnp.float32,
            )
            * softmax_scale
        )
        probs = jnp.exp(scores - log_ref[rows, :])
        probs_half = probs.astype(jnp.bfloat16)
        dv_acc[keys, :] += lax.dot_general(
            probs_half, grad_block, (((0,), (0,)), ((), ())), preferred_element_type=jnp.float32
        )
        prob_grad = lax.dot_general(
            grad_block, value_block, (((1,), (1,)), ((), ())), preferred_element_type=jnp.float32
        )
        score_grad = (probs * (prob_grad - delta_ref[rows, :])).astype(jnp.bfloat16)
        dq_acc[rows, :] += (
            jnp.dot(score_grad, key_block, preferred_element_type=jnp.float32) * softmax_scale
        )
        dk_acc[keys, :] += (
            lax.dot_general(
                score_grad, query_block, (((0,), (0,)), ((), ())),
                preferred_element_type=jnp.float32,
            )
            * softmax_scale
        )
        return carry

    lax.fori_loop(0, live_tiles, visit, 0)
    dq_ref[...] = dq_acc[...].astype(dq_ref.dtype)
    dk_ref[...] = dk_acc[...].astype(dk_ref.dtype)
    dv_ref[...] = dv_acc[...].astype(dv_ref.dtype)


def backward_item(
    query_item, key_head, value_head, grad_item, attended, stats, listing, live_tiles, softmax_scale,
):
    query_rows, head_width = query_item.shape
    key_rows = key_head.shape[0]
    smem = pl.BlockSpec(memory_space=pltpu.SMEM)
    vmem = pl.BlockSpec(memory_space=pltpu.VMEM)
    return pl.pallas_call(
        lambda *refs: backward_kernel(softmax_scale, *refs),
        out_shape=(
            jax.ShapeDtypeStruct((query_rows, head_width), jnp.bfloat16),
            jax.ShapeDtypeStruct((key_rows, head_width), jnp.bfloat16),
            jax.ShapeDtypeStruct((key_rows, head_width), jnp.bfloat16),
        ),
        in_specs=[smem, smem] + [vmem] * 6,
        out_specs=(vmem, vmem, vmem),
        scratch_shapes=[
            pltpu.VMEM((query_rows, head_width), jnp.float32),
            pltpu.VMEM((key_rows, head_width), jnp.float32),
            pltpu.VMEM((key_rows, head_width), jnp.float32),
            pltpu.VMEM((query_rows, 1), jnp.float32),
            pltpu.VMEM((query_rows, 1), jnp.float32),
        ],
    )(
        listing,
        live_tiles.reshape(1),
        query_item,
        key_head,
        value_head,
        grad_item,
        attended,
        stats,
    )


def exchange_kernel(broadcast, x_ref, y_ref, send_sem, recv_sem):
    groups = y_ref.shape[0]
    me = lax.axis_index("grp")
    lane = lax.axis_index("seq")
    mesh_ids = pl.DeviceIdType.MESH
    barrier = pltpu.get_barrier_semaphore()
    for step in range(1, groups):
        pl.semaphore_signal(
            barrier, inc=1, device_id=(lax.rem(me + step, groups), lane), device_id_type=mesh_ids
        )
    pl.semaphore_wait(barrier, groups - 1)
    copies = []
    for step in range(1, groups):
        target = lax.rem(me + step, groups)
        copy = pltpu.make_async_remote_copy(
            src_ref=x_ref if broadcast else x_ref.at[target],
            dst_ref=y_ref.at[me],
            send_sem=send_sem.at[step],
            recv_sem=recv_sem.at[step],
            device_id=(target, lane),
            device_id_type=mesh_ids,
        )
        copy.start()
        copies.append(copy)
    y_ref[me] = x_ref[...] if broadcast else x_ref[me]
    for copy in copies:
        copy.wait()


def grp_exchange(x, groups, broadcast, collective):
    out_shape = (groups,) + (x.shape if broadcast else x.shape[1:])
    vmem = pl.BlockSpec(memory_space=pltpu.VMEM)
    return pl.pallas_call(
        lambda *refs: exchange_kernel(broadcast, *refs),
        out_shape=jax.ShapeDtypeStruct(out_shape, x.dtype),
        in_specs=[vmem],
        out_specs=vmem,
        scratch_shapes=[pltpu.SemaphoreType.DMA((groups,)), pltpu.SemaphoreType.DMA((groups,))],
        compiler_params=pltpu.CompilerParams(collective_id=collective, has_side_effects=True),
    )(x)


def reduce_kernel(x_ref, y_ref, part_ref, send_sem, recv_sem, back_send, back_recv):
    groups = y_ref.shape[0]
    me = lax.axis_index("grp")
    lane = lax.axis_index("seq")
    mesh_ids = pl.DeviceIdType.MESH
    barrier = pltpu.get_barrier_semaphore()
    for step in range(1, groups):
        pl.semaphore_signal(
            barrier, inc=1, device_id=(lax.rem(me + step, groups), lane), device_id_type=mesh_ids
        )
    pl.semaphore_wait(barrier, groups - 1)
    copies = []
    for step in range(1, groups):
        target = lax.rem(me + step, groups)
        copy = pltpu.make_async_remote_copy(
            src_ref=x_ref.at[target],
            dst_ref=part_ref.at[me],
            send_sem=send_sem.at[step],
            recv_sem=recv_sem.at[step],
            device_id=(target, lane),
            device_id_type=mesh_ids,
        )
        copy.start()
        copies.append(copy)
    part_ref[me] = x_ref[me]
    for copy in copies:
        copy.wait()
    y_ref[me] = jnp.sum(part_ref[...].astype(jnp.float32), axis=0).astype(y_ref.dtype)
    copies = []
    for step in range(1, groups):
        target = lax.rem(me + step, groups)
        copy = pltpu.make_async_remote_copy(
            src_ref=y_ref.at[me],
            dst_ref=y_ref.at[me],
            send_sem=back_send.at[step],
            recv_sem=back_recv.at[step],
            device_id=(target, lane),
            device_id_type=mesh_ids,
        )
        copy.start()
        copies.append(copy)
    for copy in copies:
        copy.wait()


def grp_reduce(x, groups, collective):
    vmem = pl.BlockSpec(memory_space=pltpu.VMEM)
    sems = pltpu.SemaphoreType.DMA((groups,))
    return pl.pallas_call(
        reduce_kernel,
        out_shape=jax.ShapeDtypeStruct(x.shape, x.dtype),
        in_specs=[vmem],
        out_specs=vmem,
        scratch_shapes=[pltpu.VMEM(x.shape, x.dtype), sems, sems, sems, sems],
        compiler_params=pltpu.CompilerParams(collective_id=collective, has_side_effects=True),
    )(x)


def combine_kernel(
    acc_in, stats_in, out_ref, stats_out, acc_part, stats_part,
    send_acc, recv_acc, send_stats, recv_stats, back_send, back_recv, stat_send, stat_recv,
):
    groups, chunk_rows, head_width = out_ref.shape
    me = lax.axis_index("grp")
    lane = lax.axis_index("seq")
    mesh_ids = pl.DeviceIdType.MESH
    barrier = pltpu.get_barrier_semaphore()
    for step in range(1, groups):
        pl.semaphore_signal(
            barrier, inc=1, device_id=(lax.rem(me + step, groups), lane), device_id_type=mesh_ids
        )
    pl.semaphore_wait(barrier, groups - 1)
    copies = []
    for step in range(1, groups):
        target = lax.rem(me + step, groups)
        for source, landing, sent, got in (
            (acc_in, acc_part, send_acc, recv_acc),
            (stats_in, stats_part, send_stats, recv_stats),
        ):
            copy = pltpu.make_async_remote_copy(
                src_ref=source.at[target],
                dst_ref=landing.at[me],
                send_sem=sent.at[step],
                recv_sem=got.at[step],
                device_id=(target, lane),
                device_id_type=mesh_ids,
            )
            copy.start()
            copies.append(copy)
    acc_part[me] = acc_in[me]
    stats_part[me] = stats_in[me]
    for copy in copies:
        copy.wait()
    columns = jnp.transpose(stats_part[...].reshape(groups * 8, 128))
    maxima = [columns[:chunk_rows, 8 * g : 8 * g + 1] for g in range(groups)]
    totals = [columns[chunk_rows:, 8 * g : 8 * g + 1] for g in range(groups)]
    top = maxima[0]
    for g in range(1, groups):
        top = jnp.maximum(top, maxima[g])
    row_total = jnp.zeros_like(top)
    row_accum = jnp.zeros((chunk_rows, head_width), jnp.float32)
    for g in range(groups):
        shrink = jnp.exp(maxima[g] - top)
        row_total = row_total + totals[g] * shrink
        row_accum = row_accum + acc_part[g].astype(jnp.float32) * shrink
    out_ref[me] = (row_accum / row_total).astype(out_ref.dtype)
    spread = jnp.concatenate(
        [jnp.broadcast_to(top, (chunk_rows, 128)), jnp.broadcast_to(row_total, (chunk_rows, 128))], axis=0
    )
    stats_out[me] = jnp.transpose(spread)[:8, :]
    copies = []
    for step in range(1, groups):
        target = lax.rem(me + step, groups)
        for source, sent, got in ((out_ref, back_send, back_recv), (stats_out, stat_send, stat_recv)):
            copy = pltpu.make_async_remote_copy(
                src_ref=source.at[me],
                dst_ref=source.at[me],
                send_sem=sent.at[step],
                recv_sem=got.at[step],
                device_id=(target, lane),
                device_id_type=mesh_ids,
            )
            copy.start()
            copies.append(copy)
    for copy in copies:
        copy.wait()


def grp_combine(accum, stats, collective):
    groups = accum.shape[0]
    vmem = pl.BlockSpec(memory_space=pltpu.VMEM)
    sems = pltpu.SemaphoreType.DMA((groups,))
    return pl.pallas_call(
        combine_kernel,
        out_shape=(
            jax.ShapeDtypeStruct(accum.shape, accum.dtype),
            jax.ShapeDtypeStruct(stats.shape, stats.dtype),
        ),
        in_specs=[vmem, vmem],
        out_specs=(vmem, vmem),
        scratch_shapes=[pltpu.VMEM(accum.shape, accum.dtype), pltpu.VMEM(stats.shape, stats.dtype)]
        + [sems] * 8,
        compiler_params=pltpu.CompilerParams(collective_id=collective, has_side_effects=True),
    )(accum, stats)


def scatter_rows(rows, parts, collective):
    return grp_exchange(
        rows.reshape(parts, rows.shape[0] // parts, rows.shape[1]), parts, False, collective
    )


def broadcast_rows(chunk, parts, collective):
    gathered = grp_exchange(chunk, parts, True, collective)
    return gathered.reshape(parts * chunk.shape[0], chunk.shape[1])


def per_device(queries, scene_keys, scene_values, grad_output, tile_list, tile_counts):
    items_here = queries.shape[0]
    head_width = queries.shape[2]
    query_rows = queries.shape[1]
    scene_here = scene_keys.shape[0]
    heads_total = scene_keys.shape[1] // head_width
    seq_devices = lax.axis_size("seq")
    groups = lax.axis_size("grp")
    chunk_rows = query_rows // groups
    group_keys = scene_here * seq_devices
    copies = max(1, QPARTS // items_here)
    heads_here = max(1, items_here // QPARTS)
    softmax_scale = head_width ** (-0.5)
    half_keys = scene_here // QPARTS
    both_here = jnp.stack(
        [
            scene_keys.reshape(QPARTS, half_keys, heads_total, head_width),
            scene_values.reshape(QPARTS, half_keys, heads_total, head_width),
        ],
        axis=3,
    ).transpose(2, 0, 1, 3, 4)
    mine = lax.all_to_all(
        both_here.reshape(seq_devices, half_keys, 2 * head_width), "seq", 0, 0, tiled=True
    )
    pairs = [(2 * h + c, 2 * h + 1 - c) for h in range(seq_devices // 2) for c in range(2)]
    other = lax.ppermute(mine, "seq", pairs)
    core = lax.rem(lax.axis_index("seq"), 2)
    both_group = jnp.where(
        core == 0, jnp.stack([mine, other], axis=1), jnp.stack([other, mine], axis=1)
    ).reshape(group_keys, 2 * head_width)
    key_group = both_group[:, None, :head_width]
    value_group = both_group[:, None, head_width:]
    part_accum, stats = forward_item(
        queries[0],
        key_group[:, 0, :],
        value_group[:, 0, :],
        tile_list[0, 0],
        tile_counts[0, 0],
        softmax_scale,
        groups,
    )
    out_rows, out_stats = grp_combine(part_accum, stats, 0)
    attended = out_rows.reshape(1, query_rows, head_width)
    query_grad, key_grad, value_grad = backward_item(
        queries[0],
        key_group[:, 0, :],
        value_group[:, 0, :],
        grad_output[0],
        attended[0],
        out_stats,
        tile_list[0, 0],
        tile_counts[0, 0],
        softmax_scale,
    )
    both_parts = jnp.concatenate([key_grad, value_grad], axis=1).reshape(
        seq_devices, QPARTS, half_keys, 2 * head_width
    )
    kept = lax.dynamic_index_in_dim(both_parts, core, axis=1, keepdims=False)
    given = lax.dynamic_index_in_dim(both_parts, 1 - core, axis=1, keepdims=False)
    summed = (kept.astype(jnp.float32) + lax.ppermute(given, "seq", pairs).astype(jnp.float32)).astype(
        jnp.bfloat16
    )
    both_back = lax.all_to_all(summed, "seq", 0, 0, tiled=True)
    both_back = both_back.reshape(heads_total, QPARTS, half_keys, 2, head_width).transpose(1, 2, 0, 3, 4)
    both_back = both_back.reshape(scene_here, heads_total, 2, head_width)
    grad_keys = both_back[:, :, 0, :].reshape(scene_here, -1)
    grad_values = both_back[:, :, 1, :].reshape(scene_here, -1)
    grad_queries = grp_reduce(
        query_grad.reshape(groups, chunk_rows, head_width), groups, 2
    ).reshape(1, query_rows, head_width)
    return (attended, grad_queries, grad_keys, grad_values)


def solution(mesh):
    in_specs = (
        P("seq", None, None),
        P(("grp", "seq"), None),
        P(("grp", "seq"), None),
        P("seq", None, None),
        P("grp", "seq", None, None),
        P("grp", "seq"),
    )
    out_specs = (
        P("seq", None, None),
        P("seq", None, None),
        P(("grp", "seq"), None),
        P(("grp", "seq"), None),
    )
    return jax.shard_map(
        per_device, mesh=mesh, in_specs=in_specs, out_specs=out_specs, check_vma=False
    )
```

```python
import jax
import jax.numpy as jnp
from jax import lax
from jax.experimental import pallas as pl
from jax.experimental.pallas import tpu as pltpu
from jax.sharding import PartitionSpec as P

QPARTS = 2
QBLK = 512
KBLK = 512


NEG_START = -1e30


LIST_SLOTS = 9


def tile_starts(list_ref, position):
    query_block = jnp.clip(list_ref[position, 0], 0, QPARTS - 1)
    key_block = jnp.clip(list_ref[position, 1], 0, 7)
    return (
        pl.multiple_of(query_block * QBLK, QBLK),
        pl.multiple_of(key_block * KBLK, KBLK),
    )


def forward_kernel(
    softmax_scale, list_ref, count_ref, q_ref, k_ref, v_ref, acc_out, stats_out, max_ref, total_ref, accum_ref
):
    max_ref[...] = jnp.full(max_ref.shape, NEG_START, jnp.float32)
    total_ref[...] = jnp.zeros(total_ref.shape, jnp.float32)
    accum_ref[...] = jnp.zeros(accum_ref.shape, jnp.float32)
    live_tiles = jnp.clip(count_ref[0], 0, LIST_SLOTS)

    def visit(position, carry):
        query_start, key_start = tile_starts(list_ref, position)
        rows = pl.ds(query_start, QBLK)
        keys = pl.ds(key_start, KBLK)
        scores = (
            lax.dot_general(
                q_ref[rows, :], k_ref[keys, :], (((1,), (1,)), ((), ())),
                preferred_element_type=jnp.float32,
            )
            * softmax_scale
        )
        old_max = max_ref[rows, :]
        new_max = jnp.maximum(old_max, jnp.max(scores, axis=1, keepdims=True))
        new_max = new_max.astype(jnp.bfloat16).astype(jnp.float32)
        weights = jnp.exp(scores - new_max[:, :1])
        shrink = jnp.exp(old_max - new_max)
        total_ref[rows, :] = total_ref[rows, :] * shrink + jnp.sum(weights, axis=1, keepdims=True)
        accum_ref[rows, :] = accum_ref[rows, :] * shrink[:, :1] + jnp.dot(
            weights.astype(jnp.bfloat16), v_ref[keys, :], preferred_element_type=jnp.float32
        )
        max_ref[rows, :] = new_max
        return carry

    lax.fori_loop(0, live_tiles, visit, 0)
    groups, chunk_rows = acc_out.shape[0], acc_out.shape[1]
    for g in range(groups):
        rows = pl.ds(g * chunk_rows, chunk_rows)
        acc_out[g] = accum_ref[rows, :].astype(acc_out.dtype)
        stacked = jnp.concatenate([max_ref[rows, :], total_ref[rows, :]], axis=0)
        stats_out[g] = jnp.transpose(stacked)[:8, :]


def forward_item(query_item, key_head, value_head, listing, live_tiles, softmax_scale, groups):
    query_rows, head_width = query_item.shape
    chunk_rows = query_rows // groups
    smem = pl.BlockSpec(memory_space=pltpu.SMEM)
    vmem = pl.BlockSpec(memory_space=pltpu.VMEM)
    rows_f32 = pltpu.VMEM((query_rows, head_width), jnp.float32)
    return pl.pallas_call(
        lambda *refs: forward_kernel(softmax_scale, *refs),
        out_shape=(
            jax.ShapeDtypeStruct((groups, chunk_rows, head_width), jnp.bfloat16),
            jax.ShapeDtypeStruct((groups, 8, 2 * chunk_rows), jnp.float32),
        ),
        in_specs=[smem, smem, vmem, vmem, vmem],
        out_specs=(vmem, vmem),
        scratch_shapes=[rows_f32, rows_f32, rows_f32],
    )(listing, live_tiles.reshape(1), query_item, key_head, value_head)


def backward_kernel(
    softmax_scale, list_ref, count_ref, q_ref, k_ref, v_ref, do_ref, att_ref, stats_ref,
    dq_ref, kept_ref, given_ref, dq_acc, dk_acc, dv_acc, log_ref, delta_ref,
):
    groups = stats_ref.shape[0]
    chunk_rows = stats_ref.shape[2] // 2
    for g in range(groups):
        rows = pl.ds(g * chunk_rows, chunk_rows)
        columns = jnp.transpose(jnp.broadcast_to(stats_ref[g][0:1, :], (2 * chunk_rows, 2 * chunk_rows)))
        log_ref[rows, :] = columns[:chunk_rows, 0:1] + jnp.log(columns[chunk_rows:, 0:1])
        delta_ref[rows, :] = jnp.sum(
            att_ref[rows, :].astype(jnp.float32) * do_ref[rows, :].astype(jnp.float32),
            axis=1,
            keepdims=True,
        )
    dq_acc[...] = jnp.zeros(dq_acc.shape, jnp.float32)
    dk_acc[...] = jnp.zeros(dk_acc.shape, jnp.float32)
    dv_acc[...] = jnp.zeros(dv_acc.shape, jnp.float32)
    live_tiles = jnp.clip(count_ref[0], 0, LIST_SLOTS)

    def visit(position, carry):
        query_start, key_start = tile_starts(list_ref, position)
        rows = pl.ds(query_start, QBLK)
        keys = pl.ds(key_start, KBLK)
        query_block = q_ref[rows, :]
        grad_block = do_ref[rows, :]
        key_block = k_ref[keys, :]
        value_block = v_ref[keys, :]
        scores = (
            lax.dot_general(
                query_block, key_block, (((1,), (1,)), ((), ())),
                preferred_element_type=jnp.float32,
            )
            * softmax_scale
        )
        probs = jnp.exp(scores - log_ref[rows, :])
        probs_half = probs.astype(jnp.bfloat16)
        dv_acc[keys, :] += lax.dot_general(
            probs_half, grad_block, (((0,), (0,)), ((), ())), preferred_element_type=jnp.float32
        )
        prob_grad = lax.dot_general(
            grad_block, value_block, (((1,), (1,)), ((), ())), preferred_element_type=jnp.float32
        )
        score_grad = (probs * (prob_grad - delta_ref[rows, :])).astype(jnp.bfloat16)
        dq_acc[rows, :] += (
            jnp.dot(score_grad, key_block, preferred_element_type=jnp.float32) * softmax_scale
        )
        dk_acc[keys, :] += (
            lax.dot_general(
                score_grad, query_block, (((0,), (0,)), ((), ())),
                preferred_element_type=jnp.float32,
            )
            * softmax_scale
        )
        return carry

    lax.fori_loop(0, live_tiles, visit, 0)
    dq_ref[...] = dq_acc[...].astype(dq_ref.dtype)
    sources, half, width = kept_ref.shape
    head_width = width // 2
    core = lax.rem(lax.axis_index("seq"), 2)
    for source in range(sources):
        for out_ref, which in ((kept_ref, core), (given_ref, 1 - core)):
            rows = pl.ds(pl.multiple_of(source * 2 * half + which * half, half), half)
            out_ref[source, :, :head_width] = dk_acc[rows, :].astype(out_ref.dtype)
            out_ref[source, :, head_width:] = dv_acc[rows, :].astype(out_ref.dtype)


def backward_item(
    query_item, key_head, value_head, grad_item, attended, stats, listing, live_tiles, softmax_scale,
):
    query_rows, head_width = query_item.shape
    key_rows = key_head.shape[0]
    sources = lax.axis_size("seq")
    halves = (sources, key_rows // sources // QPARTS, 2 * head_width)
    smem = pl.BlockSpec(memory_space=pltpu.SMEM)
    vmem = pl.BlockSpec(memory_space=pltpu.VMEM)
    return pl.pallas_call(
        lambda *refs: backward_kernel(softmax_scale, *refs),
        out_shape=(
            jax.ShapeDtypeStruct((query_rows, head_width), jnp.bfloat16),
            jax.ShapeDtypeStruct(halves, jnp.bfloat16),
            jax.ShapeDtypeStruct(halves, jnp.bfloat16),
        ),
        in_specs=[smem, smem] + [vmem] * 6,
        out_specs=(vmem, vmem, vmem),
        scratch_shapes=[
            pltpu.VMEM((query_rows, head_width), jnp.float32),
            pltpu.VMEM((key_rows, head_width), jnp.float32),
            pltpu.VMEM((key_rows, head_width), jnp.float32),
            pltpu.VMEM((query_rows, 1), jnp.float32),
            pltpu.VMEM((query_rows, 1), jnp.float32),
        ],
    )(
        listing,
        live_tiles.reshape(1),
        query_item,
        key_head,
        value_head,
        grad_item,
        attended,
        stats,
    )


def exchange_kernel(broadcast, x_ref, y_ref, send_sem, recv_sem):
    groups = y_ref.shape[0]
    me = lax.axis_index("grp")
    lane = lax.axis_index("seq")
    mesh_ids = pl.DeviceIdType.MESH
    barrier = pltpu.get_barrier_semaphore()
    for step in range(1, groups):
        pl.semaphore_signal(
            barrier, inc=1, device_id=(lax.rem(me + step, groups), lane), device_id_type=mesh_ids
        )
    pl.semaphore_wait(barrier, groups - 1)
    copies = []
    for step in range(1, groups):
        target = lax.rem(me + step, groups)
        copy = pltpu.make_async_remote_copy(
            src_ref=x_ref if broadcast else x_ref.at[target],
            dst_ref=y_ref.at[me],
            send_sem=send_sem.at[step],
            recv_sem=recv_sem.at[step],
            device_id=(target, lane),
            device_id_type=mesh_ids,
        )
        copy.start()
        copies.append(copy)
    y_ref[me] = x_ref[...] if broadcast else x_ref[me]
    for copy in copies:
        copy.wait()


def grp_exchange(x, groups, broadcast, collective):
    out_shape = (groups,) + (x.shape if broadcast else x.shape[1:])
    vmem = pl.BlockSpec(memory_space=pltpu.VMEM)
    return pl.pallas_call(
        lambda *refs: exchange_kernel(broadcast, *refs),
        out_shape=jax.ShapeDtypeStruct(out_shape, x.dtype),
        in_specs=[vmem],
        out_specs=vmem,
        scratch_shapes=[pltpu.SemaphoreType.DMA((groups,)), pltpu.SemaphoreType.DMA((groups,))],
        compiler_params=pltpu.CompilerParams(collective_id=collective, has_side_effects=True),
    )(x)


def reduce_kernel(x_ref, y_ref, part_ref, send_sem, recv_sem, back_send, back_recv):
    groups = y_ref.shape[0]
    me = lax.axis_index("grp")
    lane = lax.axis_index("seq")
    mesh_ids = pl.DeviceIdType.MESH
    barrier = pltpu.get_barrier_semaphore()
    for step in range(1, groups):
        pl.semaphore_signal(
            barrier, inc=1, device_id=(lax.rem(me + step, groups), lane), device_id_type=mesh_ids
        )
    pl.semaphore_wait(barrier, groups - 1)
    copies = []
    for step in range(1, groups):
        target = lax.rem(me + step, groups)
        copy = pltpu.make_async_remote_copy(
            src_ref=x_ref.at[target],
            dst_ref=part_ref.at[me],
            send_sem=send_sem.at[step],
            recv_sem=recv_sem.at[step],
            device_id=(target, lane),
            device_id_type=mesh_ids,
        )
        copy.start()
        copies.append(copy)
    part_ref[me] = x_ref[me]
    for copy in copies:
        copy.wait()
    y_ref[me] = jnp.sum(part_ref[...].astype(jnp.float32), axis=0).astype(y_ref.dtype)
    copies = []
    for step in range(1, groups):
        target = lax.rem(me + step, groups)
        copy = pltpu.make_async_remote_copy(
            src_ref=y_ref.at[me],
            dst_ref=y_ref.at[me],
            send_sem=back_send.at[step],
            recv_sem=back_recv.at[step],
            device_id=(target, lane),
            device_id_type=mesh_ids,
        )
        copy.start()
        copies.append(copy)
    for copy in copies:
        copy.wait()


def grp_reduce(x, groups, collective):
    vmem = pl.BlockSpec(memory_space=pltpu.VMEM)
    sems = pltpu.SemaphoreType.DMA((groups,))
    return pl.pallas_call(
        reduce_kernel,
        out_shape=jax.ShapeDtypeStruct(x.shape, x.dtype),
        in_specs=[vmem],
        out_specs=vmem,
        scratch_shapes=[pltpu.VMEM(x.shape, x.dtype), sems, sems, sems, sems],
        compiler_params=pltpu.CompilerParams(collective_id=collective, has_side_effects=True),
    )(x)


def combine_kernel(
    acc_in, stats_in, out_ref, stats_out, acc_part, stats_part,
    send_acc, recv_acc, send_stats, recv_stats, back_send, back_recv, stat_send, stat_recv,
):
    groups, chunk_rows, head_width = out_ref.shape
    me = lax.axis_index("grp")
    lane = lax.axis_index("seq")
    mesh_ids = pl.DeviceIdType.MESH
    barrier = pltpu.get_barrier_semaphore()
    for step in range(1, groups):
        pl.semaphore_signal(
            barrier, inc=1, device_id=(lax.rem(me + step, groups), lane), device_id_type=mesh_ids
        )
    pl.semaphore_wait(barrier, groups - 1)
    copies = []
    for step in range(1, groups):
        target = lax.rem(me + step, groups)
        for source, landing, sent, got in (
            (acc_in, acc_part, send_acc, recv_acc),
            (stats_in, stats_part, send_stats, recv_stats),
        ):
            copy = pltpu.make_async_remote_copy(
                src_ref=source.at[target],
                dst_ref=landing.at[me],
                send_sem=sent.at[step],
                recv_sem=got.at[step],
                device_id=(target, lane),
                device_id_type=mesh_ids,
            )
            copy.start()
            copies.append(copy)
    acc_part[me] = acc_in[me]
    stats_part[me] = stats_in[me]
    for copy in copies:
        copy.wait()
    columns = jnp.transpose(stats_part[...].reshape(groups * 8, 128))
    maxima = [columns[:chunk_rows, 8 * g : 8 * g + 1] for g in range(groups)]
    totals = [columns[chunk_rows:, 8 * g : 8 * g + 1] for g in range(groups)]
    top = maxima[0]
    for g in range(1, groups):
        top = jnp.maximum(top, maxima[g])
    row_total = jnp.zeros_like(top)
    row_accum = jnp.zeros((chunk_rows, head_width), jnp.float32)
    for g in range(groups):
        shrink = jnp.exp(maxima[g] - top)
        row_total = row_total + totals[g] * shrink
        row_accum = row_accum + acc_part[g].astype(jnp.float32) * shrink
    out_ref[me] = (row_accum / row_total).astype(out_ref.dtype)
    spread = jnp.concatenate(
        [jnp.broadcast_to(top, (chunk_rows, 128)), jnp.broadcast_to(row_total, (chunk_rows, 128))], axis=0
    )
    stats_out[me] = jnp.transpose(spread)[:8, :]
    copies = []
    for step in range(1, groups):
        target = lax.rem(me + step, groups)
        for source, sent, got in ((out_ref, back_send, back_recv), (stats_out, stat_send, stat_recv)):
            copy = pltpu.make_async_remote_copy(
                src_ref=source.at[me],
                dst_ref=source.at[me],
                send_sem=sent.at[step],
                recv_sem=got.at[step],
                device_id=(target, lane),
                device_id_type=mesh_ids,
            )
            copy.start()
            copies.append(copy)
    for copy in copies:
        copy.wait()


def grp_combine(accum, stats, collective):
    groups = accum.shape[0]
    vmem = pl.BlockSpec(memory_space=pltpu.VMEM)
    sems = pltpu.SemaphoreType.DMA((groups,))
    return pl.pallas_call(
        combine_kernel,
        out_shape=(
            jax.ShapeDtypeStruct(accum.shape, accum.dtype),
            jax.ShapeDtypeStruct(stats.shape, stats.dtype),
        ),
        in_specs=[vmem, vmem],
        out_specs=(vmem, vmem),
        scratch_shapes=[pltpu.VMEM(accum.shape, accum.dtype), pltpu.VMEM(stats.shape, stats.dtype)]
        + [sems] * 8,
        compiler_params=pltpu.CompilerParams(collective_id=collective, has_side_effects=True),
    )(accum, stats)


def scatter_rows(rows, parts, collective):
    return grp_exchange(
        rows.reshape(parts, rows.shape[0] // parts, rows.shape[1]), parts, False, collective
    )


def broadcast_rows(chunk, parts, collective):
    gathered = grp_exchange(chunk, parts, True, collective)
    return gathered.reshape(parts * chunk.shape[0], chunk.shape[1])


def per_device(queries, scene_keys, scene_values, grad_output, tile_list, tile_counts):
    items_here = queries.shape[0]
    head_width = queries.shape[2]
    query_rows = queries.shape[1]
    scene_here = scene_keys.shape[0]
    heads_total = scene_keys.shape[1] // head_width
    seq_devices = lax.axis_size("seq")
    groups = lax.axis_size("grp")
    chunk_rows = query_rows // groups
    group_keys = scene_here * seq_devices
    copies = max(1, QPARTS // items_here)
    heads_here = max(1, items_here // QPARTS)
    softmax_scale = head_width ** (-0.5)
    half_keys = scene_here // QPARTS
    both_here = jnp.stack(
        [
            scene_keys.reshape(QPARTS, half_keys, heads_total, head_width),
            scene_values.reshape(QPARTS, half_keys, heads_total, head_width),
        ],
        axis=3,
    ).transpose(2, 0, 1, 3, 4)
    mine = lax.all_to_all(
        both_here.reshape(seq_devices, half_keys, 2 * head_width), "seq", 0, 0, tiled=True
    )
    pairs = [(2 * h + c, 2 * h + 1 - c) for h in range(seq_devices // 2) for c in range(2)]
    other = lax.ppermute(mine, "seq", pairs)
    core = lax.rem(lax.axis_index("seq"), 2)
    both_group = jnp.where(
        core == 0, jnp.stack([mine, other], axis=1), jnp.stack([other, mine], axis=1)
    ).reshape(group_keys, 2 * head_width)
    key_group = both_group[:, None, :head_width]
    value_group = both_group[:, None, head_width:]
    part_accum, stats = forward_item(
        queries[0],
        key_group[:, 0, :],
        value_group[:, 0, :],
        tile_list[0, 0],
        tile_counts[0, 0],
        softmax_scale,
        groups,
    )
    out_rows, out_stats = grp_combine(part_accum, stats, 0)
    attended = out_rows.reshape(1, query_rows, head_width)
    query_grad, kept, given = backward_item(
        queries[0],
        key_group[:, 0, :],
        value_group[:, 0, :],
        grad_output[0],
        attended[0],
        out_stats,
        tile_list[0, 0],
        tile_counts[0, 0],
        softmax_scale,
    )
    summed = (kept.astype(jnp.float32) + lax.ppermute(given, "seq", pairs).astype(jnp.float32)).astype(
        jnp.bfloat16
    )
    both_back = lax.all_to_all(summed, "seq", 0, 0, tiled=True)
    both_back = both_back.reshape(heads_total, QPARTS, half_keys, 2, head_width).transpose(1, 2, 0, 3, 4)
    both_back = both_back.reshape(scene_here, heads_total, 2, head_width)
    grad_keys = both_back[:, :, 0, :].reshape(scene_here, -1)
    grad_values = both_back[:, :, 1, :].reshape(scene_here, -1)
    grad_queries = grp_reduce(
        query_grad.reshape(groups, chunk_rows, head_width), groups, 2
    ).reshape(1, query_rows, head_width)
    return (attended, grad_queries, grad_keys, grad_values)


def solution(mesh):
    in_specs = (
        P("seq", None, None),
        P(("grp", "seq"), None),
        P(("grp", "seq"), None),
        P("seq", None, None),
        P("grp", "seq", None, None),
        P("grp", "seq"),
    )
    out_specs = (
        P("seq", None, None),
        P("seq", None, None),
        P(("grp", "seq"), None),
        P(("grp", "seq"), None),
    )
    return jax.shard_map(
        per_device, mesh=mesh, in_specs=in_specs, out_specs=out_specs, check_vma=False
    )
```

```python
import jax
import jax.numpy as jnp
from jax import lax
from jax.experimental import pallas as pl
from jax.experimental.pallas import tpu as pltpu
from jax.sharding import PartitionSpec as P

QPARTS = 2
QBLK = 512
KBLK = 512


NEG_START = -1e30


LIST_SLOTS = 9


def tile_starts(list_ref, position):
    query_block = jnp.clip(list_ref[position, 0], 0, QPARTS - 1)
    key_block = jnp.clip(list_ref[position, 1], 0, 7)
    return (
        pl.multiple_of(query_block * QBLK, QBLK),
        pl.multiple_of(key_block * KBLK, KBLK),
    )


def forward_kernel(
    softmax_scale, list_ref, count_ref, q_ref, k_ref, v_ref, acc_out, stats_out, max_ref, total_ref, accum_ref
):
    max_ref[...] = jnp.full(max_ref.shape, NEG_START, jnp.float32)
    total_ref[...] = jnp.zeros(total_ref.shape, jnp.float32)
    accum_ref[...] = jnp.zeros(accum_ref.shape, jnp.float32)
    live_tiles = jnp.clip(count_ref[0], 0, LIST_SLOTS)

    def visit(position, carry):
        query_start, key_start = tile_starts(list_ref, position)
        rows = pl.ds(query_start, QBLK)
        keys = pl.ds(key_start, KBLK)
        scores = (
            lax.dot_general(
                q_ref[rows, :], k_ref[keys, :], (((1,), (1,)), ((), ())),
                preferred_element_type=jnp.float32,
            )
            * softmax_scale
        )
        old_max = max_ref[rows, :]
        new_max = jnp.maximum(old_max, jnp.max(scores, axis=1, keepdims=True))
        new_max = new_max.astype(jnp.bfloat16).astype(jnp.float32)
        weights = jnp.exp(scores - new_max[:, :1])
        shrink = jnp.exp(old_max - new_max)
        total_ref[rows, :] = total_ref[rows, :] * shrink + jnp.sum(weights, axis=1, keepdims=True)
        accum_ref[rows, :] = accum_ref[rows, :] * shrink[:, :1] + jnp.dot(
            weights.astype(jnp.bfloat16), v_ref[keys, :], preferred_element_type=jnp.float32
        )
        max_ref[rows, :] = new_max
        return carry

    lax.fori_loop(0, live_tiles, visit, 0)
    groups, chunk_rows = acc_out.shape[0], acc_out.shape[1]
    for g in range(groups):
        rows = pl.ds(g * chunk_rows, chunk_rows)
        acc_out[g] = accum_ref[rows, :].astype(acc_out.dtype)
        stacked = jnp.concatenate([max_ref[rows, :], total_ref[rows, :]], axis=0)
        stats_out[g] = jnp.transpose(stacked)[:8, :]


def forward_item(query_item, key_head, value_head, listing, live_tiles, softmax_scale, groups):
    query_rows, head_width = query_item.shape
    chunk_rows = query_rows // groups
    smem = pl.BlockSpec(memory_space=pltpu.SMEM)
    vmem = pl.BlockSpec(memory_space=pltpu.VMEM)
    rows_f32 = pltpu.VMEM((query_rows, head_width), jnp.float32)
    return pl.pallas_call(
        lambda *refs: forward_kernel(softmax_scale, *refs),
        out_shape=(
            jax.ShapeDtypeStruct((groups, chunk_rows, head_width), jnp.bfloat16),
            jax.ShapeDtypeStruct((groups, 8, 2 * chunk_rows), jnp.float32),
        ),
        in_specs=[smem, smem, vmem, vmem, vmem],
        out_specs=(vmem, vmem),
        scratch_shapes=[rows_f32, rows_f32, rows_f32],
    )(listing, live_tiles.reshape(1), query_item, key_head, value_head)


def backward_kernel(
    softmax_scale, list_ref, count_ref, q_ref, k_ref, v_ref, do_ref, att_ref, stats_ref,
    dq_ref, dk_ref, dv_ref, dq_acc, dk_acc, dv_acc, log_ref, delta_ref,
):
    groups = stats_ref.shape[0]
    chunk_rows = stats_ref.shape[2] // 2
    for g in range(groups):
        rows = pl.ds(g * chunk_rows, chunk_rows)
        columns = jnp.transpose(jnp.broadcast_to(stats_ref[g][0:1, :], (2 * chunk_rows, 2 * chunk_rows)))
        log_ref[rows, :] = columns[:chunk_rows, 0:1] + jnp.log(columns[chunk_rows:, 0:1])
        delta_ref[rows, :] = jnp.sum(
            att_ref[rows, :].astype(jnp.float32) * do_ref[rows, :].astype(jnp.float32),
            axis=1,
            keepdims=True,
        )
    dq_acc[...] = jnp.zeros(dq_acc.shape, jnp.float32)
    dk_acc[...] = jnp.zeros(dk_acc.shape, jnp.float32)
    dv_acc[...] = jnp.zeros(dv_acc.shape, jnp.float32)
    live_tiles = jnp.clip(count_ref[0], 0, LIST_SLOTS)

    def visit(position, carry):
        query_start, key_start = tile_starts(list_ref, position)
        rows = pl.ds(query_start, QBLK)
        keys = pl.ds(key_start, KBLK)
        query_block = q_ref[rows, :]
        grad_block = do_ref[rows, :]
        key_block = k_ref[keys, :]
        value_block = v_ref[keys, :]
        scores = (
            lax.dot_general(
                query_block, key_block, (((1,), (1,)), ((), ())),
                preferred_element_type=jnp.float32,
            )
            * softmax_scale
        )
        probs = jnp.exp(scores - log_ref[rows, :])
        probs_half = probs.astype(jnp.bfloat16)
        dv_acc[keys, :] += lax.dot_general(
            probs_half, grad_block, (((0,), (0,)), ((), ())), preferred_element_type=jnp.float32
        )
        prob_grad = lax.dot_general(
            grad_block, value_block, (((1,), (1,)), ((), ())), preferred_element_type=jnp.float32
        )
        score_grad = (probs * (prob_grad - delta_ref[rows, :])).astype(jnp.bfloat16)
        dq_acc[rows, :] += (
            jnp.dot(score_grad, key_block, preferred_element_type=jnp.float32) * softmax_scale
        )
        dk_acc[keys, :] += (
            lax.dot_general(
                score_grad, query_block, (((0,), (0,)), ((), ())),
                preferred_element_type=jnp.float32,
            )
            * softmax_scale
        )
        return carry

    lax.fori_loop(0, live_tiles, visit, 0)
    dq_ref[...] = dq_acc[...].astype(dq_ref.dtype)
    dk_ref[...] = dk_acc[...].astype(dk_ref.dtype)
    dv_ref[...] = dv_acc[...].astype(dv_ref.dtype)


def backward_item(
    query_item, key_head, value_head, grad_item, attended, stats, listing, live_tiles, softmax_scale,
):
    query_rows, head_width = query_item.shape
    key_rows = key_head.shape[0]
    smem = pl.BlockSpec(memory_space=pltpu.SMEM)
    vmem = pl.BlockSpec(memory_space=pltpu.VMEM)
    return pl.pallas_call(
        lambda *refs: backward_kernel(softmax_scale, *refs),
        out_shape=(
            jax.ShapeDtypeStruct((query_rows, head_width), jnp.bfloat16),
            jax.ShapeDtypeStruct((key_rows, head_width), jnp.bfloat16),
            jax.ShapeDtypeStruct((key_rows, head_width), jnp.bfloat16),
        ),
        in_specs=[smem, smem] + [vmem] * 6,
        out_specs=(vmem, vmem, vmem),
        scratch_shapes=[
            pltpu.VMEM((query_rows, head_width), jnp.float32),
            pltpu.VMEM((key_rows, head_width), jnp.float32),
            pltpu.VMEM((key_rows, head_width), jnp.float32),
            pltpu.VMEM((query_rows, 1), jnp.float32),
            pltpu.VMEM((query_rows, 1), jnp.float32),
        ],
    )(
        listing,
        live_tiles.reshape(1),
        query_item,
        key_head,
        value_head,
        grad_item,
        attended,
        stats,
    )


def exchange_kernel(broadcast, x_ref, y_ref, send_sem, recv_sem):
    groups = y_ref.shape[0]
    me = lax.axis_index("grp")
    lane = lax.axis_index("seq")
    mesh_ids = pl.DeviceIdType.MESH
    barrier = pltpu.get_barrier_semaphore()
    for step in range(1, groups):
        pl.semaphore_signal(
            barrier, inc=1, device_id=(lax.rem(me + step, groups), lane), device_id_type=mesh_ids
        )
    pl.semaphore_wait(barrier, groups - 1)
    copies = []
    for step in range(1, groups):
        target = lax.rem(me + step, groups)
        copy = pltpu.make_async_remote_copy(
            src_ref=x_ref if broadcast else x_ref.at[target],
            dst_ref=y_ref.at[me],
            send_sem=send_sem.at[step],
            recv_sem=recv_sem.at[step],
            device_id=(target, lane),
            device_id_type=mesh_ids,
        )
        copy.start()
        copies.append(copy)
    y_ref[me] = x_ref[...] if broadcast else x_ref[me]
    for copy in copies:
        copy.wait()


def grp_exchange(x, groups, broadcast, collective):
    out_shape = (groups,) + (x.shape if broadcast else x.shape[1:])
    vmem = pl.BlockSpec(memory_space=pltpu.VMEM)
    return pl.pallas_call(
        lambda *refs: exchange_kernel(broadcast, *refs),
        out_shape=jax.ShapeDtypeStruct(out_shape, x.dtype),
        in_specs=[vmem],
        out_specs=vmem,
        scratch_shapes=[pltpu.SemaphoreType.DMA((groups,)), pltpu.SemaphoreType.DMA((groups,))],
        compiler_params=pltpu.CompilerParams(collective_id=collective, has_side_effects=True),
    )(x)


def reduce_kernel(x_ref, y_ref, part_ref, send_sem, recv_sem, back_send, back_recv):
    groups = y_ref.shape[0]
    me = lax.axis_index("grp")
    lane = lax.axis_index("seq")
    mesh_ids = pl.DeviceIdType.MESH
    barrier = pltpu.get_barrier_semaphore()
    for step in range(1, groups):
        pl.semaphore_signal(
            barrier, inc=1, device_id=(lax.rem(me + step, groups), lane), device_id_type=mesh_ids
        )
    pl.semaphore_wait(barrier, groups - 1)
    copies = []
    for step in range(1, groups):
        target = lax.rem(me + step, groups)
        copy = pltpu.make_async_remote_copy(
            src_ref=x_ref.at[target],
            dst_ref=part_ref.at[me],
            send_sem=send_sem.at[step],
            recv_sem=recv_sem.at[step],
            device_id=(target, lane),
            device_id_type=mesh_ids,
        )
        copy.start()
        copies.append(copy)
    part_ref[me] = x_ref[me]
    for copy in copies:
        copy.wait()
    y_ref[me] = jnp.sum(part_ref[...].astype(jnp.float32), axis=0).astype(y_ref.dtype)
    copies = []
    for step in range(1, groups):
        target = lax.rem(me + step, groups)
        copy = pltpu.make_async_remote_copy(
            src_ref=y_ref.at[me],
            dst_ref=y_ref.at[me],
            send_sem=back_send.at[step],
            recv_sem=back_recv.at[step],
            device_id=(target, lane),
            device_id_type=mesh_ids,
        )
        copy.start()
        copies.append(copy)
    for copy in copies:
        copy.wait()


def grp_reduce(x, groups, collective):
    vmem = pl.BlockSpec(memory_space=pltpu.VMEM)
    sems = pltpu.SemaphoreType.DMA((groups,))
    return pl.pallas_call(
        reduce_kernel,
        out_shape=jax.ShapeDtypeStruct(x.shape, x.dtype),
        in_specs=[vmem],
        out_specs=vmem,
        scratch_shapes=[pltpu.VMEM(x.shape, x.dtype), sems, sems, sems, sems],
        compiler_params=pltpu.CompilerParams(collective_id=collective, has_side_effects=True),
    )(x)


def combine_kernel(
    acc_in, stats_in, out_ref, stats_out, acc_part, stats_part,
    send_acc, recv_acc, send_stats, recv_stats, back_send, back_recv, stat_send, stat_recv,
):
    groups, chunk_rows, head_width = out_ref.shape
    me = lax.axis_index("grp")
    lane = lax.axis_index("seq")
    mesh_ids = pl.DeviceIdType.MESH
    barrier = pltpu.get_barrier_semaphore()
    for step in range(1, groups):
        pl.semaphore_signal(
            barrier, inc=1, device_id=(lax.rem(me + step, groups), lane), device_id_type=mesh_ids
        )
    pl.semaphore_wait(barrier, groups - 1)
    copies = []
    for step in range(1, groups):
        target = lax.rem(me + step, groups)
        for source, landing, sent, got in (
            (acc_in, acc_part, send_acc, recv_acc),
            (stats_in, stats_part, send_stats, recv_stats),
        ):
            copy = pltpu.make_async_remote_copy(
                src_ref=source.at[target],
                dst_ref=landing.at[me],
                send_sem=sent.at[step],
                recv_sem=got.at[step],
                device_id=(target, lane),
                device_id_type=mesh_ids,
            )
            copy.start()
            copies.append(copy)
    acc_part[me] = acc_in[me]
    stats_part[me] = stats_in[me]
    for copy in copies:
        copy.wait()
    columns = jnp.transpose(stats_part[...].reshape(groups * 8, 128))
    maxima = [columns[:chunk_rows, 8 * g : 8 * g + 1] for g in range(groups)]
    totals = [columns[chunk_rows:, 8 * g : 8 * g + 1] for g in range(groups)]
    top = maxima[0]
    for g in range(1, groups):
        top = jnp.maximum(top, maxima[g])
    row_total = jnp.zeros_like(top)
    row_accum = jnp.zeros((chunk_rows, head_width), jnp.float32)
    for g in range(groups):
        shrink = jnp.exp(maxima[g] - top)
        row_total = row_total + totals[g] * shrink
        row_accum = row_accum + acc_part[g].astype(jnp.float32) * shrink
    out_ref[me] = (row_accum / row_total).astype(out_ref.dtype)
    spread = jnp.concatenate(
        [jnp.broadcast_to(top, (chunk_rows, 128)), jnp.broadcast_to(row_total, (chunk_rows, 128))], axis=0
    )
    stats_out[me] = jnp.transpose(spread)[:8, :]
    copies = []
    for step in range(1, groups):
        target = lax.rem(me + step, groups)
        for source, sent, got in ((out_ref, back_send, back_recv), (stats_out, stat_send, stat_recv)):
            copy = pltpu.make_async_remote_copy(
                src_ref=source.at[me],
                dst_ref=source.at[me],
                send_sem=sent.at[step],
                recv_sem=got.at[step],
                device_id=(target, lane),
                device_id_type=mesh_ids,
            )
            copy.start()
            copies.append(copy)
    for copy in copies:
        copy.wait()


def grp_combine(accum, stats, collective):
    groups = accum.shape[0]
    vmem = pl.BlockSpec(memory_space=pltpu.VMEM)
    sems = pltpu.SemaphoreType.DMA((groups,))
    return pl.pallas_call(
        combine_kernel,
        out_shape=(
            jax.ShapeDtypeStruct(accum.shape, accum.dtype),
            jax.ShapeDtypeStruct(stats.shape, stats.dtype),
        ),
        in_specs=[vmem, vmem],
        out_specs=(vmem, vmem),
        scratch_shapes=[pltpu.VMEM(accum.shape, accum.dtype), pltpu.VMEM(stats.shape, stats.dtype)]
        + [sems] * 8,
        compiler_params=pltpu.CompilerParams(collective_id=collective, has_side_effects=True),
    )(accum, stats)


def gather_kernel(k_ref, v_ref, k_out, v_out, send_sem, recv_sem, pair_send, pair_recv):
    halves, sources, half, head_width = k_out.shape
    me = lax.axis_index("seq")
    grp_here = lax.axis_index("grp")
    mine = lax.rem(me, 2)
    partner = me + 1 - 2 * mine
    head = me // 2
    mesh_ids = pl.DeviceIdType.MESH
    barrier = pltpu.get_barrier_semaphore()
    for step in range(1, sources):
        pl.semaphore_signal(
            barrier, inc=1, device_id=(grp_here, lax.rem(me + step, sources)), device_id_type=mesh_ids
        )
    pl.semaphore_wait(barrier, sources - 1)
    copies = []
    for step in range(1, sources):
        target = lax.rem(me + step, sources)
        rows = pl.ds(pl.multiple_of(lax.rem(target, 2) * half, half), half)
        cols = pl.ds(pl.multiple_of((target // 2) * head_width, head_width), head_width)
        for index, (source, landing) in enumerate(((k_ref, k_out), (v_ref, v_out))):
            copy = pltpu.make_async_remote_copy(
                src_ref=source.at[rows, cols],
                dst_ref=landing.at[lax.rem(target, 2), me],
                send_sem=send_sem.at[index, step],
                recv_sem=recv_sem.at[index, step],
                device_id=(grp_here, target),
                device_id_type=mesh_ids,
            )
            copy.start()
            copies.append(copy)
    own_rows = pl.ds(pl.multiple_of(mine * half, half), half)
    own_cols = pl.ds(pl.multiple_of(head * head_width, head_width), head_width)
    k_out[mine, me] = k_ref[own_rows, own_cols]
    v_out[mine, me] = v_ref[own_rows, own_cols]
    for copy in copies:
        copy.wait()
    copies = []
    for index, landing in enumerate((k_out, v_out)):
        copy = pltpu.make_async_remote_copy(
            src_ref=landing.at[mine],
            dst_ref=landing.at[mine],
            send_sem=pair_send.at[index],
            recv_sem=pair_recv.at[index],
            device_id=(grp_here, partner),
            device_id_type=mesh_ids,
        )
        copy.start()
        copies.append(copy)
    for copy in copies:
        copy.wait()


def seq_gather(scene_keys, scene_values, sources, head_width, collective):
    half = scene_keys.shape[0] // QPARTS
    vmem = pl.BlockSpec(memory_space=pltpu.VMEM)
    out = jax.ShapeDtypeStruct((QPARTS, sources, half, head_width), scene_keys.dtype)
    return pl.pallas_call(
        gather_kernel,
        out_shape=(out, out),
        in_specs=[vmem, vmem],
        out_specs=(vmem, vmem),
        scratch_shapes=[
            pltpu.SemaphoreType.DMA((2, sources)),
            pltpu.SemaphoreType.DMA((2, sources)),
            pltpu.SemaphoreType.DMA((2,)),
            pltpu.SemaphoreType.DMA((2,)),
        ],
        compiler_params=pltpu.CompilerParams(collective_id=collective, has_side_effects=True),
    )(scene_keys, scene_values)


def scatter_rows(rows, parts, collective):
    return grp_exchange(
        rows.reshape(parts, rows.shape[0] // parts, rows.shape[1]), parts, False, collective
    )


def broadcast_rows(chunk, parts, collective):
    gathered = grp_exchange(chunk, parts, True, collective)
    return gathered.reshape(parts * chunk.shape[0], chunk.shape[1])


def per_device(queries, scene_keys, scene_values, grad_output, tile_list, tile_counts):
    items_here = queries.shape[0]
    head_width = queries.shape[2]
    query_rows = queries.shape[1]
    scene_here = scene_keys.shape[0]
    heads_total = scene_keys.shape[1] // head_width
    seq_devices = lax.axis_size("seq")
    groups = lax.axis_size("grp")
    chunk_rows = query_rows // groups
    group_keys = scene_here * seq_devices
    copies = max(1, QPARTS // items_here)
    heads_here = max(1, items_here // QPARTS)
    softmax_scale = head_width ** (-0.5)
    half_keys = scene_here // QPARTS
    key_halves, value_halves = seq_gather(scene_keys, scene_values, seq_devices, head_width, 4)
    key_group = key_halves.transpose(1, 0, 2, 3).reshape(group_keys, 1, head_width)
    value_group = value_halves.transpose(1, 0, 2, 3).reshape(group_keys, 1, head_width)
    pairs = [(2 * h + c, 2 * h + 1 - c) for h in range(seq_devices // 2) for c in range(2)]
    core = lax.rem(lax.axis_index("seq"), 2)
    part_accum, stats = forward_item(
        queries[0],
        key_group[:, 0, :],
        value_group[:, 0, :],
        tile_list[0, 0],
        tile_counts[0, 0],
        softmax_scale,
        groups,
    )
    out_rows, out_stats = grp_combine(part_accum, stats, 0)
    attended = out_rows.reshape(1, query_rows, head_width)
    query_grad, key_grad, value_grad = backward_item(
        queries[0],
        key_group[:, 0, :],
        value_group[:, 0, :],
        grad_output[0],
        attended[0],
        out_stats,
        tile_list[0, 0],
        tile_counts[0, 0],
        softmax_scale,
    )
    both_parts = jnp.concatenate([key_grad, value_grad], axis=1).reshape(
        seq_devices, QPARTS, half_keys, 2 * head_width
    )
    kept = lax.dynamic_index_in_dim(both_parts, core, axis=1, keepdims=False)
    given = lax.dynamic_index_in_dim(both_parts, 1 - core, axis=1, keepdims=False)
    summed = (kept.astype(jnp.float32) + lax.ppermute(given, "seq", pairs).astype(jnp.float32)).astype(
        jnp.bfloat16
    )
    both_back = lax.all_to_all(summed, "seq", 0, 0, tiled=True)
    both_back = both_back.reshape(heads_total, QPARTS, half_keys, 2, head_width).transpose(1, 2, 0, 3, 4)
    both_back = both_back.reshape(scene_here, heads_total, 2, head_width)
    grad_keys = both_back[:, :, 0, :].reshape(scene_here, -1)
    grad_values = both_back[:, :, 1, :].reshape(scene_here, -1)
    grad_queries = grp_reduce(
        query_grad.reshape(groups, chunk_rows, head_width), groups, 2
    ).reshape(1, query_rows, head_width)
    return (attended, grad_queries, grad_keys, grad_values)


def solution(mesh):
    in_specs = (
        P("seq", None, None),
        P(("grp", "seq"), None),
        P(("grp", "seq"), None),
        P("seq", None, None),
        P("grp", "seq", None, None),
        P("grp", "seq"),
    )
    out_specs = (
        P("seq", None, None),
        P("seq", None, None),
        P(("grp", "seq"), None),
        P(("grp", "seq"), None),
    )
    return jax.shard_map(
        per_device, mesh=mesh, in_specs=in_specs, out_specs=out_specs, check_vma=False
    )
```

```python
import jax
import jax.numpy as jnp
from jax import lax
from jax.experimental import pallas as pl
from jax.experimental.pallas import tpu as pltpu
from jax.sharding import PartitionSpec as P

QPARTS = 2
QBLK = 512
KBLK = 512


NEG_START = -1e30


LIST_SLOTS = 9


def tile_starts(list_ref, position):
    query_block = jnp.clip(list_ref[position, 0], 0, QPARTS - 1)
    key_block = jnp.clip(list_ref[position, 1], 0, 7)
    return (
        pl.multiple_of(query_block * QBLK, QBLK),
        pl.multiple_of(key_block * KBLK, KBLK),
    )


def forward_kernel(
    softmax_scale, list_ref, count_ref, q_ref, k_ref, v_ref, acc_out, stats_out, max_ref, total_ref, accum_ref
):
    max_ref[...] = jnp.full(max_ref.shape, NEG_START, jnp.float32)
    total_ref[...] = jnp.zeros(total_ref.shape, jnp.float32)
    accum_ref[...] = jnp.zeros(accum_ref.shape, jnp.float32)
    live_tiles = jnp.clip(count_ref[0], 0, LIST_SLOTS)

    def visit(position, carry):
        query_start, key_start = tile_starts(list_ref, position)
        rows = pl.ds(query_start, QBLK)
        keys = pl.ds(key_start, KBLK)
        scores = (
            lax.dot_general(
                q_ref[rows, :], k_ref[keys, :], (((1,), (1,)), ((), ())),
                preferred_element_type=jnp.float32,
            )
            * softmax_scale
        )
        old_max = max_ref[rows, :]
        new_max = jnp.maximum(old_max, jnp.max(scores, axis=1, keepdims=True))
        new_max = new_max.astype(jnp.bfloat16).astype(jnp.float32)
        weights = jnp.exp(scores - new_max[:, :1])
        shrink = jnp.exp(old_max - new_max)
        total_ref[rows, :] = total_ref[rows, :] * shrink + jnp.sum(weights, axis=1, keepdims=True)
        accum_ref[rows, :] = accum_ref[rows, :] * shrink[:, :1] + jnp.dot(
            weights.astype(jnp.bfloat16), v_ref[keys, :], preferred_element_type=jnp.float32
        )
        max_ref[rows, :] = new_max
        return carry

    lax.fori_loop(0, live_tiles, visit, 0)
    groups, chunk_rows = acc_out.shape[0], acc_out.shape[1]
    for g in range(groups):
        rows = pl.ds(g * chunk_rows, chunk_rows)
        acc_out[g] = accum_ref[rows, :].astype(acc_out.dtype)
        stacked = jnp.concatenate([max_ref[rows, :], total_ref[rows, :]], axis=0)
        stats_out[g] = jnp.transpose(stacked)[:8, :]


def forward_item(query_item, key_head, value_head, listing, live_tiles, softmax_scale, groups):
    query_rows, head_width = query_item.shape
    chunk_rows = query_rows // groups
    smem = pl.BlockSpec(memory_space=pltpu.SMEM)
    vmem = pl.BlockSpec(memory_space=pltpu.VMEM)
    rows_f32 = pltpu.VMEM((query_rows, head_width), jnp.float32)
    return pl.pallas_call(
        lambda *refs: forward_kernel(softmax_scale, *refs),
        out_shape=(
            jax.ShapeDtypeStruct((groups, chunk_rows, head_width), jnp.bfloat16),
            jax.ShapeDtypeStruct((groups, 8, 2 * chunk_rows), jnp.float32),
        ),
        in_specs=[smem, smem, vmem, vmem, vmem],
        out_specs=(vmem, vmem),
        scratch_shapes=[rows_f32, rows_f32, rows_f32],
    )(listing, live_tiles.reshape(1), query_item, key_head, value_head)


def backward_kernel(
    softmax_scale, list_ref, count_ref, q_ref, k_ref, v_ref, do_ref, att_ref, stats_ref,
    dq_ref, dk_ref, dv_ref, dq_acc, dk_acc, dv_acc, log_ref, delta_ref,
):
    groups = stats_ref.shape[0]
    chunk_rows = stats_ref.shape[2] // 2
    for g in range(groups):
        rows = pl.ds(g * chunk_rows, chunk_rows)
        columns = jnp.transpose(jnp.broadcast_to(stats_ref[g][0:1, :], (2 * chunk_rows, 2 * chunk_rows)))
        log_ref[rows, :] = columns[:chunk_rows, 0:1] + jnp.log(columns[chunk_rows:, 0:1])
        delta_ref[rows, :] = jnp.sum(
            att_ref[rows, :].astype(jnp.float32) * do_ref[rows, :].astype(jnp.float32),
            axis=1,
            keepdims=True,
        )
    dq_acc[...] = jnp.zeros(dq_acc.shape, jnp.float32)
    dk_acc[...] = jnp.zeros(dk_acc.shape, jnp.float32)
    dv_acc[...] = jnp.zeros(dv_acc.shape, jnp.float32)
    live_tiles = jnp.clip(count_ref[0], 0, LIST_SLOTS)

    def visit(position, carry):
        query_start, key_start = tile_starts(list_ref, position)
        rows = pl.ds(query_start, QBLK)
        keys = pl.ds(key_start, KBLK)
        query_block = q_ref[rows, :]
        grad_block = do_ref[rows, :]
        key_block = k_ref[keys, :]
        value_block = v_ref[keys, :]
        scores = (
            lax.dot_general(
                query_block, key_block, (((1,), (1,)), ((), ())),
                preferred_element_type=jnp.float32,
            )
            * softmax_scale
        )
        probs = jnp.exp(scores - log_ref[rows, :])
        probs_half = probs.astype(jnp.bfloat16)
        dv_acc[keys, :] += lax.dot_general(
            probs_half, grad_block, (((0,), (0,)), ((), ())), preferred_element_type=jnp.float32
        )
        prob_grad = lax.dot_general(
            grad_block, value_block, (((1,), (1,)), ((), ())), preferred_element_type=jnp.float32
        )
        score_grad = (probs * (prob_grad - delta_ref[rows, :])).astype(jnp.bfloat16)
        dq_acc[rows, :] += (
            jnp.dot(score_grad, key_block, preferred_element_type=jnp.float32) * softmax_scale
        )
        dk_acc[keys, :] += (
            lax.dot_general(
                score_grad, query_block, (((0,), (0,)), ((), ())),
                preferred_element_type=jnp.float32,
            )
            * softmax_scale
        )
        return carry

    lax.fori_loop(0, live_tiles, visit, 0)
    dq_ref[...] = dq_acc[...].astype(dq_ref.dtype)
    dk_ref[...] = dk_acc[...].astype(dk_ref.dtype)
    dv_ref[...] = dv_acc[...].astype(dv_ref.dtype)


def backward_item(
    query_item, key_head, value_head, grad_item, attended, stats, listing, live_tiles, softmax_scale,
):
    query_rows, head_width = query_item.shape
    key_rows = key_head.shape[0]
    smem = pl.BlockSpec(memory_space=pltpu.SMEM)
    vmem = pl.BlockSpec(memory_space=pltpu.VMEM)
    return pl.pallas_call(
        lambda *refs: backward_kernel(softmax_scale, *refs),
        out_shape=(
            jax.ShapeDtypeStruct((query_rows, head_width), jnp.bfloat16),
            jax.ShapeDtypeStruct((key_rows, head_width), jnp.bfloat16),
            jax.ShapeDtypeStruct((key_rows, head_width), jnp.bfloat16),
        ),
        in_specs=[smem, smem] + [vmem] * 6,
        out_specs=(vmem, vmem, vmem),
        scratch_shapes=[
            pltpu.VMEM((query_rows, head_width), jnp.float32),
            pltpu.VMEM((key_rows, head_width), jnp.float32),
            pltpu.VMEM((key_rows, head_width), jnp.float32),
            pltpu.VMEM((query_rows, 1), jnp.float32),
            pltpu.VMEM((query_rows, 1), jnp.float32),
        ],
    )(
        listing,
        live_tiles.reshape(1),
        query_item,
        key_head,
        value_head,
        grad_item,
        attended,
        stats,
    )


def exchange_kernel(broadcast, x_ref, y_ref, send_sem, recv_sem):
    groups = y_ref.shape[0]
    me = lax.axis_index("grp")
    lane = lax.axis_index("seq")
    mesh_ids = pl.DeviceIdType.MESH
    barrier = pltpu.get_barrier_semaphore()
    for step in range(1, groups):
        pl.semaphore_signal(
            barrier, inc=1, device_id=(lax.rem(me + step, groups), lane), device_id_type=mesh_ids
        )
    pl.semaphore_wait(barrier, groups - 1)
    copies = []
    for step in range(1, groups):
        target = lax.rem(me + step, groups)
        copy = pltpu.make_async_remote_copy(
            src_ref=x_ref if broadcast else x_ref.at[target],
            dst_ref=y_ref.at[me],
            send_sem=send_sem.at[step],
            recv_sem=recv_sem.at[step],
            device_id=(target, lane),
            device_id_type=mesh_ids,
        )
        copy.start()
        copies.append(copy)
    y_ref[me] = x_ref[...] if broadcast else x_ref[me]
    for copy in copies:
        copy.wait()


def grp_exchange(x, groups, broadcast, collective):
    out_shape = (groups,) + (x.shape if broadcast else x.shape[1:])
    vmem = pl.BlockSpec(memory_space=pltpu.VMEM)
    return pl.pallas_call(
        lambda *refs: exchange_kernel(broadcast, *refs),
        out_shape=jax.ShapeDtypeStruct(out_shape, x.dtype),
        in_specs=[vmem],
        out_specs=vmem,
        scratch_shapes=[pltpu.SemaphoreType.DMA((groups,)), pltpu.SemaphoreType.DMA((groups,))],
        compiler_params=pltpu.CompilerParams(collective_id=collective, has_side_effects=True),
    )(x)


def reduce_kernel(x_ref, y_ref, part_ref, send_sem, recv_sem, back_send, back_recv):
    groups = y_ref.shape[0]
    me = lax.axis_index("grp")
    lane = lax.axis_index("seq")
    mesh_ids = pl.DeviceIdType.MESH
    barrier = pltpu.get_barrier_semaphore()
    for step in range(1, groups):
        pl.semaphore_signal(
            barrier, inc=1, device_id=(lax.rem(me + step, groups), lane), device_id_type=mesh_ids
        )
    pl.semaphore_wait(barrier, groups - 1)
    copies = []
    for step in range(1, groups):
        target = lax.rem(me + step, groups)
        copy = pltpu.make_async_remote_copy(
            src_ref=x_ref.at[target],
            dst_ref=part_ref.at[me],
            send_sem=send_sem.at[step],
            recv_sem=recv_sem.at[step],
            device_id=(target, lane),
            device_id_type=mesh_ids,
        )
        copy.start()
        copies.append(copy)
    part_ref[me] = x_ref[me]
    for copy in copies:
        copy.wait()
    y_ref[me] = jnp.sum(part_ref[...].astype(jnp.float32), axis=0).astype(y_ref.dtype)
    copies = []
    for step in range(1, groups):
        target = lax.rem(me + step, groups)
        copy = pltpu.make_async_remote_copy(
            src_ref=y_ref.at[me],
            dst_ref=y_ref.at[me],
            send_sem=back_send.at[step],
            recv_sem=back_recv.at[step],
            device_id=(target, lane),
            device_id_type=mesh_ids,
        )
        copy.start()
        copies.append(copy)
    for copy in copies:
        copy.wait()


def grp_reduce(x, groups, collective):
    vmem = pl.BlockSpec(memory_space=pltpu.VMEM)
    sems = pltpu.SemaphoreType.DMA((groups,))
    return pl.pallas_call(
        reduce_kernel,
        out_shape=jax.ShapeDtypeStruct(x.shape, x.dtype),
        in_specs=[vmem],
        out_specs=vmem,
        scratch_shapes=[pltpu.VMEM(x.shape, x.dtype), sems, sems, sems, sems],
        compiler_params=pltpu.CompilerParams(collective_id=collective, has_side_effects=True),
    )(x)


def combine_kernel(
    acc_in, stats_in, out_ref, stats_out, acc_part, stats_part,
    send_acc, recv_acc, send_stats, recv_stats, back_send, back_recv, stat_send, stat_recv,
):
    groups, chunk_rows, head_width = out_ref.shape
    me = lax.axis_index("grp")
    lane = lax.axis_index("seq")
    mesh_ids = pl.DeviceIdType.MESH
    barrier = pltpu.get_barrier_semaphore()
    for step in range(1, groups):
        pl.semaphore_signal(
            barrier, inc=1, device_id=(lax.rem(me + step, groups), lane), device_id_type=mesh_ids
        )
    pl.semaphore_wait(barrier, groups - 1)
    copies = []
    for step in range(1, groups):
        target = lax.rem(me + step, groups)
        for source, landing, sent, got in (
            (acc_in, acc_part, send_acc, recv_acc),
            (stats_in, stats_part, send_stats, recv_stats),
        ):
            copy = pltpu.make_async_remote_copy(
                src_ref=source.at[target],
                dst_ref=landing.at[me],
                send_sem=sent.at[step],
                recv_sem=got.at[step],
                device_id=(target, lane),
                device_id_type=mesh_ids,
            )
            copy.start()
            copies.append(copy)
    acc_part[me] = acc_in[me]
    stats_part[me] = stats_in[me]
    for copy in copies:
        copy.wait()
    columns = jnp.transpose(stats_part[...].reshape(groups * 8, 128))
    maxima = [columns[:chunk_rows, 8 * g : 8 * g + 1] for g in range(groups)]
    totals = [columns[chunk_rows:, 8 * g : 8 * g + 1] for g in range(groups)]
    top = maxima[0]
    for g in range(1, groups):
        top = jnp.maximum(top, maxima[g])
    row_total = jnp.zeros_like(top)
    row_accum = jnp.zeros((chunk_rows, head_width), jnp.float32)
    for g in range(groups):
        shrink = jnp.exp(maxima[g] - top)
        row_total = row_total + totals[g] * shrink
        row_accum = row_accum + acc_part[g].astype(jnp.float32) * shrink
    out_ref[me] = (row_accum / row_total).astype(out_ref.dtype)
    spread = jnp.concatenate(
        [jnp.broadcast_to(top, (chunk_rows, 128)), jnp.broadcast_to(row_total, (chunk_rows, 128))], axis=0
    )
    stats_out[me] = jnp.transpose(spread)[:8, :]
    copies = []
    for step in range(1, groups):
        target = lax.rem(me + step, groups)
        for source, sent, got in ((out_ref, back_send, back_recv), (stats_out, stat_send, stat_recv)):
            copy = pltpu.make_async_remote_copy(
                src_ref=source.at[me],
                dst_ref=source.at[me],
                send_sem=sent.at[step],
                recv_sem=got.at[step],
                device_id=(target, lane),
                device_id_type=mesh_ids,
            )
            copy.start()
            copies.append(copy)
    for copy in copies:
        copy.wait()


def grp_combine(accum, stats, collective):
    groups = accum.shape[0]
    vmem = pl.BlockSpec(memory_space=pltpu.VMEM)
    sems = pltpu.SemaphoreType.DMA((groups,))
    return pl.pallas_call(
        combine_kernel,
        out_shape=(
            jax.ShapeDtypeStruct(accum.shape, accum.dtype),
            jax.ShapeDtypeStruct(stats.shape, stats.dtype),
        ),
        in_specs=[vmem, vmem],
        out_specs=(vmem, vmem),
        scratch_shapes=[pltpu.VMEM(accum.shape, accum.dtype), pltpu.VMEM(stats.shape, stats.dtype)]
        + [sems] * 8,
        compiler_params=pltpu.CompilerParams(collective_id=collective, has_side_effects=True),
    )(accum, stats)


def back_kernel(
    dq_in, dk_in, dv_in, dq_out, gk_out, gv_out, part_ref, recv_k, recv_v,
    send_sem, recv_sem, back_send, back_recv, kv_send, kv_recv,
):
    groups = dq_out.shape[0]
    sources, block, head_width = recv_k.shape
    me = lax.axis_index("grp")
    lane = lax.axis_index("seq")
    mesh_ids = pl.DeviceIdType.MESH
    barrier = pltpu.get_barrier_semaphore()
    for step in range(1, groups):
        pl.semaphore_signal(
            barrier, inc=1, device_id=(lax.rem(me + step, groups), lane), device_id_type=mesh_ids
        )
    for step in range(1, sources):
        pl.semaphore_signal(
            barrier, inc=1, device_id=(me, lax.rem(lane + step, sources)), device_id_type=mesh_ids
        )
    pl.semaphore_wait(barrier, groups - 1 + sources - 1)
    returns = []
    for step in range(1, sources):
        target = lax.rem(lane + step, sources)
        rows = pl.ds(pl.multiple_of(target * block, block), block)
        for index, (source, landing) in enumerate(((dk_in, recv_k), (dv_in, recv_v))):
            copy = pltpu.make_async_remote_copy(
                src_ref=source.at[rows],
                dst_ref=landing.at[lane],
                send_sem=kv_send.at[index, step],
                recv_sem=kv_recv.at[index, step],
                device_id=(me, target),
                device_id_type=mesh_ids,
            )
            copy.start()
            returns.append(copy)
    copies = []
    for step in range(1, groups):
        target = lax.rem(me + step, groups)
        copy = pltpu.make_async_remote_copy(
            src_ref=dq_in.at[target],
            dst_ref=part_ref.at[me],
            send_sem=send_sem.at[step],
            recv_sem=recv_sem.at[step],
            device_id=(target, lane),
            device_id_type=mesh_ids,
        )
        copy.start()
        copies.append(copy)
    own_rows = pl.ds(pl.multiple_of(lane * block, block), block)
    recv_k[lane] = dk_in[own_rows, :]
    recv_v[lane] = dv_in[own_rows, :]
    part_ref[me] = dq_in[me]
    for copy in copies:
        copy.wait()
    dq_out[me] = jnp.sum(part_ref[...].astype(jnp.float32), axis=0).astype(dq_out.dtype)
    copies = []
    for step in range(1, groups):
        target = lax.rem(me + step, groups)
        copy = pltpu.make_async_remote_copy(
            src_ref=dq_out.at[me],
            dst_ref=dq_out.at[me],
            send_sem=back_send.at[step],
            recv_sem=back_recv.at[step],
            device_id=(target, lane),
            device_id_type=mesh_ids,
        )
        copy.start()
        copies.append(copy)
    for copy in returns:
        copy.wait()
    for head in range(sources // 2):
        cols = pl.ds(head * head_width, head_width)
        for landing, out_ref in ((recv_k, gk_out), (recv_v, gv_out)):
            out_ref[:, cols] = (
                landing[2 * head].astype(jnp.float32) + landing[2 * head + 1].astype(jnp.float32)
            ).astype(out_ref.dtype)
    for copy in copies:
        copy.wait()


def back_exchange(query_grad, key_grad, value_grad, groups, sources, collective):
    head_width = query_grad.shape[-1]
    block = key_grad.shape[0] // sources
    vmem = pl.BlockSpec(memory_space=pltpu.VMEM)
    grad_shape = jax.ShapeDtypeStruct((block, sources // 2 * head_width), key_grad.dtype)
    sems = pltpu.SemaphoreType.DMA((groups,))
    return pl.pallas_call(
        back_kernel,
        out_shape=(jax.ShapeDtypeStruct(query_grad.shape, query_grad.dtype), grad_shape, grad_shape),
        in_specs=[vmem, vmem, vmem],
        out_specs=(vmem, vmem, vmem),
        scratch_shapes=[
            pltpu.VMEM(query_grad.shape, query_grad.dtype),
            pltpu.VMEM((sources, block, head_width), key_grad.dtype),
            pltpu.VMEM((sources, block, head_width), key_grad.dtype),
            sems,
            sems,
            sems,
            sems,
            pltpu.SemaphoreType.DMA((2, sources)),
            pltpu.SemaphoreType.DMA((2, sources)),
        ],
        compiler_params=pltpu.CompilerParams(collective_id=collective, has_side_effects=True),
    )(query_grad, key_grad, value_grad)


def scatter_rows(rows, parts, collective):
    return grp_exchange(
        rows.reshape(parts, rows.shape[0] // parts, rows.shape[1]), parts, False, collective
    )


def broadcast_rows(chunk, parts, collective):
    gathered = grp_exchange(chunk, parts, True, collective)
    return gathered.reshape(parts * chunk.shape[0], chunk.shape[1])


def per_device(queries, scene_keys, scene_values, grad_output, tile_list, tile_counts):
    items_here = queries.shape[0]
    head_width = queries.shape[2]
    query_rows = queries.shape[1]
    scene_here = scene_keys.shape[0]
    heads_total = scene_keys.shape[1] // head_width
    seq_devices = lax.axis_size("seq")
    groups = lax.axis_size("grp")
    chunk_rows = query_rows // groups
    group_keys = scene_here * seq_devices
    copies = max(1, QPARTS // items_here)
    heads_here = max(1, items_here // QPARTS)
    softmax_scale = head_width ** (-0.5)
    half_keys = scene_here // QPARTS
    both_here = jnp.stack(
        [
            scene_keys.reshape(QPARTS, half_keys, heads_total, head_width),
            scene_values.reshape(QPARTS, half_keys, heads_total, head_width),
        ],
        axis=3,
    ).transpose(2, 0, 1, 3, 4)
    mine = lax.all_to_all(
        both_here.reshape(seq_devices, half_keys, 2 * head_width), "seq", 0, 0, tiled=True
    )
    pairs = [(2 * h + c, 2 * h + 1 - c) for h in range(seq_devices // 2) for c in range(2)]
    other = lax.ppermute(mine, "seq", pairs)
    core = lax.rem(lax.axis_index("seq"), 2)
    both_group = jnp.where(
        core == 0, jnp.stack([mine, other], axis=1), jnp.stack([other, mine], axis=1)
    ).reshape(group_keys, 2 * head_width)
    key_group = both_group[:, None, :head_width]
    value_group = both_group[:, None, head_width:]
    part_accum, stats = forward_item(
        queries[0],
        key_group[:, 0, :],
        value_group[:, 0, :],
        tile_list[0, 0],
        tile_counts[0, 0],
        softmax_scale,
        groups,
    )
    out_rows, out_stats = grp_combine(part_accum, stats, 0)
    attended = out_rows.reshape(1, query_rows, head_width)
    query_grad, key_grad, value_grad = backward_item(
        queries[0],
        key_group[:, 0, :],
        value_group[:, 0, :],
        grad_output[0],
        attended[0],
        out_stats,
        tile_list[0, 0],
        tile_counts[0, 0],
        softmax_scale,
    )
    grad_queries, grad_keys, grad_values = back_exchange(
        query_grad.reshape(groups, chunk_rows, head_width), key_grad, value_grad, groups, seq_devices, 2
    )
    grad_queries = grad_queries.reshape(1, query_rows, head_width)
    return (attended, grad_queries, grad_keys, grad_values)


def solution(mesh):
    in_specs = (
        P("seq", None, None),
        P(("grp", "seq"), None),
        P(("grp", "seq"), None),
        P("seq", None, None),
        P("grp", "seq", None, None),
        P("grp", "seq"),
    )
    out_specs = (
        P("seq", None, None),
        P("seq", None, None),
        P(("grp", "seq"), None),
        P(("grp", "seq"), None),
    )
    return jax.shard_map(
        per_device, mesh=mesh, in_specs=in_specs, out_specs=out_specs, check_vma=False
    )
```

```python
import jax
import jax.numpy as jnp
from jax import lax
from jax.experimental import pallas as pl
from jax.experimental.pallas import tpu as pltpu
from jax.sharding import PartitionSpec as P

QPARTS = 2
QBLK = 512
KBLK = 512


NEG_START = -1e30


LIST_SLOTS = 9


def tile_starts(list_ref, position):
    query_block = jnp.clip(list_ref[position, 0], 0, QPARTS - 1)
    key_block = jnp.clip(list_ref[position, 1], 0, 7)
    return (
        pl.multiple_of(query_block * QBLK, QBLK),
        pl.multiple_of(key_block * KBLK, KBLK),
    )


def forward_kernel(
    softmax_scale, list_ref, count_ref, q_ref, k_ref, v_ref, acc_out, stats_out, max_ref, total_ref, accum_ref
):
    max_ref[...] = jnp.full(max_ref.shape, NEG_START, jnp.float32)
    total_ref[...] = jnp.zeros(total_ref.shape, jnp.float32)
    accum_ref[...] = jnp.zeros(accum_ref.shape, jnp.float32)
    live_tiles = jnp.clip(count_ref[0], 0, LIST_SLOTS)

    def visit(position, carry):
        query_start, key_start = tile_starts(list_ref, position)
        rows = pl.ds(query_start, QBLK)
        keys = pl.ds(key_start, KBLK)
        scores = (
            lax.dot_general(
                q_ref[rows, :], k_ref[keys, :], (((1,), (1,)), ((), ())),
                preferred_element_type=jnp.float32,
            )
            * softmax_scale
        )
        old_max = max_ref[rows, :]
        new_max = jnp.maximum(old_max, jnp.max(scores, axis=1, keepdims=True))
        new_max = new_max.astype(jnp.bfloat16).astype(jnp.float32)
        weights = jnp.exp(scores - new_max[:, :1])
        shrink = jnp.exp(old_max - new_max)
        total_ref[rows, :] = total_ref[rows, :] * shrink + jnp.sum(weights, axis=1, keepdims=True)
        accum_ref[rows, :] = accum_ref[rows, :] * shrink[:, :1] + jnp.dot(
            weights.astype(jnp.bfloat16), v_ref[keys, :], preferred_element_type=jnp.float32
        )
        max_ref[rows, :] = new_max
        return carry

    lax.fori_loop(0, live_tiles, visit, 0)
    groups, chunk_rows = acc_out.shape[0], acc_out.shape[1]
    for g in range(groups):
        rows = pl.ds(g * chunk_rows, chunk_rows)
        acc_out[g] = accum_ref[rows, :].astype(acc_out.dtype)
        stacked = jnp.concatenate([max_ref[rows, :], total_ref[rows, :]], axis=0)
        stats_out[g] = jnp.transpose(stacked)[:8, :]


def forward_item(query_item, key_head, value_head, listing, live_tiles, softmax_scale, groups):
    query_rows, head_width = query_item.shape
    chunk_rows = query_rows // groups
    smem = pl.BlockSpec(memory_space=pltpu.SMEM)
    vmem = pl.BlockSpec(memory_space=pltpu.VMEM)
    rows_f32 = pltpu.VMEM((query_rows, head_width), jnp.float32)
    return pl.pallas_call(
        lambda *refs: forward_kernel(softmax_scale, *refs),
        out_shape=(
            jax.ShapeDtypeStruct((groups, chunk_rows, head_width), jnp.bfloat16),
            jax.ShapeDtypeStruct((groups, 8, 2 * chunk_rows), jnp.float32),
        ),
        in_specs=[smem, smem, vmem, vmem, vmem],
        out_specs=(vmem, vmem),
        scratch_shapes=[rows_f32, rows_f32, rows_f32],
    )(listing, live_tiles.reshape(1), query_item, key_head, value_head)


def backward_kernel(
    softmax_scale, list_ref, count_ref, q_ref, k_ref, v_ref, do_ref, att_ref, stats_ref,
    dq_ref, dk_ref, dv_ref, dq_acc, dk_acc, dv_acc, log_ref, delta_ref,
):
    groups = stats_ref.shape[0]
    chunk_rows = stats_ref.shape[2] // 2
    for g in range(groups):
        rows = pl.ds(g * chunk_rows, chunk_rows)
        columns = jnp.transpose(jnp.broadcast_to(stats_ref[g][0:1, :], (2 * chunk_rows, 2 * chunk_rows)))
        log_ref[rows, :] = columns[:chunk_rows, 0:1] + jnp.log(columns[chunk_rows:, 0:1])
        delta_ref[rows, :] = jnp.sum(
            att_ref[rows, :].astype(jnp.float32) * do_ref[rows, :].astype(jnp.float32),
            axis=1,
            keepdims=True,
        )
    dq_acc[...] = jnp.zeros(dq_acc.shape, jnp.float32)
    dk_acc[...] = jnp.zeros(dk_acc.shape, jnp.float32)
    dv_acc[...] = jnp.zeros(dv_acc.shape, jnp.float32)
    live_tiles = jnp.clip(count_ref[0], 0, LIST_SLOTS)

    def visit(position, carry):
        query_start, key_start = tile_starts(list_ref, position)
        rows = pl.ds(query_start, QBLK)
        keys = pl.ds(key_start, KBLK)
        query_block = q_ref[rows, :]
        grad_block = do_ref[rows, :]
        key_block = k_ref[keys, :]
        value_block = v_ref[keys, :]
        scores = (
            lax.dot_general(
                query_block, key_block, (((1,), (1,)), ((), ())),
                preferred_element_type=jnp.float32,
            )
            * softmax_scale
        )
        probs = jnp.exp(scores - log_ref[rows, :])
        probs_half = probs.astype(jnp.bfloat16)
        dv_acc[keys, :] += lax.dot_general(
            probs_half, grad_block, (((0,), (0,)), ((), ())), preferred_element_type=jnp.float32
        )
        prob_grad = lax.dot_general(
            grad_block, value_block, (((1,), (1,)), ((), ())), preferred_element_type=jnp.float32
        )
        score_grad = (probs * (prob_grad - delta_ref[rows, :])).astype(jnp.bfloat16)
        dq_acc[rows, :] += (
            jnp.dot(score_grad, key_block, preferred_element_type=jnp.float32) * softmax_scale
        )
        dk_acc[keys, :] += (
            lax.dot_general(
                score_grad, query_block, (((0,), (0,)), ((), ())),
                preferred_element_type=jnp.float32,
            )
            * softmax_scale
        )
        return carry

    lax.fori_loop(0, live_tiles, visit, 0)
    dq_ref[...] = dq_acc[...].astype(dq_ref.dtype)
    dk_ref[...] = dk_acc[...].astype(dk_ref.dtype)
    dv_ref[...] = dv_acc[...].astype(dv_ref.dtype)


def backward_item(
    query_item, key_head, value_head, grad_item, attended, stats, listing, live_tiles, softmax_scale,
):
    query_rows, head_width = query_item.shape
    key_rows = key_head.shape[0]
    smem = pl.BlockSpec(memory_space=pltpu.SMEM)
    vmem = pl.BlockSpec(memory_space=pltpu.VMEM)
    return pl.pallas_call(
        lambda *refs: backward_kernel(softmax_scale, *refs),
        out_shape=(
            jax.ShapeDtypeStruct((query_rows, head_width), jnp.bfloat16),
            jax.ShapeDtypeStruct((key_rows, head_width), jnp.bfloat16),
            jax.ShapeDtypeStruct((key_rows, head_width), jnp.bfloat16),
        ),
        in_specs=[smem, smem] + [vmem] * 6,
        out_specs=(vmem, vmem, vmem),
        scratch_shapes=[
            pltpu.VMEM((query_rows, head_width), jnp.float32),
            pltpu.VMEM((key_rows, head_width), jnp.float32),
            pltpu.VMEM((key_rows, head_width), jnp.float32),
            pltpu.VMEM((query_rows, 1), jnp.float32),
            pltpu.VMEM((query_rows, 1), jnp.float32),
        ],
    )(
        listing,
        live_tiles.reshape(1),
        query_item,
        key_head,
        value_head,
        grad_item,
        attended,
        stats,
    )


def exchange_kernel(broadcast, x_ref, y_ref, send_sem, recv_sem):
    groups = y_ref.shape[0]
    me = lax.axis_index("grp")
    lane = lax.axis_index("seq")
    mesh_ids = pl.DeviceIdType.MESH
    barrier = pltpu.get_barrier_semaphore()
    for step in range(1, groups):
        pl.semaphore_signal(
            barrier, inc=1, device_id=(lax.rem(me + step, groups), lane), device_id_type=mesh_ids
        )
    pl.semaphore_wait(barrier, groups - 1)
    copies = []
    for step in range(1, groups):
        target = lax.rem(me + step, groups)
        copy = pltpu.make_async_remote_copy(
            src_ref=x_ref if broadcast else x_ref.at[target],
            dst_ref=y_ref.at[me],
            send_sem=send_sem.at[step],
            recv_sem=recv_sem.at[step],
            device_id=(target, lane),
            device_id_type=mesh_ids,
        )
        copy.start()
        copies.append(copy)
    y_ref[me] = x_ref[...] if broadcast else x_ref[me]
    for copy in copies:
        copy.wait()


def grp_exchange(x, groups, broadcast, collective):
    out_shape = (groups,) + (x.shape if broadcast else x.shape[1:])
    vmem = pl.BlockSpec(memory_space=pltpu.VMEM)
    return pl.pallas_call(
        lambda *refs: exchange_kernel(broadcast, *refs),
        out_shape=jax.ShapeDtypeStruct(out_shape, x.dtype),
        in_specs=[vmem],
        out_specs=vmem,
        scratch_shapes=[pltpu.SemaphoreType.DMA((groups,)), pltpu.SemaphoreType.DMA((groups,))],
        compiler_params=pltpu.CompilerParams(collective_id=collective, has_side_effects=True),
    )(x)


def reduce_kernel(x_ref, y_ref, part_ref, send_sem, recv_sem, back_send, back_recv):
    groups = y_ref.shape[0]
    me = lax.axis_index("grp")
    lane = lax.axis_index("seq")
    mesh_ids = pl.DeviceIdType.MESH
    barrier = pltpu.get_barrier_semaphore()
    for step in range(1, groups):
        pl.semaphore_signal(
            barrier, inc=1, device_id=(lax.rem(me + step, groups), lane), device_id_type=mesh_ids
        )
    pl.semaphore_wait(barrier, groups - 1)
    copies = []
    for step in range(1, groups):
        target = lax.rem(me + step, groups)
        copy = pltpu.make_async_remote_copy(
            src_ref=x_ref.at[target],
            dst_ref=part_ref.at[me],
            send_sem=send_sem.at[step],
            recv_sem=recv_sem.at[step],
            device_id=(target, lane),
            device_id_type=mesh_ids,
        )
        copy.start()
        copies.append(copy)
    part_ref[me] = x_ref[me]
    for copy in copies:
        copy.wait()
    y_ref[me] = jnp.sum(part_ref[...].astype(jnp.float32), axis=0).astype(y_ref.dtype)
    copies = []
    for step in range(1, groups):
        target = lax.rem(me + step, groups)
        copy = pltpu.make_async_remote_copy(
            src_ref=y_ref.at[me],
            dst_ref=y_ref.at[me],
            send_sem=back_send.at[step],
            recv_sem=back_recv.at[step],
            device_id=(target, lane),
            device_id_type=mesh_ids,
        )
        copy.start()
        copies.append(copy)
    for copy in copies:
        copy.wait()


def grp_reduce(x, groups, collective):
    vmem = pl.BlockSpec(memory_space=pltpu.VMEM)
    sems = pltpu.SemaphoreType.DMA((groups,))
    return pl.pallas_call(
        reduce_kernel,
        out_shape=jax.ShapeDtypeStruct(x.shape, x.dtype),
        in_specs=[vmem],
        out_specs=vmem,
        scratch_shapes=[pltpu.VMEM(x.shape, x.dtype), sems, sems, sems, sems],
        compiler_params=pltpu.CompilerParams(collective_id=collective, has_side_effects=True),
    )(x)


def combine_kernel(
    acc_in, stats_in, out_ref, stats_out, acc_part, stats_part,
    send_acc, recv_acc, send_stats, recv_stats, back_send, back_recv, stat_send, stat_recv,
):
    groups, chunk_rows, head_width = out_ref.shape
    me = lax.axis_index("grp")
    lane = lax.axis_index("seq")
    mesh_ids = pl.DeviceIdType.MESH
    barrier = pltpu.get_barrier_semaphore()
    for step in range(1, groups):
        pl.semaphore_signal(
            barrier, inc=1, device_id=(lax.rem(me + step, groups), lane), device_id_type=mesh_ids
        )
    pl.semaphore_wait(barrier, groups - 1)
    copies = []
    for step in range(1, groups):
        target = lax.rem(me + step, groups)
        for source, landing, sent, got in (
            (acc_in, acc_part, send_acc, recv_acc),
            (stats_in, stats_part, send_stats, recv_stats),
        ):
            copy = pltpu.make_async_remote_copy(
                src_ref=source.at[target],
                dst_ref=landing.at[me],
                send_sem=sent.at[step],
                recv_sem=got.at[step],
                device_id=(target, lane),
                device_id_type=mesh_ids,
            )
            copy.start()
            copies.append(copy)
    acc_part[me] = acc_in[me]
    stats_part[me] = stats_in[me]
    for copy in copies:
        copy.wait()
    columns = jnp.transpose(stats_part[...].reshape(groups * 8, 128))
    maxima = [columns[:chunk_rows, 8 * g : 8 * g + 1] for g in range(groups)]
    totals = [columns[chunk_rows:, 8 * g : 8 * g + 1] for g in range(groups)]
    top = maxima[0]
    for g in range(1, groups):
        top = jnp.maximum(top, maxima[g])
    row_total = jnp.zeros_like(top)
    row_accum = jnp.zeros((chunk_rows, head_width), jnp.float32)
    for g in range(groups):
        shrink = jnp.exp(maxima[g] - top)
        row_total = row_total + totals[g] * shrink
        row_accum = row_accum + acc_part[g].astype(jnp.float32) * shrink
    out_ref[me] = (row_accum / row_total).astype(out_ref.dtype)
    spread = jnp.concatenate(
        [jnp.broadcast_to(top, (chunk_rows, 128)), jnp.broadcast_to(row_total, (chunk_rows, 128))], axis=0
    )
    stats_out[me] = jnp.transpose(spread)[:8, :]
    copies = []
    for step in range(1, groups):
        target = lax.rem(me + step, groups)
        for source, sent, got in ((out_ref, back_send, back_recv), (stats_out, stat_send, stat_recv)):
            copy = pltpu.make_async_remote_copy(
                src_ref=source.at[me],
                dst_ref=source.at[me],
                send_sem=sent.at[step],
                recv_sem=got.at[step],
                device_id=(target, lane),
                device_id_type=mesh_ids,
            )
            copy.start()
            copies.append(copy)
    for copy in copies:
        copy.wait()


def grp_combine(accum, stats, collective):
    groups = accum.shape[0]
    vmem = pl.BlockSpec(memory_space=pltpu.VMEM)
    sems = pltpu.SemaphoreType.DMA((groups,))
    return pl.pallas_call(
        combine_kernel,
        out_shape=(
            jax.ShapeDtypeStruct(accum.shape, accum.dtype),
            jax.ShapeDtypeStruct(stats.shape, stats.dtype),
        ),
        in_specs=[vmem, vmem],
        out_specs=(vmem, vmem),
        scratch_shapes=[pltpu.VMEM(accum.shape, accum.dtype), pltpu.VMEM(stats.shape, stats.dtype)]
        + [sems] * 8,
        compiler_params=pltpu.CompilerParams(collective_id=collective, has_side_effects=True),
    )(accum, stats)


def back_kernel(
    dq_in, dk_in, dv_in, dq_out, gk_out, gv_out, part_ref, recv_k, recv_v,
    send_sem, recv_sem, back_send, back_recv, kv_send, kv_recv,
):
    groups = dq_out.shape[0]
    sources, block, head_width = recv_k.shape
    me = lax.axis_index("grp")
    lane = lax.axis_index("seq")
    mesh_ids = pl.DeviceIdType.MESH
    barrier = pltpu.get_barrier_semaphore()
    for step in range(1, groups):
        pl.semaphore_signal(
            barrier, inc=1, device_id=(lax.rem(me + step, groups), lane), device_id_type=mesh_ids
        )
    for step in range(1, sources):
        pl.semaphore_signal(
            barrier, inc=1, device_id=(me, lax.rem(lane + step, sources)), device_id_type=mesh_ids
        )
    pl.semaphore_wait(barrier, groups - 1 + sources - 1)
    returns = []
    for step in range(1, sources):
        target = lax.rem(lane + step, sources)
        rows = pl.ds(pl.multiple_of(target * block, block), block)
        for index, (source, landing) in enumerate(((dk_in, recv_k), (dv_in, recv_v))):
            copy = pltpu.make_async_remote_copy(
                src_ref=source.at[rows],
                dst_ref=landing.at[lane],
                send_sem=kv_send.at[index, step],
                recv_sem=kv_recv.at[index, step],
                device_id=(me, target),
                device_id_type=mesh_ids,
            )
            copy.start()
            returns.append(copy)
    copies = []
    for step in range(1, groups):
        target = lax.rem(me + step, groups)
        copy = pltpu.make_async_remote_copy(
            src_ref=dq_in.at[target],
            dst_ref=part_ref.at[me],
            send_sem=send_sem.at[step],
            recv_sem=recv_sem.at[step],
            device_id=(target, lane),
            device_id_type=mesh_ids,
        )
        copy.start()
        copies.append(copy)
    own_rows = pl.ds(pl.multiple_of(lane * block, block), block)
    recv_k[lane] = dk_in[own_rows, :]
    recv_v[lane] = dv_in[own_rows, :]
    part_ref[me] = dq_in[me]
    for copy in copies:
        copy.wait()
    dq_out[me] = jnp.sum(part_ref[...].astype(jnp.float32), axis=0).astype(dq_out.dtype)
    copies = []
    for step in range(1, groups):
        target = lax.rem(me + step, groups)
        copy = pltpu.make_async_remote_copy(
            src_ref=dq_out.at[me],
            dst_ref=dq_out.at[me],
            send_sem=back_send.at[step],
            recv_sem=back_recv.at[step],
            device_id=(target, lane),
            device_id_type=mesh_ids,
        )
        copy.start()
        copies.append(copy)
    for copy in returns:
        copy.wait()
    for head in range(sources // 2):
        cols = pl.ds(head * head_width, head_width)
        for landing, out_ref in ((recv_k, gk_out), (recv_v, gv_out)):
            out_ref[:, cols] = (
                landing[2 * head].astype(jnp.float32) + landing[2 * head + 1].astype(jnp.float32)
            ).astype(out_ref.dtype)
    for copy in copies:
        copy.wait()


def back_exchange(query_grad, key_grad, value_grad, groups, sources, collective):
    head_width = query_grad.shape[-1]
    block = key_grad.shape[0] // sources
    vmem = pl.BlockSpec(memory_space=pltpu.VMEM)
    grad_shape = jax.ShapeDtypeStruct((block, sources // 2 * head_width), key_grad.dtype)
    sems = pltpu.SemaphoreType.DMA((groups,))
    return pl.pallas_call(
        back_kernel,
        out_shape=(jax.ShapeDtypeStruct(query_grad.shape, query_grad.dtype), grad_shape, grad_shape),
        in_specs=[vmem, vmem, vmem],
        out_specs=(vmem, vmem, vmem),
        scratch_shapes=[
            pltpu.VMEM(query_grad.shape, query_grad.dtype),
            pltpu.VMEM((sources, block, head_width), key_grad.dtype),
            pltpu.VMEM((sources, block, head_width), key_grad.dtype),
            sems,
            sems,
            sems,
            sems,
            pltpu.SemaphoreType.DMA((2, sources)),
            pltpu.SemaphoreType.DMA((2, sources)),
        ],
        compiler_params=pltpu.CompilerParams(collective_id=collective, has_side_effects=True),
    )(query_grad, key_grad, value_grad)


def gather_kernel(k_ref, v_ref, k_out, v_out, send_sem, recv_sem, pair_send, pair_recv):
    sources, halves, half, head_width = k_out.shape
    me = lax.axis_index("seq")
    grp_here = lax.axis_index("grp")
    mine = lax.rem(me, 2)
    partner = me + 1 - 2 * mine
    head = me // 2
    mesh_ids = pl.DeviceIdType.MESH
    barrier = pltpu.get_barrier_semaphore()
    for step in range(1, sources):
        pl.semaphore_signal(
            barrier, inc=1, device_id=(grp_here, lax.rem(me + step, sources)), device_id_type=mesh_ids
        )
    pl.semaphore_wait(barrier, sources - 1)
    copies = []
    for step in range(1, sources):
        target = lax.rem(me + step, sources)
        rows = pl.ds(pl.multiple_of(lax.rem(target, 2) * half, half), half)
        cols = pl.ds(pl.multiple_of((target // 2) * head_width, head_width), head_width)
        for index, (source, landing) in enumerate(((k_ref, k_out), (v_ref, v_out))):
            copy = pltpu.make_async_remote_copy(
                src_ref=source.at[rows, cols],
                dst_ref=landing.at[me, lax.rem(target, 2)],
                send_sem=send_sem.at[index, step],
                recv_sem=recv_sem.at[index, step],
                device_id=(grp_here, target),
                device_id_type=mesh_ids,
            )
            copy.start()
            copies.append(copy)
    own_rows = pl.ds(pl.multiple_of(mine * half, half), half)
    own_cols = pl.ds(pl.multiple_of(head * head_width, head_width), head_width)
    k_out[me, mine] = k_ref[own_rows, own_cols]
    v_out[me, mine] = v_ref[own_rows, own_cols]
    for copy in copies:
        copy.wait()
    copies = []
    for index, landing in enumerate((k_out, v_out)):
        copy = pltpu.make_async_remote_copy(
            src_ref=landing.at[:, mine],
            dst_ref=landing.at[:, mine],
            send_sem=pair_send.at[index],
            recv_sem=pair_recv.at[index],
            device_id=(grp_here, partner),
            device_id_type=mesh_ids,
        )
        copy.start()
        copies.append(copy)
    for copy in copies:
        copy.wait()


def seq_gather(scene_keys, scene_values, sources, head_width, collective):
    half = scene_keys.shape[0] // QPARTS
    vmem = pl.BlockSpec(memory_space=pltpu.VMEM)
    out = jax.ShapeDtypeStruct((sources, QPARTS, half, head_width), scene_keys.dtype)
    return pl.pallas_call(
        gather_kernel,
        out_shape=(out, out),
        in_specs=[vmem, vmem],
        out_specs=(vmem, vmem),
        scratch_shapes=[
            pltpu.SemaphoreType.DMA((2, sources)),
            pltpu.SemaphoreType.DMA((2, sources)),
            pltpu.SemaphoreType.DMA((2,)),
            pltpu.SemaphoreType.DMA((2,)),
        ],
        compiler_params=pltpu.CompilerParams(collective_id=collective, has_side_effects=True),
    )(scene_keys, scene_values)


def scatter_rows(rows, parts, collective):
    return grp_exchange(
        rows.reshape(parts, rows.shape[0] // parts, rows.shape[1]), parts, False, collective
    )


def broadcast_rows(chunk, parts, collective):
    gathered = grp_exchange(chunk, parts, True, collective)
    return gathered.reshape(parts * chunk.shape[0], chunk.shape[1])


def per_device(queries, scene_keys, scene_values, grad_output, tile_list, tile_counts):
    items_here = queries.shape[0]
    head_width = queries.shape[2]
    query_rows = queries.shape[1]
    scene_here = scene_keys.shape[0]
    heads_total = scene_keys.shape[1] // head_width
    seq_devices = lax.axis_size("seq")
    groups = lax.axis_size("grp")
    chunk_rows = query_rows // groups
    group_keys = scene_here * seq_devices
    copies = max(1, QPARTS // items_here)
    heads_here = max(1, items_here // QPARTS)
    softmax_scale = head_width ** (-0.5)
    half_keys = scene_here // QPARTS
    key_halves, value_halves = seq_gather(scene_keys, scene_values, seq_devices, head_width, 4)
    key_group = key_halves.reshape(group_keys, 1, head_width)
    value_group = value_halves.reshape(group_keys, 1, head_width)
    part_accum, stats = forward_item(
        queries[0],
        key_group[:, 0, :],
        value_group[:, 0, :],
        tile_list[0, 0],
        tile_counts[0, 0],
        softmax_scale,
        groups,
    )
    out_rows, out_stats = grp_combine(part_accum, stats, 0)
    attended = out_rows.reshape(1, query_rows, head_width)
    query_grad, key_grad, value_grad = backward_item(
        queries[0],
        key_group[:, 0, :],
        value_group[:, 0, :],
        grad_output[0],
        attended[0],
        out_stats,
        tile_list[0, 0],
        tile_counts[0, 0],
        softmax_scale,
    )
    grad_queries, grad_keys, grad_values = back_exchange(
        query_grad.reshape(groups, chunk_rows, head_width), key_grad, value_grad, groups, seq_devices, 2
    )
    grad_queries = grad_queries.reshape(1, query_rows, head_width)
    return (attended, grad_queries, grad_keys, grad_values)


def solution(mesh):
    in_specs = (
        P("seq", None, None),
        P(("grp", "seq"), None),
        P(("grp", "seq"), None),
        P("seq", None, None),
        P("grp", "seq", None, None),
        P("grp", "seq"),
    )
    out_specs = (
        P("seq", None, None),
        P("seq", None, None),
        P(("grp", "seq"), None),
        P(("grp", "seq"), None),
    )
    return jax.shard_map(
        per_device, mesh=mesh, in_specs=in_specs, out_specs=out_specs, check_vma=False
    )
```

```python
import jax
import jax.numpy as jnp
from jax import lax
from jax.experimental import pallas as pl
from jax.experimental.pallas import tpu as pltpu
from jax.sharding import PartitionSpec as P

QPARTS = 2
QBLK = 512
KBLK = 512


NEG_START = -1e30


LIST_SLOTS = 9


def tile_starts(list_ref, position):
    query_block = jnp.clip(list_ref[position, 0], 0, QPARTS - 1)
    key_block = jnp.clip(list_ref[position, 1], 0, 7)
    return (
        pl.multiple_of(query_block * QBLK, QBLK),
        pl.multiple_of(key_block * KBLK, KBLK),
    )


def forward_kernel(
    softmax_scale, list_ref, count_ref, q_ref, k_ref, v_ref, acc_out, stats_out, max_ref, total_ref, accum_ref
):
    max_ref[...] = jnp.full(max_ref.shape, NEG_START, jnp.float32)
    total_ref[...] = jnp.zeros(total_ref.shape, jnp.float32)
    accum_ref[...] = jnp.zeros(accum_ref.shape, jnp.float32)
    live_tiles = jnp.clip(count_ref[0], 0, LIST_SLOTS)

    def visit(position, carry):
        query_start, key_start = tile_starts(list_ref, position)
        rows = pl.ds(query_start, QBLK)
        keys = pl.ds(key_start, KBLK)
        scores = (
            lax.dot_general(
                q_ref[rows, :], k_ref[keys, :], (((1,), (1,)), ((), ())),
                preferred_element_type=jnp.float32,
            )
            * softmax_scale
        )
        old_max = max_ref[rows, :]
        new_max = jnp.maximum(old_max, jnp.max(scores, axis=1, keepdims=True))
        new_max = new_max.astype(jnp.bfloat16).astype(jnp.float32)
        weights = jnp.exp(scores - new_max[:, :1])
        shrink = jnp.exp(old_max - new_max)
        total_ref[rows, :] = total_ref[rows, :] * shrink + jnp.sum(weights, axis=1, keepdims=True)
        accum_ref[rows, :] = accum_ref[rows, :] * shrink[:, :1] + jnp.dot(
            weights.astype(jnp.bfloat16), v_ref[keys, :], preferred_element_type=jnp.float32
        )
        max_ref[rows, :] = new_max
        return carry

    lax.fori_loop(0, live_tiles, visit, 0)
    groups, chunk_rows = acc_out.shape[0], acc_out.shape[1]
    for g in range(groups):
        rows = pl.ds(g * chunk_rows, chunk_rows)
        acc_out[g] = accum_ref[rows, :].astype(acc_out.dtype)
        stacked = jnp.concatenate([max_ref[rows, :], total_ref[rows, :]], axis=0)
        stats_out[g] = jnp.transpose(stacked)[:8, :]


def forward_item(query_item, key_head, value_head, listing, live_tiles, softmax_scale, groups):
    query_rows, head_width = query_item.shape
    chunk_rows = query_rows // groups
    smem = pl.BlockSpec(memory_space=pltpu.SMEM)
    vmem = pl.BlockSpec(memory_space=pltpu.VMEM)
    rows_f32 = pltpu.VMEM((query_rows, head_width), jnp.float32)
    return pl.pallas_call(
        lambda *refs: forward_kernel(softmax_scale, *refs),
        out_shape=(
            jax.ShapeDtypeStruct((groups, chunk_rows, head_width), jnp.bfloat16),
            jax.ShapeDtypeStruct((groups, 8, 2 * chunk_rows), jnp.float32),
        ),
        in_specs=[smem, smem, vmem, vmem, vmem],
        out_specs=(vmem, vmem),
        scratch_shapes=[rows_f32, rows_f32, rows_f32],
    )(listing, live_tiles.reshape(1), query_item, key_head, value_head)


def backward_kernel(
    softmax_scale, list_ref, count_ref, q_ref, k_ref, v_ref, do_ref, att_ref, stats_ref,
    dq_ref, dk_ref, dv_ref, dq_acc, dk_acc, dv_acc, log_ref, delta_ref,
):
    groups = stats_ref.shape[0]
    chunk_rows = stats_ref.shape[2] // 2
    for g in range(groups):
        rows = pl.ds(g * chunk_rows, chunk_rows)
        columns = jnp.transpose(jnp.broadcast_to(stats_ref[g][0:1, :], (2 * chunk_rows, 2 * chunk_rows)))
        log_ref[rows, :] = columns[:chunk_rows, 0:1] + jnp.log(columns[chunk_rows:, 0:1])
        delta_ref[rows, :] = jnp.sum(
            att_ref[rows, :].astype(jnp.float32) * do_ref[rows, :].astype(jnp.float32),
            axis=1,
            keepdims=True,
        )
    dq_acc[...] = jnp.zeros(dq_acc.shape, jnp.float32)
    dk_acc[...] = jnp.zeros(dk_acc.shape, jnp.float32)
    dv_acc[...] = jnp.zeros(dv_acc.shape, jnp.float32)
    live_tiles = jnp.clip(count_ref[0], 0, LIST_SLOTS)

    def visit(position, carry):
        query_start, key_start = tile_starts(list_ref, position)
        rows = pl.ds(query_start, QBLK)
        keys = pl.ds(key_start, KBLK)
        query_block = q_ref[rows, :]
        grad_block = do_ref[rows, :]
        key_block = k_ref[keys, :]
        value_block = v_ref[keys, :]
        scores = (
            lax.dot_general(
                query_block, key_block, (((1,), (1,)), ((), ())),
                preferred_element_type=jnp.float32,
            )
            * softmax_scale
        )
        probs = jnp.exp(scores - log_ref[rows, :])
        probs_half = probs.astype(jnp.bfloat16)
        dv_acc[keys, :] += lax.dot_general(
            probs_half, grad_block, (((0,), (0,)), ((), ())), preferred_element_type=jnp.float32
        )
        prob_grad = lax.dot_general(
            grad_block, value_block, (((1,), (1,)), ((), ())), preferred_element_type=jnp.float32
        )
        score_grad = (probs * (prob_grad - delta_ref[rows, :])).astype(jnp.bfloat16)
        dq_acc[rows, :] += (
            jnp.dot(score_grad, key_block, preferred_element_type=jnp.float32) * softmax_scale
        )
        dk_acc[keys, :] += (
            lax.dot_general(
                score_grad, query_block, (((0,), (0,)), ((), ())),
                preferred_element_type=jnp.float32,
            )
            * softmax_scale
        )
        return carry

    lax.fori_loop(0, live_tiles, visit, 0)
    dq_ref[...] = dq_acc[...].astype(dq_ref.dtype)
    dk_ref[...] = dk_acc[...].astype(dk_ref.dtype)
    dv_ref[...] = dv_acc[...].astype(dv_ref.dtype)


def backward_item(
    query_item, key_head, value_head, grad_item, attended, stats, listing, live_tiles, softmax_scale,
):
    query_rows, head_width = query_item.shape
    key_rows = key_head.shape[0]
    smem = pl.BlockSpec(memory_space=pltpu.SMEM)
    vmem = pl.BlockSpec(memory_space=pltpu.VMEM)
    return pl.pallas_call(
        lambda *refs: backward_kernel(softmax_scale, *refs),
        out_shape=(
            jax.ShapeDtypeStruct((query_rows, head_width), jnp.bfloat16),
            jax.ShapeDtypeStruct((key_rows, head_width), jnp.bfloat16),
            jax.ShapeDtypeStruct((key_rows, head_width), jnp.bfloat16),
        ),
        in_specs=[smem, smem] + [vmem] * 6,
        out_specs=(vmem, vmem, vmem),
        scratch_shapes=[
            pltpu.VMEM((query_rows, head_width), jnp.float32),
            pltpu.VMEM((key_rows, head_width), jnp.float32),
            pltpu.VMEM((key_rows, head_width), jnp.float32),
            pltpu.VMEM((query_rows, 1), jnp.float32),
            pltpu.VMEM((query_rows, 1), jnp.float32),
        ],
    )(
        listing,
        live_tiles.reshape(1),
        query_item,
        key_head,
        value_head,
        grad_item,
        attended,
        stats,
    )


def exchange_kernel(broadcast, x_ref, y_ref, send_sem, recv_sem):
    groups = y_ref.shape[0]
    me = lax.axis_index("grp")
    lane = lax.axis_index("seq")
    mesh_ids = pl.DeviceIdType.MESH
    barrier = pltpu.get_barrier_semaphore()
    for step in range(1, groups):
        pl.semaphore_signal(
            barrier, inc=1, device_id=(lax.rem(me + step, groups), lane), device_id_type=mesh_ids
        )
    pl.semaphore_wait(barrier, groups - 1)
    copies = []
    for step in range(1, groups):
        target = lax.rem(me + step, groups)
        copy = pltpu.make_async_remote_copy(
            src_ref=x_ref if broadcast else x_ref.at[target],
            dst_ref=y_ref.at[me],
            send_sem=send_sem.at[step],
            recv_sem=recv_sem.at[step],
            device_id=(target, lane),
            device_id_type=mesh_ids,
        )
        copy.start()
        copies.append(copy)
    y_ref[me] = x_ref[...] if broadcast else x_ref[me]
    for copy in copies:
        copy.wait()


def grp_exchange(x, groups, broadcast, collective):
    out_shape = (groups,) + (x.shape if broadcast else x.shape[1:])
    vmem = pl.BlockSpec(memory_space=pltpu.VMEM)
    return pl.pallas_call(
        lambda *refs: exchange_kernel(broadcast, *refs),
        out_shape=jax.ShapeDtypeStruct(out_shape, x.dtype),
        in_specs=[vmem],
        out_specs=vmem,
        scratch_shapes=[pltpu.SemaphoreType.DMA((groups,)), pltpu.SemaphoreType.DMA((groups,))],
        compiler_params=pltpu.CompilerParams(collective_id=collective, has_side_effects=True),
    )(x)


def reduce_kernel(x_ref, y_ref, part_ref, send_sem, recv_sem, back_send, back_recv):
    groups = y_ref.shape[0]
    me = lax.axis_index("grp")
    lane = lax.axis_index("seq")
    mesh_ids = pl.DeviceIdType.MESH
    barrier = pltpu.get_barrier_semaphore()
    for step in range(1, groups):
        pl.semaphore_signal(
            barrier, inc=1, device_id=(lax.rem(me + step, groups), lane), device_id_type=mesh_ids
        )
    pl.semaphore_wait(barrier, groups - 1)
    copies = []
    for step in range(1, groups):
        target = lax.rem(me + step, groups)
        copy = pltpu.make_async_remote_copy(
            src_ref=x_ref.at[target],
            dst_ref=part_ref.at[me],
            send_sem=send_sem.at[step],
            recv_sem=recv_sem.at[step],
            device_id=(target, lane),
            device_id_type=mesh_ids,
        )
        copy.start()
        copies.append(copy)
    part_ref[me] = x_ref[me]
    for copy in copies:
        copy.wait()
    y_ref[me] = jnp.sum(part_ref[...].astype(jnp.float32), axis=0).astype(y_ref.dtype)
    copies = []
    for step in range(1, groups):
        target = lax.rem(me + step, groups)
        copy = pltpu.make_async_remote_copy(
            src_ref=y_ref.at[me],
            dst_ref=y_ref.at[me],
            send_sem=back_send.at[step],
            recv_sem=back_recv.at[step],
            device_id=(target, lane),
            device_id_type=mesh_ids,
        )
        copy.start()
        copies.append(copy)
    for copy in copies:
        copy.wait()


def grp_reduce(x, groups, collective):
    vmem = pl.BlockSpec(memory_space=pltpu.VMEM)
    sems = pltpu.SemaphoreType.DMA((groups,))
    return pl.pallas_call(
        reduce_kernel,
        out_shape=jax.ShapeDtypeStruct(x.shape, x.dtype),
        in_specs=[vmem],
        out_specs=vmem,
        scratch_shapes=[pltpu.VMEM(x.shape, x.dtype), sems, sems, sems, sems],
        compiler_params=pltpu.CompilerParams(collective_id=collective, has_side_effects=True),
    )(x)


def combine_kernel(
    acc_in, stats_in, out_ref, stats_out, acc_part, stats_part,
    send_acc, recv_acc, send_stats, recv_stats, back_send, back_recv, stat_send, stat_recv,
):
    groups, chunk_rows, head_width = out_ref.shape
    me = lax.axis_index("grp")
    lane = lax.axis_index("seq")
    mesh_ids = pl.DeviceIdType.MESH
    barrier = pltpu.get_barrier_semaphore()
    for step in range(1, groups):
        pl.semaphore_signal(
            barrier, inc=1, device_id=(lax.rem(me + step, groups), lane), device_id_type=mesh_ids
        )
    pl.semaphore_wait(barrier, groups - 1)
    copies = []
    for step in range(1, groups):
        target = lax.rem(me + step, groups)
        for source, landing, sent, got in (
            (acc_in, acc_part, send_acc, recv_acc),
            (stats_in, stats_part, send_stats, recv_stats),
        ):
            copy = pltpu.make_async_remote_copy(
                src_ref=source.at[target],
                dst_ref=landing.at[me],
                send_sem=sent.at[step],
                recv_sem=got.at[step],
                device_id=(target, lane),
                device_id_type=mesh_ids,
            )
            copy.start()
            copies.append(copy)
    acc_part[me] = acc_in[me]
    stats_part[me] = stats_in[me]
    for copy in copies:
        copy.wait()
    columns = jnp.transpose(stats_part[...].reshape(groups * 8, 128))
    maxima = [columns[:chunk_rows, 8 * g : 8 * g + 1] for g in range(groups)]
    totals = [columns[chunk_rows:, 8 * g : 8 * g + 1] for g in range(groups)]
    top = maxima[0]
    for g in range(1, groups):
        top = jnp.maximum(top, maxima[g])
    row_total = jnp.zeros_like(top)
    row_accum = jnp.zeros((chunk_rows, head_width), jnp.float32)
    for g in range(groups):
        shrink = jnp.exp(maxima[g] - top)
        row_total = row_total + totals[g] * shrink
        row_accum = row_accum + acc_part[g].astype(jnp.float32) * shrink
    out_ref[me] = (row_accum / row_total).astype(out_ref.dtype)
    spread = jnp.concatenate(
        [jnp.broadcast_to(top, (chunk_rows, 128)), jnp.broadcast_to(row_total, (chunk_rows, 128))], axis=0
    )
    stats_out[me] = jnp.transpose(spread)[:8, :]
    copies = []
    for step in range(1, groups):
        target = lax.rem(me + step, groups)
        for source, sent, got in ((out_ref, back_send, back_recv), (stats_out, stat_send, stat_recv)):
            copy = pltpu.make_async_remote_copy(
                src_ref=source.at[me],
                dst_ref=source.at[me],
                send_sem=sent.at[step],
                recv_sem=got.at[step],
                device_id=(target, lane),
                device_id_type=mesh_ids,
            )
            copy.start()
            copies.append(copy)
    for copy in copies:
        copy.wait()


def grp_combine(accum, stats, collective):
    groups = accum.shape[0]
    vmem = pl.BlockSpec(memory_space=pltpu.VMEM)
    sems = pltpu.SemaphoreType.DMA((groups,))
    return pl.pallas_call(
        combine_kernel,
        out_shape=(
            jax.ShapeDtypeStruct(accum.shape, accum.dtype),
            jax.ShapeDtypeStruct(stats.shape, stats.dtype),
        ),
        in_specs=[vmem, vmem],
        out_specs=(vmem, vmem),
        scratch_shapes=[pltpu.VMEM(accum.shape, accum.dtype), pltpu.VMEM(stats.shape, stats.dtype)]
        + [sems] * 8,
        compiler_params=pltpu.CompilerParams(collective_id=collective, has_side_effects=True),
    )(accum, stats)


def back_kernel(
    dq_in, dk_in, dv_in, dq_out, recv_k, recv_v, part_ref,
    send_sem, recv_sem, back_send, back_recv, kv_send, kv_recv,
):
    groups = dq_out.shape[0]
    sources, block, head_width = recv_k.shape
    me = lax.axis_index("grp")
    lane = lax.axis_index("seq")
    mesh_ids = pl.DeviceIdType.MESH
    barrier = pltpu.get_barrier_semaphore()
    for step in range(1, groups):
        pl.semaphore_signal(
            barrier, inc=1, device_id=(lax.rem(me + step, groups), lane), device_id_type=mesh_ids
        )
    for step in range(1, sources):
        pl.semaphore_signal(
            barrier, inc=1, device_id=(me, lax.rem(lane + step, sources)), device_id_type=mesh_ids
        )
    pl.semaphore_wait(barrier, groups - 1 + sources - 1)
    returns = []
    for step in range(1, sources):
        target = lax.rem(lane + step, sources)
        rows = pl.ds(pl.multiple_of(target * block, block), block)
        for index, (source, landing) in enumerate(((dk_in, recv_k), (dv_in, recv_v))):
            copy = pltpu.make_async_remote_copy(
                src_ref=source.at[rows],
                dst_ref=landing.at[lane],
                send_sem=kv_send.at[index, step],
                recv_sem=kv_recv.at[index, step],
                device_id=(me, target),
                device_id_type=mesh_ids,
            )
            copy.start()
            returns.append(copy)
    copies = []
    for step in range(1, groups):
        target = lax.rem(me + step, groups)
        copy = pltpu.make_async_remote_copy(
            src_ref=dq_in.at[target],
            dst_ref=part_ref.at[me],
            send_sem=send_sem.at[step],
            recv_sem=recv_sem.at[step],
            device_id=(target, lane),
            device_id_type=mesh_ids,
        )
        copy.start()
        copies.append(copy)
    own_rows = pl.ds(pl.multiple_of(lane * block, block), block)
    recv_k[lane] = dk_in[own_rows, :]
    recv_v[lane] = dv_in[own_rows, :]
    part_ref[me] = dq_in[me]
    for copy in copies:
        copy.wait()
    dq_out[me] = jnp.sum(part_ref[...].astype(jnp.float32), axis=0).astype(dq_out.dtype)
    copies = []
    for step in range(1, groups):
        target = lax.rem(me + step, groups)
        copy = pltpu.make_async_remote_copy(
            src_ref=dq_out.at[me],
            dst_ref=dq_out.at[me],
            send_sem=back_send.at[step],
            recv_sem=back_recv.at[step],
            device_id=(target, lane),
            device_id_type=mesh_ids,
        )
        copy.start()
        copies.append(copy)
    for copy in returns:
        copy.wait()
    for copy in copies:
        copy.wait()


def head_sum_kernel(recv_k, recv_v, gk_out, gv_out):
    head_width = recv_k.shape[2]
    for head in range(recv_k.shape[0] // 2):
        cols = pl.ds(head * head_width, head_width)
        for landing, out_ref in ((recv_k, gk_out), (recv_v, gv_out)):
            out_ref[:, cols] = (
                landing[2 * head].astype(jnp.float32) + landing[2 * head + 1].astype(jnp.float32)
            ).astype(out_ref.dtype)


def back_exchange(query_grad, key_grad, value_grad, groups, sources, collective):
    head_width = query_grad.shape[-1]
    block = key_grad.shape[0] // sources
    vmem = pl.BlockSpec(memory_space=pltpu.VMEM)
    grad_shape = jax.ShapeDtypeStruct((block, sources // 2 * head_width), key_grad.dtype)
    landing = jax.ShapeDtypeStruct((sources, block, head_width), key_grad.dtype)
    sems = pltpu.SemaphoreType.DMA((groups,))
    grad_queries, recv_k, recv_v = pl.pallas_call(
        back_kernel,
        out_shape=(jax.ShapeDtypeStruct(query_grad.shape, query_grad.dtype), landing, landing),
        in_specs=[vmem, vmem, vmem],
        out_specs=(vmem, vmem, vmem),
        scratch_shapes=[
            pltpu.VMEM(query_grad.shape, query_grad.dtype),
            sems,
            sems,
            sems,
            sems,
            pltpu.SemaphoreType.DMA((2, sources)),
            pltpu.SemaphoreType.DMA((2, sources)),
        ],
        compiler_params=pltpu.CompilerParams(collective_id=collective, has_side_effects=True),
    )(query_grad, key_grad, value_grad)
    grad_keys, grad_values = pl.pallas_call(
        head_sum_kernel,
        out_shape=(grad_shape, grad_shape),
        in_specs=[vmem, vmem],
        out_specs=(vmem, vmem),
    )(recv_k, recv_v)
    return grad_queries, grad_keys, grad_values


def gather_kernel(k_ref, v_ref, k_out, v_out, send_sem, recv_sem, pair_send, pair_recv):
    sources, halves, half, head_width = k_out.shape
    me = lax.axis_index("seq")
    grp_here = lax.axis_index("grp")
    mine = lax.rem(me, 2)
    partner = me + 1 - 2 * mine
    head = me // 2
    mesh_ids = pl.DeviceIdType.MESH
    barrier = pltpu.get_barrier_semaphore()
    for step in range(1, sources):
        pl.semaphore_signal(
            barrier, inc=1, device_id=(grp_here, lax.rem(me + step, sources)), device_id_type=mesh_ids
        )
    pl.semaphore_wait(barrier, sources - 1)
    copies = []
    for step in range(1, sources):
        target = lax.rem(me + step, sources)
        rows = pl.ds(pl.multiple_of(lax.rem(target, 2) * half, half), half)
        cols = pl.ds(pl.multiple_of((target // 2) * head_width, head_width), head_width)
        for index, (source, landing) in enumerate(((k_ref, k_out), (v_ref, v_out))):
            copy = pltpu.make_async_remote_copy(
                src_ref=source.at[rows, cols],
                dst_ref=landing.at[me, lax.rem(target, 2)],
                send_sem=send_sem.at[index, step],
                recv_sem=recv_sem.at[index, step],
                device_id=(grp_here, target),
                device_id_type=mesh_ids,
            )
            copy.start()
            copies.append(copy)
    own_rows = pl.ds(pl.multiple_of(mine * half, half), half)
    own_cols = pl.ds(pl.multiple_of(head * head_width, head_width), head_width)
    k_out[me, mine] = k_ref[own_rows, own_cols]
    v_out[me, mine] = v_ref[own_rows, own_cols]
    for copy in copies:
        copy.wait()
    copies = []
    for index, landing in enumerate((k_out, v_out)):
        copy = pltpu.make_async_remote_copy(
            src_ref=landing.at[:, mine],
            dst_ref=landing.at[:, mine],
            send_sem=pair_send.at[index],
            recv_sem=pair_recv.at[index],
            device_id=(grp_here, partner),
            device_id_type=mesh_ids,
        )
        copy.start()
        copies.append(copy)
    for copy in copies:
        copy.wait()


def seq_gather(scene_keys, scene_values, sources, head_width, collective):
    half = scene_keys.shape[0] // QPARTS
    vmem = pl.BlockSpec(memory_space=pltpu.VMEM)
    out = jax.ShapeDtypeStruct((sources, QPARTS, half, head_width), scene_keys.dtype)
    return pl.pallas_call(
        gather_kernel,
        out_shape=(out, out),
        in_specs=[vmem, vmem],
        out_specs=(vmem, vmem),
        scratch_shapes=[
            pltpu.SemaphoreType.DMA((2, sources)),
            pltpu.SemaphoreType.DMA((2, sources)),
            pltpu.SemaphoreType.DMA((2,)),
            pltpu.SemaphoreType.DMA((2,)),
        ],
        compiler_params=pltpu.CompilerParams(collective_id=collective, has_side_effects=True),
    )(scene_keys, scene_values)


def scatter_rows(rows, parts, collective):
    return grp_exchange(
        rows.reshape(parts, rows.shape[0] // parts, rows.shape[1]), parts, False, collective
    )


def broadcast_rows(chunk, parts, collective):
    gathered = grp_exchange(chunk, parts, True, collective)
    return gathered.reshape(parts * chunk.shape[0], chunk.shape[1])


def per_device(queries, scene_keys, scene_values, grad_output, tile_list, tile_counts):
    items_here = queries.shape[0]
    head_width = queries.shape[2]
    query_rows = queries.shape[1]
    scene_here = scene_keys.shape[0]
    heads_total = scene_keys.shape[1] // head_width
    seq_devices = lax.axis_size("seq")
    groups = lax.axis_size("grp")
    chunk_rows = query_rows // groups
    group_keys = scene_here * seq_devices
    copies = max(1, QPARTS // items_here)
    heads_here = max(1, items_here // QPARTS)
    softmax_scale = head_width ** (-0.5)
    half_keys = scene_here // QPARTS
    key_halves, value_halves = seq_gather(scene_keys, scene_values, seq_devices, head_width, 4)
    key_group = key_halves.reshape(group_keys, 1, head_width)
    value_group = value_halves.reshape(group_keys, 1, head_width)
    part_accum, stats = forward_item(
        queries[0],
        key_group[:, 0, :],
        value_group[:, 0, :],
        tile_list[0, 0],
        tile_counts[0, 0],
        softmax_scale,
        groups,
    )
    out_rows, out_stats = grp_combine(part_accum, stats, 0)
    attended = out_rows.reshape(1, query_rows, head_width)
    query_grad, key_grad, value_grad = backward_item(
        queries[0],
        key_group[:, 0, :],
        value_group[:, 0, :],
        grad_output[0],
        attended[0],
        out_stats,
        tile_list[0, 0],
        tile_counts[0, 0],
        softmax_scale,
    )
    grad_queries, grad_keys, grad_values = back_exchange(
        query_grad.reshape(groups, chunk_rows, head_width), key_grad, value_grad, groups, seq_devices, 2
    )
    grad_queries = grad_queries.reshape(1, query_rows, head_width)
    return (attended, grad_queries, grad_keys, grad_values)


def solution(mesh):
    in_specs = (
        P("seq", None, None),
        P(("grp", "seq"), None),
        P(("grp", "seq"), None),
        P("seq", None, None),
        P("grp", "seq", None, None),
        P("grp", "seq"),
    )
    out_specs = (
        P("seq", None, None),
        P("seq", None, None),
        P(("grp", "seq"), None),
        P(("grp", "seq"), None),
    )
    return jax.shard_map(
        per_device, mesh=mesh, in_specs=in_specs, out_specs=out_specs, check_vma=False
    )
```

```python
import jax
import jax.numpy as jnp
from jax import lax
from jax.experimental import pallas as pl
from jax.experimental.pallas import tpu as pltpu
from jax.sharding import PartitionSpec as P

QPARTS = 2
QBLK = 512
KBLK = 512


NEG_START = -1e30


LIST_SLOTS = 9


def tile_starts(list_ref, position):
    query_block = jnp.clip(list_ref[position, 0], 0, QPARTS - 1)
    key_block = jnp.clip(list_ref[position, 1], 0, 7)
    return (
        pl.multiple_of(query_block * QBLK, QBLK),
        pl.multiple_of(key_block * KBLK, KBLK),
    )


def forward_kernel(
    softmax_scale, list_ref, count_ref, q_ref, k_ref, v_ref, acc_out, stats_out, max_ref, total_ref, accum_ref
):
    max_ref[...] = jnp.full(max_ref.shape, NEG_START, jnp.float32)
    total_ref[...] = jnp.zeros(total_ref.shape, jnp.float32)
    accum_ref[...] = jnp.zeros(accum_ref.shape, jnp.float32)
    live_tiles = jnp.clip(count_ref[0], 0, LIST_SLOTS)

    def visit(position, carry):
        query_start, key_start = tile_starts(list_ref, position)
        rows = pl.ds(query_start, QBLK)
        keys = pl.ds(key_start, KBLK)
        scores = (
            lax.dot_general(
                q_ref[rows, :], k_ref[keys, :], (((1,), (1,)), ((), ())),
                preferred_element_type=jnp.float32,
            )
            * softmax_scale
        )
        old_max = max_ref[rows, :]
        new_max = jnp.maximum(old_max, jnp.max(scores, axis=1, keepdims=True))
        new_max = new_max.astype(jnp.bfloat16).astype(jnp.float32)
        weights = jnp.exp(scores - new_max[:, :1])
        shrink = jnp.exp(old_max - new_max)
        total_ref[rows, :] = total_ref[rows, :] * shrink + jnp.sum(weights, axis=1, keepdims=True)
        accum_ref[rows, :] = accum_ref[rows, :] * shrink[:, :1] + jnp.dot(
            weights.astype(jnp.bfloat16), v_ref[keys, :], preferred_element_type=jnp.float32
        )
        max_ref[rows, :] = new_max
        return carry

    lax.fori_loop(0, live_tiles, visit, 0)
    groups, chunk_rows = acc_out.shape[0], acc_out.shape[1]
    for g in range(groups):
        rows = pl.ds(g * chunk_rows, chunk_rows)
        acc_out[g] = accum_ref[rows, :].astype(acc_out.dtype)
        stacked = jnp.concatenate([max_ref[rows, :], total_ref[rows, :]], axis=0)
        stats_out[g] = jnp.transpose(stacked)[:8, :]


def forward_item(query_item, key_head, value_head, listing, live_tiles, softmax_scale, groups):
    query_rows, head_width = query_item.shape
    chunk_rows = query_rows // groups
    smem = pl.BlockSpec(memory_space=pltpu.SMEM)
    vmem = pl.BlockSpec(memory_space=pltpu.VMEM)
    rows_f32 = pltpu.VMEM((query_rows, head_width), jnp.float32)
    return pl.pallas_call(
        lambda *refs: forward_kernel(softmax_scale, *refs),
        out_shape=(
            jax.ShapeDtypeStruct((groups, chunk_rows, head_width), jnp.bfloat16),
            jax.ShapeDtypeStruct((groups, 8, 2 * chunk_rows), jnp.float32),
        ),
        in_specs=[smem, smem, vmem, vmem, vmem],
        out_specs=(vmem, vmem),
        scratch_shapes=[rows_f32, rows_f32, rows_f32],
    )(listing, live_tiles.reshape(1), query_item, key_head, value_head)


def backward_kernel(
    softmax_scale, list_ref, count_ref, q_ref, k_ref, v_ref, do_ref, att_ref, stats_ref,
    dq_ref, dk_ref, dv_ref, dq_acc, dk_acc, dv_acc, log_ref, delta_ref,
):
    groups = stats_ref.shape[0]
    chunk_rows = stats_ref.shape[2] // 2
    for g in range(groups):
        rows = pl.ds(g * chunk_rows, chunk_rows)
        columns = jnp.transpose(jnp.broadcast_to(stats_ref[g][0:1, :], (2 * chunk_rows, 2 * chunk_rows)))
        log_ref[rows, :] = columns[:chunk_rows, 0:1] + jnp.log(columns[chunk_rows:, 0:1])
        delta_ref[rows, :] = jnp.sum(
            att_ref[rows, :].astype(jnp.float32) * do_ref[rows, :].astype(jnp.float32),
            axis=1,
            keepdims=True,
        )
    dq_acc[...] = jnp.zeros(dq_acc.shape, jnp.float32)
    dk_acc[...] = jnp.zeros(dk_acc.shape, jnp.float32)
    dv_acc[...] = jnp.zeros(dv_acc.shape, jnp.float32)
    live_tiles = jnp.clip(count_ref[0], 0, LIST_SLOTS)

    def visit(position, carry):
        query_start, key_start = tile_starts(list_ref, position)
        rows = pl.ds(query_start, QBLK)
        keys = pl.ds(key_start, KBLK)
        query_block = q_ref[rows, :]
        grad_block = do_ref[rows, :]
        key_block = k_ref[keys, :]
        value_block = v_ref[keys, :]
        scores = (
            lax.dot_general(
                query_block, key_block, (((1,), (1,)), ((), ())),
                preferred_element_type=jnp.float32,
            )
            * softmax_scale
        )
        probs = jnp.exp(scores - log_ref[rows, :])
        probs_half = probs.astype(jnp.bfloat16)
        dv_acc[keys, :] += lax.dot_general(
            probs_half, grad_block, (((0,), (0,)), ((), ())), preferred_element_type=jnp.float32
        )
        prob_grad = lax.dot_general(
            grad_block, value_block, (((1,), (1,)), ((), ())), preferred_element_type=jnp.float32
        )
        score_grad = (probs * (prob_grad - delta_ref[rows, :])).astype(jnp.bfloat16)
        dq_acc[rows, :] += (
            jnp.dot(score_grad, key_block, preferred_element_type=jnp.float32) * softmax_scale
        )
        dk_acc[keys, :] += (
            lax.dot_general(
                score_grad, query_block, (((0,), (0,)), ((), ())),
                preferred_element_type=jnp.float32,
            )
            * softmax_scale
        )
        return carry

    lax.fori_loop(0, live_tiles, visit, 0)
    dq_ref[...] = dq_acc[...].astype(dq_ref.dtype)
    dk_ref[...] = dk_acc[...].astype(dk_ref.dtype)
    dv_ref[...] = dv_acc[...].astype(dv_ref.dtype)


def backward_item(
    query_item, key_head, value_head, grad_item, attended, stats, listing, live_tiles, softmax_scale,
):
    query_rows, head_width = query_item.shape
    key_rows = key_head.shape[0]
    smem = pl.BlockSpec(memory_space=pltpu.SMEM)
    vmem = pl.BlockSpec(memory_space=pltpu.VMEM)
    return pl.pallas_call(
        lambda *refs: backward_kernel(softmax_scale, *refs),
        out_shape=(
            jax.ShapeDtypeStruct((query_rows, head_width), jnp.bfloat16),
            jax.ShapeDtypeStruct((key_rows, head_width), jnp.bfloat16),
            jax.ShapeDtypeStruct((key_rows, head_width), jnp.bfloat16),
        ),
        in_specs=[smem, smem] + [vmem] * 6,
        out_specs=(vmem, vmem, vmem),
        scratch_shapes=[
            pltpu.VMEM((query_rows, head_width), jnp.float32),
            pltpu.VMEM((key_rows, head_width), jnp.float32),
            pltpu.VMEM((key_rows, head_width), jnp.float32),
            pltpu.VMEM((query_rows, 1), jnp.float32),
            pltpu.VMEM((query_rows, 1), jnp.float32),
        ],
    )(
        listing,
        live_tiles.reshape(1),
        query_item,
        key_head,
        value_head,
        grad_item,
        attended,
        stats,
    )


def exchange_kernel(broadcast, x_ref, y_ref, send_sem, recv_sem):
    groups = y_ref.shape[0]
    me = lax.axis_index("grp")
    lane = lax.axis_index("seq")
    mesh_ids = pl.DeviceIdType.MESH
    barrier = pltpu.get_barrier_semaphore()
    for step in range(1, groups):
        pl.semaphore_signal(
            barrier, inc=1, device_id=(lax.rem(me + step, groups), lane), device_id_type=mesh_ids
        )
    pl.semaphore_wait(barrier, groups - 1)
    copies = []
    for step in range(1, groups):
        target = lax.rem(me + step, groups)
        copy = pltpu.make_async_remote_copy(
            src_ref=x_ref if broadcast else x_ref.at[target],
            dst_ref=y_ref.at[me],
            send_sem=send_sem.at[step],
            recv_sem=recv_sem.at[step],
            device_id=(target, lane),
            device_id_type=mesh_ids,
        )
        copy.start()
        copies.append(copy)
    y_ref[me] = x_ref[...] if broadcast else x_ref[me]
    for copy in copies:
        copy.wait()


def grp_exchange(x, groups, broadcast, collective):
    out_shape = (groups,) + (x.shape if broadcast else x.shape[1:])
    vmem = pl.BlockSpec(memory_space=pltpu.VMEM)
    return pl.pallas_call(
        lambda *refs: exchange_kernel(broadcast, *refs),
        out_shape=jax.ShapeDtypeStruct(out_shape, x.dtype),
        in_specs=[vmem],
        out_specs=vmem,
        scratch_shapes=[pltpu.SemaphoreType.DMA((groups,)), pltpu.SemaphoreType.DMA((groups,))],
        compiler_params=pltpu.CompilerParams(collective_id=collective, has_side_effects=True),
    )(x)


def reduce_kernel(x_ref, y_ref, part_ref, send_sem, recv_sem, back_send, back_recv):
    groups = y_ref.shape[0]
    me = lax.axis_index("grp")
    lane = lax.axis_index("seq")
    mesh_ids = pl.DeviceIdType.MESH
    barrier = pltpu.get_barrier_semaphore()
    for step in range(1, groups):
        pl.semaphore_signal(
            barrier, inc=1, device_id=(lax.rem(me + step, groups), lane), device_id_type=mesh_ids
        )
    pl.semaphore_wait(barrier, groups - 1)
    copies = []
    for step in range(1, groups):
        target = lax.rem(me + step, groups)
        copy = pltpu.make_async_remote_copy(
            src_ref=x_ref.at[target],
            dst_ref=part_ref.at[me],
            send_sem=send_sem.at[step],
            recv_sem=recv_sem.at[step],
            device_id=(target, lane),
            device_id_type=mesh_ids,
        )
        copy.start()
        copies.append(copy)
    part_ref[me] = x_ref[me]
    for copy in copies:
        copy.wait()
    y_ref[me] = jnp.sum(part_ref[...].astype(jnp.float32), axis=0).astype(y_ref.dtype)
    copies = []
    for step in range(1, groups):
        target = lax.rem(me + step, groups)
        copy = pltpu.make_async_remote_copy(
            src_ref=y_ref.at[me],
            dst_ref=y_ref.at[me],
            send_sem=back_send.at[step],
            recv_sem=back_recv.at[step],
            device_id=(target, lane),
            device_id_type=mesh_ids,
        )
        copy.start()
        copies.append(copy)
    for copy in copies:
        copy.wait()


def grp_reduce(x, groups, collective):
    vmem = pl.BlockSpec(memory_space=pltpu.VMEM)
    sems = pltpu.SemaphoreType.DMA((groups,))
    return pl.pallas_call(
        reduce_kernel,
        out_shape=jax.ShapeDtypeStruct(x.shape, x.dtype),
        in_specs=[vmem],
        out_specs=vmem,
        scratch_shapes=[pltpu.VMEM(x.shape, x.dtype), sems, sems, sems, sems],
        compiler_params=pltpu.CompilerParams(collective_id=collective, has_side_effects=True),
    )(x)


def combine_kernel(
    acc_in, stats_in, out_ref, stats_out, acc_part, stats_part,
    send_acc, recv_acc, send_stats, recv_stats, back_send, back_recv, stat_send, stat_recv,
):
    groups, chunk_rows, head_width = out_ref.shape
    me = lax.axis_index("grp")
    lane = lax.axis_index("seq")
    mesh_ids = pl.DeviceIdType.MESH
    barrier = pltpu.get_barrier_semaphore()
    for step in range(1, groups):
        pl.semaphore_signal(
            barrier, inc=1, device_id=(lax.rem(me + step, groups), lane), device_id_type=mesh_ids
        )
    pl.semaphore_wait(barrier, groups - 1)
    copies = []
    for step in range(1, groups):
        target = lax.rem(me + step, groups)
        for source, landing, sent, got in (
            (acc_in, acc_part, send_acc, recv_acc),
            (stats_in, stats_part, send_stats, recv_stats),
        ):
            copy = pltpu.make_async_remote_copy(
                src_ref=source.at[target],
                dst_ref=landing.at[me],
                send_sem=sent.at[step],
                recv_sem=got.at[step],
                device_id=(target, lane),
                device_id_type=mesh_ids,
            )
            copy.start()
            copies.append(copy)
    acc_part[me] = acc_in[me]
    stats_part[me] = stats_in[me]
    for copy in copies:
        copy.wait()
    columns = jnp.transpose(stats_part[...].reshape(groups * 8, 128))
    maxima = [columns[:chunk_rows, 8 * g : 8 * g + 1] for g in range(groups)]
    totals = [columns[chunk_rows:, 8 * g : 8 * g + 1] for g in range(groups)]
    top = maxima[0]
    for g in range(1, groups):
        top = jnp.maximum(top, maxima[g])
    row_total = jnp.zeros_like(top)
    row_accum = jnp.zeros((chunk_rows, head_width), jnp.float32)
    for g in range(groups):
        shrink = jnp.exp(maxima[g] - top)
        row_total = row_total + totals[g] * shrink
        row_accum = row_accum + acc_part[g].astype(jnp.float32) * shrink
    out_ref[me] = (row_accum / row_total).astype(out_ref.dtype)
    spread = jnp.concatenate(
        [jnp.broadcast_to(top, (chunk_rows, 128)), jnp.broadcast_to(row_total, (chunk_rows, 128))], axis=0
    )
    stats_out[me] = jnp.transpose(spread)[:8, :]
    copies = []
    for step in range(1, groups):
        target = lax.rem(me + step, groups)
        for source, sent, got in ((out_ref, back_send, back_recv), (stats_out, stat_send, stat_recv)):
            copy = pltpu.make_async_remote_copy(
                src_ref=source.at[me],
                dst_ref=source.at[me],
                send_sem=sent.at[step],
                recv_sem=got.at[step],
                device_id=(target, lane),
                device_id_type=mesh_ids,
            )
            copy.start()
            copies.append(copy)
    for copy in copies:
        copy.wait()


def grp_combine(accum, stats, collective):
    groups = accum.shape[0]
    vmem = pl.BlockSpec(memory_space=pltpu.VMEM)
    sems = pltpu.SemaphoreType.DMA((groups,))
    return pl.pallas_call(
        combine_kernel,
        out_shape=(
            jax.ShapeDtypeStruct(accum.shape, accum.dtype),
            jax.ShapeDtypeStruct(stats.shape, stats.dtype),
        ),
        in_specs=[vmem, vmem],
        out_specs=(vmem, vmem),
        scratch_shapes=[pltpu.VMEM(accum.shape, accum.dtype), pltpu.VMEM(stats.shape, stats.dtype)]
        + [sems] * 8,
        compiler_params=pltpu.CompilerParams(collective_id=collective, has_side_effects=True),
    )(accum, stats)


def back_kernel(
    dq_in, dk_in, dv_in, dq_out, gk_out, gv_out, part_ref, recv_k, recv_v,
    send_sem, recv_sem, back_send, back_recv, kv_send, kv_recv,
):
    groups = dq_out.shape[0]
    sources, block, head_width = recv_k.shape
    me = lax.axis_index("grp")
    lane = lax.axis_index("seq")
    mesh_ids = pl.DeviceIdType.MESH
    barrier = pltpu.get_barrier_semaphore()
    for step in range(1, groups):
        pl.semaphore_signal(
            barrier, inc=1, device_id=(lax.rem(me + step, groups), lane), device_id_type=mesh_ids
        )
    for step in range(1, sources):
        pl.semaphore_signal(
            barrier, inc=1, device_id=(me, lax.rem(lane + step, sources)), device_id_type=mesh_ids
        )
    pl.semaphore_wait(barrier, groups - 1 + sources - 1)
    returns = []
    for step in range(1, sources):
        target = lax.rem(lane + step, sources)
        rows = pl.ds(pl.multiple_of(target * block, block), block)
        for index, (source, landing) in enumerate(((dk_in, recv_k), (dv_in, recv_v))):
            copy = pltpu.make_async_remote_copy(
                src_ref=source.at[rows],
                dst_ref=landing.at[lane],
                send_sem=kv_send.at[index, step],
                recv_sem=kv_recv.at[index, step],
                device_id=(me, target),
                device_id_type=mesh_ids,
            )
            copy.start()
            returns.append(copy)
    copies = []
    for step in range(1, groups):
        target = lax.rem(me + step, groups)
        copy = pltpu.make_async_remote_copy(
            src_ref=dq_in.at[target],
            dst_ref=part_ref.at[me],
            send_sem=send_sem.at[step],
            recv_sem=recv_sem.at[step],
            device_id=(target, lane),
            device_id_type=mesh_ids,
        )
        copy.start()
        copies.append(copy)
    own_rows = pl.ds(pl.multiple_of(lane * block, block), block)
    recv_k[lane] = dk_in[own_rows, :]
    recv_v[lane] = dv_in[own_rows, :]
    part_ref[me] = dq_in[me]
    for copy in copies:
        copy.wait()
    dq_out[me] = jnp.sum(part_ref[...].astype(jnp.float32), axis=0).astype(dq_out.dtype)
    copies = []
    for step in range(1, groups):
        target = lax.rem(me + step, groups)
        copy = pltpu.make_async_remote_copy(
            src_ref=dq_out.at[me],
            dst_ref=dq_out.at[me],
            send_sem=back_send.at[step],
            recv_sem=back_recv.at[step],
            device_id=(target, lane),
            device_id_type=mesh_ids,
        )
        copy.start()
        copies.append(copy)
    for copy in returns:
        copy.wait()
    for head in range(sources // 2):
        cols = pl.ds(head * head_width, head_width)
        for landing, out_ref in ((recv_k, gk_out), (recv_v, gv_out)):
            out_ref[:, cols] = (
                landing[2 * head].astype(jnp.float32) + landing[2 * head + 1].astype(jnp.float32)
            ).astype(out_ref.dtype)
    for copy in copies:
        copy.wait()


def back_exchange(query_grad, key_grad, value_grad, groups, sources, collective):
    head_width = query_grad.shape[-1]
    block = key_grad.shape[0] // sources
    vmem = pl.BlockSpec(memory_space=pltpu.VMEM)
    grad_shape = jax.ShapeDtypeStruct((block, sources // 2 * head_width), key_grad.dtype)
    sems = pltpu.SemaphoreType.DMA((groups,))
    return pl.pallas_call(
        back_kernel,
        out_shape=(jax.ShapeDtypeStruct(query_grad.shape, query_grad.dtype), grad_shape, grad_shape),
        in_specs=[vmem, vmem, vmem],
        out_specs=(vmem, vmem, vmem),
        scratch_shapes=[
            pltpu.VMEM(query_grad.shape, query_grad.dtype),
            pltpu.VMEM((sources, block, head_width), key_grad.dtype),
            pltpu.VMEM((sources, block, head_width), key_grad.dtype),
            sems,
            sems,
            sems,
            sems,
            pltpu.SemaphoreType.DMA((2, sources)),
            pltpu.SemaphoreType.DMA((2, sources)),
        ],
        compiler_params=pltpu.CompilerParams(collective_id=collective, has_side_effects=True),
    )(query_grad, key_grad, value_grad)


def gather_kernel(k_ref, v_ref, k_out, v_out, send_sem, recv_sem, pair_send, pair_recv):
    sources, halves, half, head_width = k_out.shape
    me = lax.axis_index("seq")
    grp_here = lax.axis_index("grp")
    mine = lax.rem(me, 2)
    partner = me + 1 - 2 * mine
    head = me // 2
    mesh_ids = pl.DeviceIdType.MESH
    barrier = pltpu.get_barrier_semaphore()
    for step in range(1, sources):
        pl.semaphore_signal(
            barrier, inc=1, device_id=(grp_here, lax.rem(me + step, sources)), device_id_type=mesh_ids
        )
    pl.semaphore_wait(barrier, sources - 1)
    copies = []
    for step in range(1, sources):
        target = lax.rem(me + step, sources)
        rows = pl.ds(pl.multiple_of(lax.rem(target, 2) * half, half), half)
        cols = pl.ds(pl.multiple_of((target // 2) * head_width, head_width), head_width)
        for index, (source, landing) in enumerate(((k_ref, k_out), (v_ref, v_out))):
            copy = pltpu.make_async_remote_copy(
                src_ref=source.at[rows, cols],
                dst_ref=landing.at[me, lax.rem(target, 2)],
                send_sem=send_sem.at[index, step],
                recv_sem=recv_sem.at[index, step],
                device_id=(grp_here, target),
                device_id_type=mesh_ids,
            )
            copy.start()
            copies.append(copy)
    own_rows = pl.ds(pl.multiple_of(mine * half, half), half)
    own_cols = pl.ds(pl.multiple_of(head * head_width, head_width), head_width)
    k_out[me, mine] = k_ref[own_rows, own_cols]
    v_out[me, mine] = v_ref[own_rows, own_cols]
    forwards = []

    def forward(step, block, sources_of):
        for index, (landing, source) in enumerate(zip((k_out, v_out), sources_of)):
            copy = pltpu.make_async_remote_copy(
                src_ref=source,
                dst_ref=landing.at[block, mine],
                send_sem=pair_send.at[index, step],
                recv_sem=pair_recv.at[index, step],
                device_id=(grp_here, partner),
                device_id_type=mesh_ids,
            )
            copy.start()
            forwards.append(copy)

    forward(0, me, (k_ref.at[own_rows, own_cols], v_ref.at[own_rows, own_cols]))
    for step in range(1, sources):
        for copy in copies[2 * (step - 1) : 2 * step]:
            copy.wait()
        block = lax.rem(me + sources - step, sources)
        forward(step, block, (k_out.at[block, mine], v_out.at[block, mine]))
    for copy in forwards:
        copy.wait()


def seq_gather(scene_keys, scene_values, sources, head_width, collective):
    half = scene_keys.shape[0] // QPARTS
    vmem = pl.BlockSpec(memory_space=pltpu.VMEM)
    out = jax.ShapeDtypeStruct((sources, QPARTS, half, head_width), scene_keys.dtype)
    return pl.pallas_call(
        gather_kernel,
        out_shape=(out, out),
        in_specs=[vmem, vmem],
        out_specs=(vmem, vmem),
        scratch_shapes=[
            pltpu.SemaphoreType.DMA((2, sources)),
            pltpu.SemaphoreType.DMA((2, sources)),
            pltpu.SemaphoreType.DMA((2, sources)),
            pltpu.SemaphoreType.DMA((2, sources)),
        ],
        compiler_params=pltpu.CompilerParams(collective_id=collective, has_side_effects=True),
    )(scene_keys, scene_values)


def scatter_rows(rows, parts, collective):
    return grp_exchange(
        rows.reshape(parts, rows.shape[0] // parts, rows.shape[1]), parts, False, collective
    )


def broadcast_rows(chunk, parts, collective):
    gathered = grp_exchange(chunk, parts, True, collective)
    return gathered.reshape(parts * chunk.shape[0], chunk.shape[1])


def per_device(queries, scene_keys, scene_values, grad_output, tile_list, tile_counts):
    items_here = queries.shape[0]
    head_width = queries.shape[2]
    query_rows = queries.shape[1]
    scene_here = scene_keys.shape[0]
    heads_total = scene_keys.shape[1] // head_width
    seq_devices = lax.axis_size("seq")
    groups = lax.axis_size("grp")
    chunk_rows = query_rows // groups
    group_keys = scene_here * seq_devices
    copies = max(1, QPARTS // items_here)
    heads_here = max(1, items_here // QPARTS)
    softmax_scale = head_width ** (-0.5)
    half_keys = scene_here // QPARTS
    key_halves, value_halves = seq_gather(scene_keys, scene_values, seq_devices, head_width, 4)
    key_group = key_halves.reshape(group_keys, 1, head_width)
    value_group = value_halves.reshape(group_keys, 1, head_width)
    part_accum, stats = forward_item(
        queries[0],
        key_group[:, 0, :],
        value_group[:, 0, :],
        tile_list[0, 0],
        tile_counts[0, 0],
        softmax_scale,
        groups,
    )
    out_rows, out_stats = grp_combine(part_accum, stats, 0)
    attended = out_rows.reshape(1, query_rows, head_width)
    query_grad, key_grad, value_grad = backward_item(
        queries[0],
        key_group[:, 0, :],
        value_group[:, 0, :],
        grad_output[0],
        attended[0],
        out_stats,
        tile_list[0, 0],
        tile_counts[0, 0],
        softmax_scale,
    )
    grad_queries, grad_keys, grad_values = back_exchange(
        query_grad.reshape(groups, chunk_rows, head_width), key_grad, value_grad, groups, seq_devices, 2
    )
    grad_queries = grad_queries.reshape(1, query_rows, head_width)
    return (attended, grad_queries, grad_keys, grad_values)


def solution(mesh):
    in_specs = (
        P("seq", None, None),
        P(("grp", "seq"), None),
        P(("grp", "seq"), None),
        P("seq", None, None),
        P("grp", "seq", None, None),
        P("grp", "seq"),
    )
    out_specs = (
        P("seq", None, None),
        P("seq", None, None),
        P(("grp", "seq"), None),
        P(("grp", "seq"), None),
    )
    return jax.shard_map(
        per_device, mesh=mesh, in_specs=in_specs, out_specs=out_specs, check_vma=False
    )
```

```python
import jax
import jax.numpy as jnp
from jax import lax
from jax.experimental import pallas as pl
from jax.experimental.pallas import tpu as pltpu
from jax.sharding import PartitionSpec as P

QPARTS = 2
QBLK = 512
KBLK = 512


NEG_START = -1e30


LIST_SLOTS = 9


def tile_starts(list_ref, position):
    query_block = jnp.clip(list_ref[position, 0], 0, QPARTS - 1)
    key_block = jnp.clip(list_ref[position, 1], 0, 7)
    return (
        pl.multiple_of(query_block * QBLK, QBLK),
        pl.multiple_of(key_block * KBLK, KBLK),
    )


def forward_kernel(
    softmax_scale, list_ref, count_ref, q_ref, k_ref, v_ref, acc_out, stats_out, max_ref, total_ref, accum_ref
):
    max_ref[...] = jnp.full(max_ref.shape, NEG_START, jnp.float32)
    total_ref[...] = jnp.zeros(total_ref.shape, jnp.float32)
    accum_ref[...] = jnp.zeros(accum_ref.shape, jnp.float32)
    live_tiles = jnp.clip(count_ref[0], 0, LIST_SLOTS)

    def visit(position, carry):
        query_start, key_start = tile_starts(list_ref, position)
        rows = pl.ds(query_start, QBLK)
        keys = pl.ds(key_start, KBLK)
        scores = (
            lax.dot_general(
                q_ref[rows, :], k_ref[keys, :], (((1,), (1,)), ((), ())),
                preferred_element_type=jnp.float32,
            )
            * softmax_scale
        )
        old_max = max_ref[rows, :]
        new_max = jnp.maximum(old_max, jnp.max(scores, axis=1, keepdims=True))
        new_max = new_max.astype(jnp.bfloat16).astype(jnp.float32)
        weights = jnp.exp(scores - new_max[:, :1])
        shrink = jnp.exp(old_max - new_max)
        total_ref[rows, :] = total_ref[rows, :] * shrink + jnp.sum(weights, axis=1, keepdims=True)
        accum_ref[rows, :] = accum_ref[rows, :] * shrink[:, :1] + jnp.dot(
            weights.astype(jnp.bfloat16), v_ref[keys, :], preferred_element_type=jnp.float32
        )
        max_ref[rows, :] = new_max
        return carry

    lax.fori_loop(0, live_tiles, visit, 0)
    groups, chunk_rows = acc_out.shape[0], acc_out.shape[1]
    for g in range(groups):
        rows = pl.ds(g * chunk_rows, chunk_rows)
        acc_out[g] = accum_ref[rows, :].astype(acc_out.dtype)
        stacked = jnp.concatenate([max_ref[rows, :], total_ref[rows, :]], axis=0)
        stats_out[g] = jnp.transpose(stacked)[:8, :]


def forward_item(query_item, key_head, value_head, listing, live_tiles, softmax_scale, groups):
    query_rows, head_width = query_item.shape
    chunk_rows = query_rows // groups
    smem = pl.BlockSpec(memory_space=pltpu.SMEM)
    vmem = pl.BlockSpec(memory_space=pltpu.VMEM)
    rows_f32 = pltpu.VMEM((query_rows, head_width), jnp.float32)
    return pl.pallas_call(
        lambda *refs: forward_kernel(softmax_scale, *refs),
        out_shape=(
            jax.ShapeDtypeStruct((groups, chunk_rows, head_width), jnp.bfloat16),
            jax.ShapeDtypeStruct((groups, 8, 2 * chunk_rows), jnp.float32),
        ),
        in_specs=[smem, smem, vmem, vmem, vmem],
        out_specs=(vmem, vmem),
        scratch_shapes=[rows_f32, rows_f32, rows_f32],
    )(listing, live_tiles.reshape(1), query_item, key_head, value_head)


def backward_kernel(
    softmax_scale, list_ref, count_ref, q_ref, k_ref, v_ref, do_ref, att_ref, stats_ref,
    dq_ref, dk_ref, dv_ref, dq_acc, dk_acc, dv_acc, log_ref, delta_ref,
):
    groups = stats_ref.shape[0]
    chunk_rows = stats_ref.shape[2] // 2
    for g in range(groups):
        rows = pl.ds(g * chunk_rows, chunk_rows)
        columns = jnp.transpose(jnp.broadcast_to(stats_ref[g][0:1, :], (2 * chunk_rows, 2 * chunk_rows)))
        log_ref[rows, :] = columns[:chunk_rows, 0:1] + jnp.log(columns[chunk_rows:, 0:1])
        delta_ref[rows, :] = jnp.sum(
            att_ref[rows, :].astype(jnp.float32) * do_ref[rows, :].astype(jnp.float32),
            axis=1,
            keepdims=True,
        )
    dq_acc[...] = jnp.zeros(dq_acc.shape, jnp.float32)
    dk_acc[...] = jnp.zeros(dk_acc.shape, jnp.float32)
    dv_acc[...] = jnp.zeros(dv_acc.shape, jnp.float32)
    live_tiles = jnp.clip(count_ref[0], 0, LIST_SLOTS)

    def visit(position, carry):
        query_start, key_start = tile_starts(list_ref, position)
        rows = pl.ds(query_start, QBLK)
        keys = pl.ds(key_start, KBLK)
        query_block = q_ref[rows, :]
        grad_block = do_ref[rows, :]
        key_block = k_ref[keys, :]
        value_block = v_ref[keys, :]
        scores = (
            lax.dot_general(
                query_block, key_block, (((1,), (1,)), ((), ())),
                preferred_element_type=jnp.float32,
            )
            * softmax_scale
        )
        probs = jnp.exp(scores - log_ref[rows, :])
        probs_half = probs.astype(jnp.bfloat16)
        dv_acc[keys, :] += lax.dot_general(
            probs_half, grad_block, (((0,), (0,)), ((), ())), preferred_element_type=jnp.float32
        )
        prob_grad = lax.dot_general(
            grad_block, value_block, (((1,), (1,)), ((), ())), preferred_element_type=jnp.float32
        )
        score_grad = (probs * (prob_grad - delta_ref[rows, :])).astype(jnp.bfloat16)
        dq_acc[rows, :] += (
            jnp.dot(score_grad, key_block, preferred_element_type=jnp.float32) * softmax_scale
        )
        dk_acc[keys, :] += (
            lax.dot_general(
                score_grad, query_block, (((0,), (0,)), ((), ())),
                preferred_element_type=jnp.float32,
            )
            * softmax_scale
        )
        return carry

    lax.fori_loop(0, live_tiles, visit, 0)
    dq_ref[...] = dq_acc[...].astype(dq_ref.dtype)
    dk_ref[...] = dk_acc[...].astype(dk_ref.dtype)
    dv_ref[...] = dv_acc[...].astype(dv_ref.dtype)


def backward_item(
    query_item, key_head, value_head, grad_item, attended, stats, listing, live_tiles, softmax_scale,
):
    query_rows, head_width = query_item.shape
    key_rows = key_head.shape[0]
    smem = pl.BlockSpec(memory_space=pltpu.SMEM)
    vmem = pl.BlockSpec(memory_space=pltpu.VMEM)
    return pl.pallas_call(
        lambda *refs: backward_kernel(softmax_scale, *refs),
        out_shape=(
            jax.ShapeDtypeStruct((query_rows, head_width), jnp.bfloat16),
            jax.ShapeDtypeStruct((key_rows, head_width), jnp.bfloat16),
            jax.ShapeDtypeStruct((key_rows, head_width), jnp.bfloat16),
        ),
        in_specs=[smem, smem] + [vmem] * 6,
        out_specs=(vmem, vmem, vmem),
        scratch_shapes=[
            pltpu.VMEM((query_rows, head_width), jnp.float32),
            pltpu.VMEM((key_rows, head_width), jnp.float32),
            pltpu.VMEM((key_rows, head_width), jnp.float32),
            pltpu.VMEM((query_rows, 1), jnp.float32),
            pltpu.VMEM((query_rows, 1), jnp.float32),
        ],
    )(
        listing,
        live_tiles.reshape(1),
        query_item,
        key_head,
        value_head,
        grad_item,
        attended,
        stats,
    )


def exchange_kernel(broadcast, x_ref, y_ref, send_sem, recv_sem):
    groups = y_ref.shape[0]
    me = lax.axis_index("grp")
    lane = lax.axis_index("seq")
    mesh_ids = pl.DeviceIdType.MESH
    barrier = pltpu.get_barrier_semaphore()
    for step in range(1, groups):
        pl.semaphore_signal(
            barrier, inc=1, device_id=(lax.rem(me + step, groups), lane), device_id_type=mesh_ids
        )
    pl.semaphore_wait(barrier, groups - 1)
    copies = []
    for step in range(1, groups):
        target = lax.rem(me + step, groups)
        copy = pltpu.make_async_remote_copy(
            src_ref=x_ref if broadcast else x_ref.at[target],
            dst_ref=y_ref.at[me],
            send_sem=send_sem.at[step],
            recv_sem=recv_sem.at[step],
            device_id=(target, lane),
            device_id_type=mesh_ids,
        )
        copy.start()
        copies.append(copy)
    y_ref[me] = x_ref[...] if broadcast else x_ref[me]
    for copy in copies:
        copy.wait()


def grp_exchange(x, groups, broadcast, collective):
    out_shape = (groups,) + (x.shape if broadcast else x.shape[1:])
    vmem = pl.BlockSpec(memory_space=pltpu.VMEM)
    return pl.pallas_call(
        lambda *refs: exchange_kernel(broadcast, *refs),
        out_shape=jax.ShapeDtypeStruct(out_shape, x.dtype),
        in_specs=[vmem],
        out_specs=vmem,
        scratch_shapes=[pltpu.SemaphoreType.DMA((groups,)), pltpu.SemaphoreType.DMA((groups,))],
        compiler_params=pltpu.CompilerParams(collective_id=collective, has_side_effects=True),
    )(x)


def reduce_kernel(x_ref, y_ref, part_ref, send_sem, recv_sem, back_send, back_recv):
    groups = y_ref.shape[0]
    me = lax.axis_index("grp")
    lane = lax.axis_index("seq")
    mesh_ids = pl.DeviceIdType.MESH
    barrier = pltpu.get_barrier_semaphore()
    for step in range(1, groups):
        pl.semaphore_signal(
            barrier, inc=1, device_id=(lax.rem(me + step, groups), lane), device_id_type=mesh_ids
        )
    pl.semaphore_wait(barrier, groups - 1)
    copies = []
    for step in range(1, groups):
        target = lax.rem(me + step, groups)
        copy = pltpu.make_async_remote_copy(
            src_ref=x_ref.at[target],
            dst_ref=part_ref.at[me],
            send_sem=send_sem.at[step],
            recv_sem=recv_sem.at[step],
            device_id=(target, lane),
            device_id_type=mesh_ids,
        )
        copy.start()
        copies.append(copy)
    part_ref[me] = x_ref[me]
    for copy in copies:
        copy.wait()
    y_ref[me] = jnp.sum(part_ref[...].astype(jnp.float32), axis=0).astype(y_ref.dtype)
    copies = []
    for step in range(1, groups):
        target = lax.rem(me + step, groups)
        copy = pltpu.make_async_remote_copy(
            src_ref=y_ref.at[me],
            dst_ref=y_ref.at[me],
            send_sem=back_send.at[step],
            recv_sem=back_recv.at[step],
            device_id=(target, lane),
            device_id_type=mesh_ids,
        )
        copy.start()
        copies.append(copy)
    for copy in copies:
        copy.wait()


def grp_reduce(x, groups, collective):
    vmem = pl.BlockSpec(memory_space=pltpu.VMEM)
    sems = pltpu.SemaphoreType.DMA((groups,))
    return pl.pallas_call(
        reduce_kernel,
        out_shape=jax.ShapeDtypeStruct(x.shape, x.dtype),
        in_specs=[vmem],
        out_specs=vmem,
        scratch_shapes=[pltpu.VMEM(x.shape, x.dtype), sems, sems, sems, sems],
        compiler_params=pltpu.CompilerParams(collective_id=collective, has_side_effects=True),
    )(x)


def combine_kernel(
    acc_in, stats_in, out_ref, stats_out, acc_part, stats_part,
    send_acc, recv_acc, send_stats, recv_stats, back_send, back_recv, stat_send, stat_recv,
):
    groups, chunk_rows, head_width = out_ref.shape
    me = lax.axis_index("grp")
    lane = lax.axis_index("seq")
    mesh_ids = pl.DeviceIdType.MESH
    barrier = pltpu.get_barrier_semaphore()
    for step in range(1, groups):
        pl.semaphore_signal(
            barrier, inc=1, device_id=(lax.rem(me + step, groups), lane), device_id_type=mesh_ids
        )
    pl.semaphore_wait(barrier, groups - 1)
    copies = []
    for step in range(1, groups):
        target = lax.rem(me + step, groups)
        for source, landing, sent, got in (
            (acc_in, acc_part, send_acc, recv_acc),
            (stats_in, stats_part, send_stats, recv_stats),
        ):
            copy = pltpu.make_async_remote_copy(
                src_ref=source.at[target],
                dst_ref=landing.at[me],
                send_sem=sent.at[step],
                recv_sem=got.at[step],
                device_id=(target, lane),
                device_id_type=mesh_ids,
            )
            copy.start()
            copies.append(copy)
    acc_part[me] = acc_in[me]
    stats_part[me] = stats_in[me]
    for copy in copies:
        copy.wait()
    columns = jnp.transpose(stats_part[...].reshape(groups * 8, 128))
    maxima = [columns[:chunk_rows, 8 * g : 8 * g + 1] for g in range(groups)]
    totals = [columns[chunk_rows:, 8 * g : 8 * g + 1] for g in range(groups)]
    top = maxima[0]
    for g in range(1, groups):
        top = jnp.maximum(top, maxima[g])
    row_total = jnp.zeros_like(top)
    row_accum = jnp.zeros((chunk_rows, head_width), jnp.float32)
    for g in range(groups):
        shrink = jnp.exp(maxima[g] - top)
        row_total = row_total + totals[g] * shrink
        row_accum = row_accum + acc_part[g].astype(jnp.float32) * shrink
    out_ref[me] = (row_accum / row_total).astype(out_ref.dtype)
    spread = jnp.concatenate(
        [jnp.broadcast_to(top, (chunk_rows, 128)), jnp.broadcast_to(row_total, (chunk_rows, 128))], axis=0
    )
    stats_out[me] = jnp.transpose(spread)[:8, :]
    copies = []
    for step in range(1, groups):
        target = lax.rem(me + step, groups)
        for source, sent, got in ((out_ref, back_send, back_recv), (stats_out, stat_send, stat_recv)):
            copy = pltpu.make_async_remote_copy(
                src_ref=source.at[me],
                dst_ref=source.at[me],
                send_sem=sent.at[step],
                recv_sem=got.at[step],
                device_id=(target, lane),
                device_id_type=mesh_ids,
            )
            copy.start()
            copies.append(copy)
    for copy in copies:
        copy.wait()


def grp_combine(accum, stats, collective):
    groups = accum.shape[0]
    vmem = pl.BlockSpec(memory_space=pltpu.VMEM)
    sems = pltpu.SemaphoreType.DMA((groups,))
    return pl.pallas_call(
        combine_kernel,
        out_shape=(
            jax.ShapeDtypeStruct(accum.shape, accum.dtype),
            jax.ShapeDtypeStruct(stats.shape, stats.dtype),
        ),
        in_specs=[vmem, vmem],
        out_specs=(vmem, vmem),
        scratch_shapes=[pltpu.VMEM(accum.shape, accum.dtype), pltpu.VMEM(stats.shape, stats.dtype)]
        + [sems] * 8,
        compiler_params=pltpu.CompilerParams(collective_id=collective, has_side_effects=True),
    )(accum, stats)


def back_kernel(
    dq_in, dk_in, dv_in, dq_out, gk_out, gv_out, part_ref, recv_k, recv_v,
    send_sem, recv_sem, back_send, back_recv, kv_send, kv_recv,
):
    groups = dq_out.shape[0]
    sources, block, head_width = recv_k.shape
    me = lax.axis_index("grp")
    lane = lax.axis_index("seq")
    mesh_ids = pl.DeviceIdType.MESH
    barrier = pltpu.get_barrier_semaphore()
    for step in range(1, groups):
        pl.semaphore_signal(
            barrier, inc=1, device_id=(lax.rem(me + step, groups), lane), device_id_type=mesh_ids
        )
    for step in range(1, sources):
        pl.semaphore_signal(
            barrier, inc=1, device_id=(me, lax.rem(lane + step, sources)), device_id_type=mesh_ids
        )
    pl.semaphore_wait(barrier, groups - 1 + sources - 1)
    copies = []
    for step in range(1, groups):
        target = lax.rem(me + step, groups)
        copy = pltpu.make_async_remote_copy(
            src_ref=dq_in.at[target],
            dst_ref=part_ref.at[me],
            send_sem=send_sem.at[step],
            recv_sem=recv_sem.at[step],
            device_id=(target, lane),
            device_id_type=mesh_ids,
        )
        copy.start()
        copies.append(copy)
    returns = []
    for step in range(1, sources):
        target = lax.rem(lane + step, sources)
        rows = pl.ds(pl.multiple_of(target * block, block), block)
        for index, (source, landing) in enumerate(((dk_in, recv_k), (dv_in, recv_v))):
            copy = pltpu.make_async_remote_copy(
                src_ref=source.at[rows],
                dst_ref=landing.at[lane],
                send_sem=kv_send.at[index, step],
                recv_sem=kv_recv.at[index, step],
                device_id=(me, target),
                device_id_type=mesh_ids,
            )
            copy.start()
            returns.append(copy)
    own_rows = pl.ds(pl.multiple_of(lane * block, block), block)
    recv_k[lane] = dk_in[own_rows, :]
    recv_v[lane] = dv_in[own_rows, :]
    part_ref[me] = dq_in[me]
    for copy in copies:
        copy.wait()
    dq_out[me] = jnp.sum(part_ref[...].astype(jnp.float32), axis=0).astype(dq_out.dtype)
    copies = []
    for step in range(1, groups):
        target = lax.rem(me + step, groups)
        copy = pltpu.make_async_remote_copy(
            src_ref=dq_out.at[me],
            dst_ref=dq_out.at[me],
            send_sem=back_send.at[step],
            recv_sem=back_recv.at[step],
            device_id=(target, lane),
            device_id_type=mesh_ids,
        )
        copy.start()
        copies.append(copy)
    for copy in returns:
        copy.wait()
    for head in range(sources // 2):
        cols = pl.ds(head * head_width, head_width)
        for landing, out_ref in ((recv_k, gk_out), (recv_v, gv_out)):
            out_ref[:, cols] = (
                landing[2 * head].astype(jnp.float32) + landing[2 * head + 1].astype(jnp.float32)
            ).astype(out_ref.dtype)
    for copy in copies:
        copy.wait()


def back_exchange(query_grad, key_grad, value_grad, groups, sources, collective):
    head_width = query_grad.shape[-1]
    block = key_grad.shape[0] // sources
    vmem = pl.BlockSpec(memory_space=pltpu.VMEM)
    grad_shape = jax.ShapeDtypeStruct((block, sources // 2 * head_width), key_grad.dtype)
    sems = pltpu.SemaphoreType.DMA((groups,))
    return pl.pallas_call(
        back_kernel,
        out_shape=(jax.ShapeDtypeStruct(query_grad.shape, query_grad.dtype), grad_shape, grad_shape),
        in_specs=[vmem, vmem, vmem],
        out_specs=(vmem, vmem, vmem),
        scratch_shapes=[
            pltpu.VMEM(query_grad.shape, query_grad.dtype),
            pltpu.VMEM((sources, block, head_width), key_grad.dtype),
            pltpu.VMEM((sources, block, head_width), key_grad.dtype),
            sems,
            sems,
            sems,
            sems,
            pltpu.SemaphoreType.DMA((2, sources)),
            pltpu.SemaphoreType.DMA((2, sources)),
        ],
        compiler_params=pltpu.CompilerParams(collective_id=collective, has_side_effects=True),
    )(query_grad, key_grad, value_grad)


def gather_kernel(k_ref, v_ref, k_out, v_out, send_sem, recv_sem, pair_send, pair_recv):
    sources, halves, half, head_width = k_out.shape
    me = lax.axis_index("seq")
    grp_here = lax.axis_index("grp")
    mine = lax.rem(me, 2)
    partner = me + 1 - 2 * mine
    head = me // 2
    mesh_ids = pl.DeviceIdType.MESH
    barrier = pltpu.get_barrier_semaphore()
    for step in range(1, sources):
        pl.semaphore_signal(
            barrier, inc=1, device_id=(grp_here, lax.rem(me + step, sources)), device_id_type=mesh_ids
        )
    pl.semaphore_wait(barrier, sources - 1)
    copies = []
    for step in range(1, sources):
        target = lax.rem(me + step, sources)
        rows = pl.ds(pl.multiple_of(lax.rem(target, 2) * half, half), half)
        cols = pl.ds(pl.multiple_of((target // 2) * head_width, head_width), head_width)
        for index, (source, landing) in enumerate(((k_ref, k_out), (v_ref, v_out))):
            copy = pltpu.make_async_remote_copy(
                src_ref=source.at[rows, cols],
                dst_ref=landing.at[me, lax.rem(target, 2)],
                send_sem=send_sem.at[index, step],
                recv_sem=recv_sem.at[index, step],
                device_id=(grp_here, target),
                device_id_type=mesh_ids,
            )
            copy.start()
            copies.append(copy)
    own_rows = pl.ds(pl.multiple_of(mine * half, half), half)
    own_cols = pl.ds(pl.multiple_of(head * head_width, head_width), head_width)
    k_out[me, mine] = k_ref[own_rows, own_cols]
    v_out[me, mine] = v_ref[own_rows, own_cols]
    forwards = []

    def forward(step, block, sources_of):
        for index, (landing, source) in enumerate(zip((k_out, v_out), sources_of)):
            copy = pltpu.make_async_remote_copy(
                src_ref=source,
                dst_ref=landing.at[block, mine],
                send_sem=pair_send.at[index, step],
                recv_sem=pair_recv.at[index, step],
                device_id=(grp_here, partner),
                device_id_type=mesh_ids,
            )
            copy.start()
            forwards.append(copy)

    forward(0, me, (k_ref.at[own_rows, own_cols], v_ref.at[own_rows, own_cols]))
    for step in range(1, sources):
        for copy in copies[2 * (step - 1) : 2 * step]:
            copy.wait()
        block = lax.rem(me + sources - step, sources)
        forward(step, block, (k_out.at[block, mine], v_out.at[block, mine]))
    for copy in forwards:
        copy.wait()


def seq_gather(scene_keys, scene_values, sources, head_width, collective):
    half = scene_keys.shape[0] // QPARTS
    vmem = pl.BlockSpec(memory_space=pltpu.VMEM)
    out = jax.ShapeDtypeStruct((sources, QPARTS, half, head_width), scene_keys.dtype)
    return pl.pallas_call(
        gather_kernel,
        out_shape=(out, out),
        in_specs=[vmem, vmem],
        out_specs=(vmem, vmem),
        scratch_shapes=[
            pltpu.SemaphoreType.DMA((2, sources)),
            pltpu.SemaphoreType.DMA((2, sources)),
            pltpu.SemaphoreType.DMA((2, sources)),
            pltpu.SemaphoreType.DMA((2, sources)),
        ],
        compiler_params=pltpu.CompilerParams(collective_id=collective, has_side_effects=True),
    )(scene_keys, scene_values)


def scatter_rows(rows, parts, collective):
    return grp_exchange(
        rows.reshape(parts, rows.shape[0] // parts, rows.shape[1]), parts, False, collective
    )


def broadcast_rows(chunk, parts, collective):
    gathered = grp_exchange(chunk, parts, True, collective)
    return gathered.reshape(parts * chunk.shape[0], chunk.shape[1])


def per_device(queries, scene_keys, scene_values, grad_output, tile_list, tile_counts):
    items_here = queries.shape[0]
    head_width = queries.shape[2]
    query_rows = queries.shape[1]
    scene_here = scene_keys.shape[0]
    heads_total = scene_keys.shape[1] // head_width
    seq_devices = lax.axis_size("seq")
    groups = lax.axis_size("grp")
    chunk_rows = query_rows // groups
    group_keys = scene_here * seq_devices
    copies = max(1, QPARTS // items_here)
    heads_here = max(1, items_here // QPARTS)
    softmax_scale = head_width ** (-0.5)
    half_keys = scene_here // QPARTS
    key_halves, value_halves = seq_gather(scene_keys, scene_values, seq_devices, head_width, 4)
    key_group = key_halves.reshape(group_keys, 1, head_width)
    value_group = value_halves.reshape(group_keys, 1, head_width)
    part_accum, stats = forward_item(
        queries[0],
        key_group[:, 0, :],
        value_group[:, 0, :],
        tile_list[0, 0],
        tile_counts[0, 0],
        softmax_scale,
        groups,
    )
    out_rows, out_stats = grp_combine(part_accum, stats, 0)
    attended = out_rows.reshape(1, query_rows, head_width)
    query_grad, key_grad, value_grad = backward_item(
        queries[0],
        key_group[:, 0, :],
        value_group[:, 0, :],
        grad_output[0],
        attended[0],
        out_stats,
        tile_list[0, 0],
        tile_counts[0, 0],
        softmax_scale,
    )
    grad_queries, grad_keys, grad_values = back_exchange(
        query_grad.reshape(groups, chunk_rows, head_width), key_grad, value_grad, groups, seq_devices, 2
    )
    grad_queries = grad_queries.reshape(1, query_rows, head_width)
    return (attended, grad_queries, grad_keys, grad_values)


def solution(mesh):
    in_specs = (
        P("seq", None, None),
        P(("grp", "seq"), None),
        P(("grp", "seq"), None),
        P("seq", None, None),
        P("grp", "seq", None, None),
        P("grp", "seq"),
    )
    out_specs = (
        P("seq", None, None),
        P("seq", None, None),
        P(("grp", "seq"), None),
        P(("grp", "seq"), None),
    )
    return jax.shard_map(
        per_device, mesh=mesh, in_specs=in_specs, out_specs=out_specs, check_vma=False
    )
```

```python
import jax
import jax.numpy as jnp
from jax import lax
from jax.experimental import pallas as pl
from jax.experimental.pallas import tpu as pltpu
from jax.sharding import PartitionSpec as P

QPARTS = 2
QBLK = 512
KBLK = 512


NEG_START = -1e30


LIST_SLOTS = 9


def tile_starts(list_ref, position):
    query_block = jnp.clip(list_ref[position, 0], 0, QPARTS - 1)
    key_block = jnp.clip(list_ref[position, 1], 0, 7)
    return (
        pl.multiple_of(query_block * QBLK, QBLK),
        pl.multiple_of(key_block * KBLK, KBLK),
    )


def forward_kernel(
    softmax_scale, list_ref, count_ref, q_ref, k_ref, v_ref, acc_out, stats_out, max_ref, total_ref, accum_ref
):
    max_ref[...] = jnp.full(max_ref.shape, NEG_START, jnp.float32)
    total_ref[...] = jnp.zeros(total_ref.shape, jnp.float32)
    accum_ref[...] = jnp.zeros(accum_ref.shape, jnp.float32)
    live_tiles = jnp.clip(count_ref[0], 0, LIST_SLOTS)

    def visit(position, carry):
        query_start, key_start = tile_starts(list_ref, position)
        rows = pl.ds(query_start, QBLK)
        keys = pl.ds(key_start, KBLK)
        scores = (
            lax.dot_general(
                q_ref[rows, :], k_ref[keys, :], (((1,), (1,)), ((), ())),
                preferred_element_type=jnp.float32,
            )
            * softmax_scale
        )
        old_max = max_ref[rows, :]
        new_max = jnp.maximum(old_max, jnp.max(scores, axis=1, keepdims=True))
        new_max = new_max.astype(jnp.bfloat16).astype(jnp.float32)
        weights = jnp.exp(scores - new_max[:, :1])
        shrink = jnp.exp(old_max - new_max)
        total_ref[rows, :] = total_ref[rows, :] * shrink + jnp.sum(weights, axis=1, keepdims=True)
        accum_ref[rows, :] = accum_ref[rows, :] * shrink[:, :1] + jnp.dot(
            weights.astype(jnp.bfloat16), v_ref[keys, :], preferred_element_type=jnp.float32
        )
        max_ref[rows, :] = new_max
        return carry

    lax.fori_loop(0, live_tiles, visit, 0)
    groups, chunk_rows = acc_out.shape[0], acc_out.shape[1]
    for g in range(groups):
        rows = pl.ds(g * chunk_rows, chunk_rows)
        acc_out[g] = accum_ref[rows, :].astype(acc_out.dtype)
        stacked = jnp.concatenate([max_ref[rows, :], total_ref[rows, :]], axis=0)
        stats_out[g] = jnp.transpose(stacked)[:8, :]


def forward_item(query_item, key_head, value_head, listing, live_tiles, softmax_scale, groups):
    query_rows, head_width = query_item.shape
    chunk_rows = query_rows // groups
    smem = pl.BlockSpec(memory_space=pltpu.SMEM)
    vmem = pl.BlockSpec(memory_space=pltpu.VMEM)
    rows_f32 = pltpu.VMEM((query_rows, head_width), jnp.float32)
    return pl.pallas_call(
        lambda *refs: forward_kernel(softmax_scale, *refs),
        out_shape=(
            jax.ShapeDtypeStruct((groups, chunk_rows, head_width), jnp.bfloat16),
            jax.ShapeDtypeStruct((groups, 8, 2 * chunk_rows), jnp.float32),
        ),
        in_specs=[smem, smem, vmem, vmem, vmem],
        out_specs=(vmem, vmem),
        scratch_shapes=[rows_f32, rows_f32, rows_f32],
    )(listing, live_tiles.reshape(1), query_item, key_head, value_head)


def backward_kernel(
    softmax_scale, list_ref, count_ref, q_ref, k_ref, v_ref, do_ref, att_ref, stats_ref,
    dq_ref, dk_ref, dv_ref, dq_acc, dk_acc, dv_acc, log_ref, delta_ref,
):
    groups = stats_ref.shape[0]
    chunk_rows = stats_ref.shape[2] // 2
    for g in range(groups):
        rows = pl.ds(g * chunk_rows, chunk_rows)
        columns = jnp.transpose(jnp.broadcast_to(stats_ref[g][0:1, :], (2 * chunk_rows, 2 * chunk_rows)))
        log_ref[rows, :] = columns[:chunk_rows, 0:1] + jnp.log(columns[chunk_rows:, 0:1])
        delta_ref[rows, :] = jnp.sum(
            att_ref[rows, :].astype(jnp.float32) * do_ref[rows, :].astype(jnp.float32),
            axis=1,
            keepdims=True,
        )
    dq_acc[...] = jnp.zeros(dq_acc.shape, jnp.float32)
    dk_acc[...] = jnp.zeros(dk_acc.shape, jnp.float32)
    dv_acc[...] = jnp.zeros(dv_acc.shape, jnp.float32)
    live_tiles = jnp.clip(count_ref[0], 0, LIST_SLOTS)

    def visit(position, carry):
        query_start, key_start = tile_starts(list_ref, position)
        rows = pl.ds(query_start, QBLK)
        keys = pl.ds(key_start, KBLK)
        query_block = q_ref[rows, :]
        grad_block = do_ref[rows, :]
        key_block = k_ref[keys, :]
        value_block = v_ref[keys, :]
        scores = (
            lax.dot_general(
                query_block, key_block, (((1,), (1,)), ((), ())),
                preferred_element_type=jnp.float32,
            )
            * softmax_scale
        )
        probs = jnp.exp(scores - log_ref[rows, :])
        probs_half = probs.astype(jnp.bfloat16)
        dv_acc[keys, :] += lax.dot_general(
            probs_half, grad_block, (((0,), (0,)), ((), ())), preferred_element_type=jnp.float32
        )
        prob_grad = lax.dot_general(
            grad_block, value_block, (((1,), (1,)), ((), ())), preferred_element_type=jnp.float32
        )
        score_grad = (probs * (prob_grad - delta_ref[rows, :])).astype(jnp.bfloat16)
        dq_acc[rows, :] += (
            jnp.dot(score_grad, key_block, preferred_element_type=jnp.float32) * softmax_scale
        )
        dk_acc[keys, :] += (
            lax.dot_general(
                score_grad, query_block, (((0,), (0,)), ((), ())),
                preferred_element_type=jnp.float32,
            )
            * softmax_scale
        )
        return carry

    lax.fori_loop(0, live_tiles, visit, 0)
    dq_ref[...] = dq_acc[...].astype(dq_ref.dtype)
    dk_ref[...] = dk_acc[...].astype(dk_ref.dtype)
    dv_ref[...] = dv_acc[...].astype(dv_ref.dtype)


def backward_item(
    query_item, key_head, value_head, grad_item, attended, stats, listing, live_tiles, softmax_scale,
):
    query_rows, head_width = query_item.shape
    key_rows = key_head.shape[0]
    smem = pl.BlockSpec(memory_space=pltpu.SMEM)
    vmem = pl.BlockSpec(memory_space=pltpu.VMEM)
    return pl.pallas_call(
        lambda *refs: backward_kernel(softmax_scale, *refs),
        out_shape=(
            jax.ShapeDtypeStruct((query_rows, head_width), jnp.bfloat16),
            jax.ShapeDtypeStruct((key_rows, head_width), jnp.bfloat16),
            jax.ShapeDtypeStruct((key_rows, head_width), jnp.bfloat16),
        ),
        in_specs=[smem, smem] + [vmem] * 6,
        out_specs=(vmem, vmem, vmem),
        scratch_shapes=[
            pltpu.VMEM((query_rows, head_width), jnp.float32),
            pltpu.VMEM((key_rows, head_width), jnp.float32),
            pltpu.VMEM((key_rows, head_width), jnp.float32),
            pltpu.VMEM((query_rows, 1), jnp.float32),
            pltpu.VMEM((query_rows, 1), jnp.float32),
        ],
    )(
        listing,
        live_tiles.reshape(1),
        query_item,
        key_head,
        value_head,
        grad_item,
        attended,
        stats,
    )


def exchange_kernel(broadcast, x_ref, y_ref, send_sem, recv_sem):
    groups = y_ref.shape[0]
    me = lax.axis_index("grp")
    lane = lax.axis_index("seq")
    mesh_ids = pl.DeviceIdType.MESH
    barrier = pltpu.get_barrier_semaphore()
    for step in range(1, groups):
        pl.semaphore_signal(
            barrier, inc=1, device_id=(lax.rem(me + step, groups), lane), device_id_type=mesh_ids
        )
    pl.semaphore_wait(barrier, groups - 1)
    copies = []
    for step in range(1, groups):
        target = lax.rem(me + step, groups)
        copy = pltpu.make_async_remote_copy(
            src_ref=x_ref if broadcast else x_ref.at[target],
            dst_ref=y_ref.at[me],
            send_sem=send_sem.at[step],
            recv_sem=recv_sem.at[step],
            device_id=(target, lane),
            device_id_type=mesh_ids,
        )
        copy.start()
        copies.append(copy)
    y_ref[me] = x_ref[...] if broadcast else x_ref[me]
    for copy in copies:
        copy.wait()


def grp_exchange(x, groups, broadcast, collective):
    out_shape = (groups,) + (x.shape if broadcast else x.shape[1:])
    vmem = pl.BlockSpec(memory_space=pltpu.VMEM)
    return pl.pallas_call(
        lambda *refs: exchange_kernel(broadcast, *refs),
        out_shape=jax.ShapeDtypeStruct(out_shape, x.dtype),
        in_specs=[vmem],
        out_specs=vmem,
        scratch_shapes=[pltpu.SemaphoreType.DMA((groups,)), pltpu.SemaphoreType.DMA((groups,))],
        compiler_params=pltpu.CompilerParams(collective_id=collective, has_side_effects=True),
    )(x)


def reduce_kernel(x_ref, y_ref, part_ref, send_sem, recv_sem, back_send, back_recv):
    groups = y_ref.shape[0]
    me = lax.axis_index("grp")
    lane = lax.axis_index("seq")
    mesh_ids = pl.DeviceIdType.MESH
    barrier = pltpu.get_barrier_semaphore()
    for step in range(1, groups):
        pl.semaphore_signal(
            barrier, inc=1, device_id=(lax.rem(me + step, groups), lane), device_id_type=mesh_ids
        )
    pl.semaphore_wait(barrier, groups - 1)
    copies = []
    for step in range(1, groups):
        target = lax.rem(me + step, groups)
        copy = pltpu.make_async_remote_copy(
            src_ref=x_ref.at[target],
            dst_ref=part_ref.at[me],
            send_sem=send_sem.at[step],
            recv_sem=recv_sem.at[step],
            device_id=(target, lane),
            device_id_type=mesh_ids,
        )
        copy.start()
        copies.append(copy)
    part_ref[me] = x_ref[me]
    for copy in copies:
        copy.wait()
    y_ref[me] = jnp.sum(part_ref[...].astype(jnp.float32), axis=0).astype(y_ref.dtype)
    copies = []
    for step in range(1, groups):
        target = lax.rem(me + step, groups)
        copy = pltpu.make_async_remote_copy(
            src_ref=y_ref.at[me],
            dst_ref=y_ref.at[me],
            send_sem=back_send.at[step],
            recv_sem=back_recv.at[step],
            device_id=(target, lane),
            device_id_type=mesh_ids,
        )
        copy.start()
        copies.append(copy)
    for copy in copies:
        copy.wait()


def grp_reduce(x, groups, collective):
    vmem = pl.BlockSpec(memory_space=pltpu.VMEM)
    sems = pltpu.SemaphoreType.DMA((groups,))
    return pl.pallas_call(
        reduce_kernel,
        out_shape=jax.ShapeDtypeStruct(x.shape, x.dtype),
        in_specs=[vmem],
        out_specs=vmem,
        scratch_shapes=[pltpu.VMEM(x.shape, x.dtype), sems, sems, sems, sems],
        compiler_params=pltpu.CompilerParams(collective_id=collective, has_side_effects=True),
    )(x)


def combine_kernel(
    acc_in, stats_in, out_ref, stats_out, acc_part, stats_part,
    send_acc, recv_acc, send_stats, recv_stats, back_send, back_recv, stat_send, stat_recv,
):
    groups, chunk_rows, head_width = out_ref.shape
    me = lax.axis_index("grp")
    lane = lax.axis_index("seq")
    mesh_ids = pl.DeviceIdType.MESH
    barrier = pltpu.get_barrier_semaphore()
    for step in range(1, groups):
        pl.semaphore_signal(
            barrier, inc=1, device_id=(lax.rem(me + step, groups), lane), device_id_type=mesh_ids
        )
    pl.semaphore_wait(barrier, groups - 1)
    copies = []
    for step in range(1, groups):
        target = lax.rem(me + step, groups)
        for source, landing, sent, got in (
            (acc_in, acc_part, send_acc, recv_acc),
            (stats_in, stats_part, send_stats, recv_stats),
        ):
            copy = pltpu.make_async_remote_copy(
                src_ref=source.at[target],
                dst_ref=landing.at[me],
                send_sem=sent.at[step],
                recv_sem=got.at[step],
                device_id=(target, lane),
                device_id_type=mesh_ids,
            )
            copy.start()
            copies.append(copy)
    acc_part[me] = acc_in[me]
    stats_part[me] = stats_in[me]
    for copy in copies:
        copy.wait()
    columns = jnp.transpose(stats_part[...].reshape(groups * 8, 128))
    maxima = [columns[:chunk_rows, 8 * g : 8 * g + 1] for g in range(groups)]
    totals = [columns[chunk_rows:, 8 * g : 8 * g + 1] for g in range(groups)]
    top = maxima[0]
    for g in range(1, groups):
        top = jnp.maximum(top, maxima[g])
    row_total = jnp.zeros_like(top)
    row_accum = jnp.zeros((chunk_rows, head_width), jnp.float32)
    for g in range(groups):
        shrink = jnp.exp(maxima[g] - top)
        row_total = row_total + totals[g] * shrink
        row_accum = row_accum + acc_part[g].astype(jnp.float32) * shrink
    out_ref[me] = (row_accum / row_total).astype(out_ref.dtype)
    spread = jnp.concatenate(
        [jnp.broadcast_to(top, (chunk_rows, 128)), jnp.broadcast_to(row_total, (chunk_rows, 128))], axis=0
    )
    stats_out[me] = jnp.transpose(spread)[:8, :]
    copies = []
    for step in range(1, groups):
        target = lax.rem(me + step, groups)
        for source, sent, got in ((out_ref, back_send, back_recv), (stats_out, stat_send, stat_recv)):
            copy = pltpu.make_async_remote_copy(
                src_ref=source.at[me],
                dst_ref=source.at[me],
                send_sem=sent.at[step],
                recv_sem=got.at[step],
                device_id=(target, lane),
                device_id_type=mesh_ids,
            )
            copy.start()
            copies.append(copy)
    for copy in copies:
        copy.wait()


def grp_combine(accum, stats, collective):
    groups = accum.shape[0]
    vmem = pl.BlockSpec(memory_space=pltpu.VMEM)
    sems = pltpu.SemaphoreType.DMA((groups,))
    return pl.pallas_call(
        combine_kernel,
        out_shape=(
            jax.ShapeDtypeStruct(accum.shape, accum.dtype),
            jax.ShapeDtypeStruct(stats.shape, stats.dtype),
        ),
        in_specs=[vmem, vmem],
        out_specs=(vmem, vmem),
        scratch_shapes=[pltpu.VMEM(accum.shape, accum.dtype), pltpu.VMEM(stats.shape, stats.dtype)]
        + [sems] * 8,
        compiler_params=pltpu.CompilerParams(collective_id=collective, has_side_effects=True),
    )(accum, stats)


def back_kernel(
    dq_in, dk_in, dv_in, dq_out, gk_out, gv_out, part_ref, recv_k, recv_v,
    send_sem, recv_sem, back_send, back_recv, kv_send, kv_recv,
):
    groups = dq_out.shape[0]
    sources, block, head_width = recv_k.shape
    me = lax.axis_index("grp")
    lane = lax.axis_index("seq")
    mesh_ids = pl.DeviceIdType.MESH
    barrier = pltpu.get_barrier_semaphore()
    for step in range(1, groups):
        pl.semaphore_signal(
            barrier, inc=1, device_id=(lax.rem(me + step, groups), lane), device_id_type=mesh_ids
        )
    for step in range(1, sources):
        pl.semaphore_signal(
            barrier, inc=1, device_id=(me, lax.rem(lane + step, sources)), device_id_type=mesh_ids
        )
    pl.semaphore_wait(barrier, groups - 1 + sources - 1)
    returns = []
    for step in range(1, sources):
        target = lax.rem(lane + step, sources)
        rows = pl.ds(pl.multiple_of(target * block, block), block)
        for index, (source, landing) in enumerate(((dk_in, recv_k), (dv_in, recv_v))):
            copy = pltpu.make_async_remote_copy(
                src_ref=source.at[rows],
                dst_ref=landing.at[lane],
                send_sem=kv_send.at[index, step],
                recv_sem=kv_recv.at[index, step],
                device_id=(me, target),
                device_id_type=mesh_ids,
            )
            copy.start()
            returns.append(copy)
    copies = []
    for step in range(1, groups):
        target = lax.rem(me + step, groups)
        copy = pltpu.make_async_remote_copy(
            src_ref=dq_in.at[target],
            dst_ref=part_ref.at[me],
            send_sem=send_sem.at[step],
            recv_sem=recv_sem.at[step],
            device_id=(target, lane),
            device_id_type=mesh_ids,
        )
        copy.start()
        copies.append(copy)
    own_rows = pl.ds(pl.multiple_of(lane * block, block), block)
    recv_k[lane] = dk_in[own_rows, :]
    recv_v[lane] = dv_in[own_rows, :]
    part_ref[me] = dq_in[me]
    for copy in copies:
        copy.wait()
    dq_out[me] = jnp.sum(part_ref[...].astype(jnp.float32), axis=0).astype(dq_out.dtype)
    copies = []
    for step in range(1, groups):
        target = lax.rem(me + step, groups)
        copy = pltpu.make_async_remote_copy(
            src_ref=dq_out.at[me],
            dst_ref=dq_out.at[me],
            send_sem=back_send.at[step],
            recv_sem=back_recv.at[step],
            device_id=(target, lane),
            device_id_type=mesh_ids,
        )
        copy.start()
        copies.append(copy)
    for copy in returns:
        copy.wait()
    for head in range(sources // 2):
        cols = pl.ds(head * head_width, head_width)
        for landing, out_ref in ((recv_k, gk_out), (recv_v, gv_out)):
            out_ref[:, cols] = (
                landing[2 * head].astype(jnp.float32) + landing[2 * head + 1].astype(jnp.float32)
            ).astype(out_ref.dtype)
    for copy in copies:
        copy.wait()


def back_exchange(query_grad, key_grad, value_grad, groups, sources, collective):
    head_width = query_grad.shape[-1]
    block = key_grad.shape[0] // sources
    vmem = pl.BlockSpec(memory_space=pltpu.VMEM)
    grad_shape = jax.ShapeDtypeStruct((block, sources // 2 * head_width), key_grad.dtype)
    sems = pltpu.SemaphoreType.DMA((groups,))
    return pl.pallas_call(
        back_kernel,
        out_shape=(jax.ShapeDtypeStruct(query_grad.shape, query_grad.dtype), grad_shape, grad_shape),
        in_specs=[vmem, vmem, vmem],
        out_specs=(vmem, vmem, vmem),
        scratch_shapes=[
            pltpu.VMEM(query_grad.shape, query_grad.dtype),
            pltpu.VMEM((sources, block, head_width), key_grad.dtype),
            pltpu.VMEM((sources, block, head_width), key_grad.dtype),
            sems,
            sems,
            sems,
            sems,
            pltpu.SemaphoreType.DMA((2, sources)),
            pltpu.SemaphoreType.DMA((2, sources)),
        ],
        compiler_params=pltpu.CompilerParams(collective_id=collective, has_side_effects=True),
    )(query_grad, key_grad, value_grad)


def gather_kernel(k_ref, v_ref, k_out, v_out, send_sem, recv_sem, pair_send, pair_recv, own_sem):
    sources, halves, half, head_width = k_out.shape
    me = lax.axis_index("seq")
    grp_here = lax.axis_index("grp")
    mine = lax.rem(me, 2)
    partner = me + 1 - 2 * mine
    head = me // 2
    mesh_ids = pl.DeviceIdType.MESH
    barrier = pltpu.get_barrier_semaphore()
    for step in range(1, sources):
        pl.semaphore_signal(
            barrier, inc=1, device_id=(grp_here, lax.rem(me + step, sources)), device_id_type=mesh_ids
        )
    pl.semaphore_wait(barrier, sources - 1)
    copies = []
    for step in range(1, sources):
        target = lax.rem(me + step, sources)
        rows = pl.ds(pl.multiple_of(lax.rem(target, 2) * half, half), half)
        cols = pl.ds(pl.multiple_of((target // 2) * head_width, head_width), head_width)
        for index, (source, landing) in enumerate(((k_ref, k_out), (v_ref, v_out))):
            copy = pltpu.make_async_remote_copy(
                src_ref=source.at[rows, cols],
                dst_ref=landing.at[me, lax.rem(target, 2)],
                send_sem=send_sem.at[index, step],
                recv_sem=recv_sem.at[index, step],
                device_id=(grp_here, target),
                device_id_type=mesh_ids,
            )
            copy.start()
            copies.append(copy)
    own_rows = pl.ds(pl.multiple_of(mine * half, half), half)
    own_cols = pl.ds(pl.multiple_of(head * head_width, head_width), head_width)
    own = []
    for index, (source, landing) in enumerate(((k_ref, k_out), (v_ref, v_out))):
        copy = pltpu.make_async_copy(source.at[own_rows, own_cols], landing.at[me, mine], own_sem.at[index])
        copy.start()
        own.append(copy)
    forwards = []

    def forward(step, block, sources_of):
        for index, (landing, source) in enumerate(zip((k_out, v_out), sources_of)):
            copy = pltpu.make_async_remote_copy(
                src_ref=source,
                dst_ref=landing.at[block, mine],
                send_sem=pair_send.at[index, step],
                recv_sem=pair_recv.at[index, step],
                device_id=(grp_here, partner),
                device_id_type=mesh_ids,
            )
            copy.start()
            forwards.append(copy)

    forward(0, me, (k_ref.at[own_rows, own_cols], v_ref.at[own_rows, own_cols]))
    for step in range(1, sources):
        for copy in copies[2 * (step - 1) : 2 * step]:
            copy.wait()
        block = lax.rem(me + sources - step, sources)
        forward(step, block, (k_out.at[block, mine], v_out.at[block, mine]))
    for copy in forwards + own:
        copy.wait()


def seq_gather(scene_keys, scene_values, sources, head_width, collective):
    half = scene_keys.shape[0] // QPARTS
    vmem = pl.BlockSpec(memory_space=pltpu.VMEM)
    out = jax.ShapeDtypeStruct((sources, QPARTS, half, head_width), scene_keys.dtype)
    return pl.pallas_call(
        gather_kernel,
        out_shape=(out, out),
        in_specs=[pl.BlockSpec(memory_space=pl.ANY)] * 2,
        out_specs=(vmem, vmem),
        scratch_shapes=[
            pltpu.SemaphoreType.DMA((2, sources)),
            pltpu.SemaphoreType.DMA((2, sources)),
            pltpu.SemaphoreType.DMA((2, sources)),
            pltpu.SemaphoreType.DMA((2, sources)),
            pltpu.SemaphoreType.DMA((2,)),
        ],
        compiler_params=pltpu.CompilerParams(collective_id=collective, has_side_effects=True),
    )(scene_keys, scene_values)


def scatter_rows(rows, parts, collective):
    return grp_exchange(
        rows.reshape(parts, rows.shape[0] // parts, rows.shape[1]), parts, False, collective
    )


def broadcast_rows(chunk, parts, collective):
    gathered = grp_exchange(chunk, parts, True, collective)
    return gathered.reshape(parts * chunk.shape[0], chunk.shape[1])


def per_device(queries, scene_keys, scene_values, grad_output, tile_list, tile_counts):
    items_here = queries.shape[0]
    head_width = queries.shape[2]
    query_rows = queries.shape[1]
    scene_here = scene_keys.shape[0]
    heads_total = scene_keys.shape[1] // head_width
    seq_devices = lax.axis_size("seq")
    groups = lax.axis_size("grp")
    chunk_rows = query_rows // groups
    group_keys = scene_here * seq_devices
    copies = max(1, QPARTS // items_here)
    heads_here = max(1, items_here // QPARTS)
    softmax_scale = head_width ** (-0.5)
    half_keys = scene_here // QPARTS
    key_halves, value_halves = seq_gather(scene_keys, scene_values, seq_devices, head_width, 4)
    key_group = key_halves.reshape(group_keys, 1, head_width)
    value_group = value_halves.reshape(group_keys, 1, head_width)
    part_accum, stats = forward_item(
        queries[0],
        key_group[:, 0, :],
        value_group[:, 0, :],
        tile_list[0, 0],
        tile_counts[0, 0],
        softmax_scale,
        groups,
    )
    out_rows, out_stats = grp_combine(part_accum, stats, 0)
    attended = out_rows.reshape(1, query_rows, head_width)
    query_grad, key_grad, value_grad = backward_item(
        queries[0],
        key_group[:, 0, :],
        value_group[:, 0, :],
        grad_output[0],
        attended[0],
        out_stats,
        tile_list[0, 0],
        tile_counts[0, 0],
        softmax_scale,
    )
    grad_queries, grad_keys, grad_values = back_exchange(
        query_grad.reshape(groups, chunk_rows, head_width), key_grad, value_grad, groups, seq_devices, 2
    )
    grad_queries = grad_queries.reshape(1, query_rows, head_width)
    return (attended, grad_queries, grad_keys, grad_values)


def solution(mesh):
    in_specs = (
        P("seq", None, None),
        P(("grp", "seq"), None),
        P(("grp", "seq"), None),
        P("seq", None, None),
        P("grp", "seq", None, None),
        P("grp", "seq"),
    )
    out_specs = (
        P("seq", None, None),
        P("seq", None, None),
        P(("grp", "seq"), None),
        P(("grp", "seq"), None),
    )
    return jax.shard_map(
        per_device, mesh=mesh, in_specs=in_specs, out_specs=out_specs, check_vma=False
    )
```

```python
import jax
import jax.numpy as jnp
from jax import lax
from jax.experimental import pallas as pl
from jax.experimental.pallas import tpu as pltpu
from jax.sharding import PartitionSpec as P

QPARTS = 2
QBLK = 512
KBLK = 512


NEG_START = -1e30


LIST_SLOTS = 9


def tile_starts(list_ref, position):
    query_block = jnp.clip(list_ref[position, 0], 0, QPARTS - 1)
    key_block = jnp.clip(list_ref[position, 1], 0, 7)
    return (
        pl.multiple_of(query_block * QBLK, QBLK),
        pl.multiple_of(key_block * KBLK, KBLK),
    )


def forward_kernel(
    softmax_scale, list_ref, count_ref, q_ref, k_ref, v_ref, acc_out, stats_out, max_ref, total_ref, accum_ref
):
    max_ref[...] = jnp.full(max_ref.shape, NEG_START, jnp.float32)
    total_ref[...] = jnp.zeros(total_ref.shape, jnp.float32)
    accum_ref[...] = jnp.zeros(accum_ref.shape, jnp.float32)
    live_tiles = jnp.clip(count_ref[0], 0, LIST_SLOTS)

    def visit(position, carry):
        query_start, key_start = tile_starts(list_ref, position)
        rows = pl.ds(query_start, QBLK)
        keys = pl.ds(key_start, KBLK)
        scores = (
            lax.dot_general(
                q_ref[rows, :], k_ref[keys, :], (((1,), (1,)), ((), ())),
                preferred_element_type=jnp.float32,
            )
            * softmax_scale
        )
        old_max = max_ref[rows, :]
        new_max = jnp.maximum(old_max, jnp.max(scores, axis=1, keepdims=True))
        new_max = new_max.astype(jnp.bfloat16).astype(jnp.float32)
        weights = jnp.exp(scores - new_max[:, :1])
        shrink = jnp.exp(old_max - new_max)
        total_ref[rows, :] = total_ref[rows, :] * shrink + jnp.sum(weights, axis=1, keepdims=True)
        accum_ref[rows, :] = accum_ref[rows, :] * shrink[:, :1] + jnp.dot(
            weights.astype(jnp.bfloat16), v_ref[keys, :], preferred_element_type=jnp.float32
        )
        max_ref[rows, :] = new_max
        return carry

    lax.fori_loop(0, live_tiles, visit, 0)
    groups, chunk_rows = acc_out.shape[0], acc_out.shape[1]
    for g in range(groups):
        rows = pl.ds(g * chunk_rows, chunk_rows)
        acc_out[g] = accum_ref[rows, :].astype(acc_out.dtype)
        stacked = jnp.concatenate([max_ref[rows, :], total_ref[rows, :]], axis=0)
        stats_out[g] = jnp.transpose(stacked)[:8, :]


def forward_item(query_item, key_head, value_head, listing, live_tiles, softmax_scale, groups):
    query_rows, head_width = query_item.shape
    chunk_rows = query_rows // groups
    smem = pl.BlockSpec(memory_space=pltpu.SMEM)
    vmem = pl.BlockSpec(memory_space=pltpu.VMEM)
    rows_f32 = pltpu.VMEM((query_rows, head_width), jnp.float32)
    return pl.pallas_call(
        lambda *refs: forward_kernel(softmax_scale, *refs),
        out_shape=(
            jax.ShapeDtypeStruct((groups, chunk_rows, head_width), jnp.bfloat16),
            jax.ShapeDtypeStruct((groups, 8, 2 * chunk_rows), jnp.float32),
        ),
        in_specs=[smem, smem, vmem, vmem, vmem],
        out_specs=(vmem, vmem),
        scratch_shapes=[rows_f32, rows_f32, rows_f32],
    )(listing, live_tiles.reshape(1), query_item, key_head, value_head)


def backward_kernel(
    softmax_scale, list_ref, count_ref, q_ref, k_ref, v_ref, do_ref, att_ref, stats_ref,
    dq_ref, dk_ref, dv_ref, dq_acc, dk_acc, dv_acc, log_ref, delta_ref,
):
    groups = stats_ref.shape[0]
    chunk_rows = stats_ref.shape[2] // 2
    for g in range(groups):
        rows = pl.ds(g * chunk_rows, chunk_rows)
        columns = jnp.transpose(jnp.broadcast_to(stats_ref[g][0:1, :], (2 * chunk_rows, 2 * chunk_rows)))
        log_ref[rows, :] = columns[:chunk_rows, 0:1] + jnp.log(columns[chunk_rows:, 0:1])
        delta_ref[rows, :] = jnp.sum(
            att_ref[rows, :].astype(jnp.float32) * do_ref[rows, :].astype(jnp.float32),
            axis=1,
            keepdims=True,
        )
    dq_acc[...] = jnp.zeros(dq_acc.shape, jnp.float32)
    dk_acc[...] = jnp.zeros(dk_acc.shape, jnp.float32)
    dv_acc[...] = jnp.zeros(dv_acc.shape, jnp.float32)
    live_tiles = jnp.clip(count_ref[0], 0, LIST_SLOTS)

    def visit(position, carry):
        query_start, key_start = tile_starts(list_ref, position)
        rows = pl.ds(query_start, QBLK)
        keys = pl.ds(key_start, KBLK)
        query_block = q_ref[rows, :]
        grad_block = do_ref[rows, :]
        key_block = k_ref[keys, :]
        value_block = v_ref[keys, :]
        scores = (
            lax.dot_general(
                query_block, key_block, (((1,), (1,)), ((), ())),
                preferred_element_type=jnp.float32,
            )
            * softmax_scale
        )
        probs = jnp.exp(scores - log_ref[rows, :])
        probs_half = probs.astype(jnp.bfloat16)
        dv_acc[keys, :] += lax.dot_general(
            probs_half, grad_block, (((0,), (0,)), ((), ())), preferred_element_type=jnp.float32
        )
        prob_grad = lax.dot_general(
            grad_block, value_block, (((1,), (1,)), ((), ())), preferred_element_type=jnp.float32
        )
        score_grad = (probs * (prob_grad - delta_ref[rows, :])).astype(jnp.bfloat16)
        dq_acc[rows, :] += (
            jnp.dot(score_grad, key_block, preferred_element_type=jnp.float32) * softmax_scale
        )
        dk_acc[keys, :] += (
            lax.dot_general(
                score_grad, query_block, (((0,), (0,)), ((), ())),
                preferred_element_type=jnp.float32,
            )
            * softmax_scale
        )
        return carry

    lax.fori_loop(0, live_tiles, visit, 0)
    dq_ref[...] = dq_acc[...].astype(dq_ref.dtype)
    dk_ref[...] = dk_acc[...].astype(dk_ref.dtype)
    dv_ref[...] = dv_acc[...].astype(dv_ref.dtype)


def backward_item(
    query_item, key_head, value_head, grad_item, attended, stats, listing, live_tiles, softmax_scale,
):
    query_rows, head_width = query_item.shape
    key_rows = key_head.shape[0]
    smem = pl.BlockSpec(memory_space=pltpu.SMEM)
    vmem = pl.BlockSpec(memory_space=pltpu.VMEM)
    return pl.pallas_call(
        lambda *refs: backward_kernel(softmax_scale, *refs),
        out_shape=(
            jax.ShapeDtypeStruct((query_rows, head_width), jnp.bfloat16),
            jax.ShapeDtypeStruct((key_rows, head_width), jnp.bfloat16),
            jax.ShapeDtypeStruct((key_rows, head_width), jnp.bfloat16),
        ),
        in_specs=[smem, smem] + [vmem] * 6,
        out_specs=(vmem, vmem, vmem),
        scratch_shapes=[
            pltpu.VMEM((query_rows, head_width), jnp.float32),
            pltpu.VMEM((key_rows, head_width), jnp.float32),
            pltpu.VMEM((key_rows, head_width), jnp.float32),
            pltpu.VMEM((query_rows, 1), jnp.float32),
            pltpu.VMEM((query_rows, 1), jnp.float32),
        ],
    )(
        listing,
        live_tiles.reshape(1),
        query_item,
        key_head,
        value_head,
        grad_item,
        attended,
        stats,
    )


def exchange_kernel(broadcast, x_ref, y_ref, send_sem, recv_sem):
    groups = y_ref.shape[0]
    me = lax.axis_index("grp")
    lane = lax.axis_index("seq")
    mesh_ids = pl.DeviceIdType.MESH
    barrier = pltpu.get_barrier_semaphore()
    for step in range(1, groups):
        pl.semaphore_signal(
            barrier, inc=1, device_id=(lax.rem(me + step, groups), lane), device_id_type=mesh_ids
        )
    pl.semaphore_wait(barrier, groups - 1)
    copies = []
    for step in range(1, groups):
        target = lax.rem(me + step, groups)
        copy = pltpu.make_async_remote_copy(
            src_ref=x_ref if broadcast else x_ref.at[target],
            dst_ref=y_ref.at[me],
            send_sem=send_sem.at[step],
            recv_sem=recv_sem.at[step],
            device_id=(target, lane),
            device_id_type=mesh_ids,
        )
        copy.start()
        copies.append(copy)
    y_ref[me] = x_ref[...] if broadcast else x_ref[me]
    for copy in copies:
        copy.wait()


def grp_exchange(x, groups, broadcast, collective):
    out_shape = (groups,) + (x.shape if broadcast else x.shape[1:])
    vmem = pl.BlockSpec(memory_space=pltpu.VMEM)
    return pl.pallas_call(
        lambda *refs: exchange_kernel(broadcast, *refs),
        out_shape=jax.ShapeDtypeStruct(out_shape, x.dtype),
        in_specs=[vmem],
        out_specs=vmem,
        scratch_shapes=[pltpu.SemaphoreType.DMA((groups,)), pltpu.SemaphoreType.DMA((groups,))],
        compiler_params=pltpu.CompilerParams(collective_id=collective, has_side_effects=True),
    )(x)


def reduce_kernel(x_ref, y_ref, part_ref, send_sem, recv_sem, back_send, back_recv):
    groups = y_ref.shape[0]
    me = lax.axis_index("grp")
    lane = lax.axis_index("seq")
    mesh_ids = pl.DeviceIdType.MESH
    barrier = pltpu.get_barrier_semaphore()
    for step in range(1, groups):
        pl.semaphore_signal(
            barrier, inc=1, device_id=(lax.rem(me + step, groups), lane), device_id_type=mesh_ids
        )
    pl.semaphore_wait(barrier, groups - 1)
    copies = []
    for step in range(1, groups):
        target = lax.rem(me + step, groups)
        copy = pltpu.make_async_remote_copy(
            src_ref=x_ref.at[target],
            dst_ref=part_ref.at[me],
            send_sem=send_sem.at[step],
            recv_sem=recv_sem.at[step],
            device_id=(target, lane),
            device_id_type=mesh_ids,
        )
        copy.start()
        copies.append(copy)
    part_ref[me] = x_ref[me]
    for copy in copies:
        copy.wait()
    y_ref[me] = jnp.sum(part_ref[...].astype(jnp.float32), axis=0).astype(y_ref.dtype)
    copies = []
    for step in range(1, groups):
        target = lax.rem(me + step, groups)
        copy = pltpu.make_async_remote_copy(
            src_ref=y_ref.at[me],
            dst_ref=y_ref.at[me],
            send_sem=back_send.at[step],
            recv_sem=back_recv.at[step],
            device_id=(target, lane),
            device_id_type=mesh_ids,
        )
        copy.start()
        copies.append(copy)
    for copy in copies:
        copy.wait()


def grp_reduce(x, groups, collective):
    vmem = pl.BlockSpec(memory_space=pltpu.VMEM)
    sems = pltpu.SemaphoreType.DMA((groups,))
    return pl.pallas_call(
        reduce_kernel,
        out_shape=jax.ShapeDtypeStruct(x.shape, x.dtype),
        in_specs=[vmem],
        out_specs=vmem,
        scratch_shapes=[pltpu.VMEM(x.shape, x.dtype), sems, sems, sems, sems],
        compiler_params=pltpu.CompilerParams(collective_id=collective, has_side_effects=True),
    )(x)


def combine_kernel(
    acc_in, stats_in, out_ref, stats_out, acc_part, stats_part,
    send_acc, recv_acc, send_stats, recv_stats, back_send, back_recv, stat_send, stat_recv,
):
    groups, chunk_rows, head_width = out_ref.shape
    me = lax.axis_index("grp")
    lane = lax.axis_index("seq")
    mesh_ids = pl.DeviceIdType.MESH
    barrier = pltpu.get_barrier_semaphore()
    for step in range(1, groups):
        pl.semaphore_signal(
            barrier, inc=1, device_id=(lax.rem(me + step, groups), lane), device_id_type=mesh_ids
        )
    pl.semaphore_wait(barrier, groups - 1)
    copies = []
    for step in range(1, groups):
        target = lax.rem(me + step, groups)
        for source, landing, sent, got in (
            (acc_in, acc_part, send_acc, recv_acc),
            (stats_in, stats_part, send_stats, recv_stats),
        ):
            copy = pltpu.make_async_remote_copy(
                src_ref=source.at[target],
                dst_ref=landing.at[me],
                send_sem=sent.at[step],
                recv_sem=got.at[step],
                device_id=(target, lane),
                device_id_type=mesh_ids,
            )
            copy.start()
            copies.append(copy)

    def columns_of(stats_block):
        spread_row = jnp.broadcast_to(stats_block[0:1, :], (2 * chunk_rows, 2 * chunk_rows))
        columns = jnp.transpose(spread_row)
        return columns[:chunk_rows, 0:1], columns[chunk_rows:, 0:1]

    top, row_total = columns_of(stats_in[me])
    row_accum = acc_in[me].astype(jnp.float32)
    for step in range(1, groups):
        for copy in copies[2 * (step - 1) : 2 * step]:
            copy.wait()
        sender = lax.rem(me + groups - step, groups)
        their_max, their_total = columns_of(stats_part[sender])
        new_top = jnp.maximum(top, their_max)
        keep = jnp.exp(top - new_top)
        take = jnp.exp(their_max - new_top)
        row_total = row_total * keep + their_total * take
        row_accum = row_accum * keep + acc_part[sender].astype(jnp.float32) * take
        top = new_top
    out_ref[me] = (row_accum / row_total).astype(out_ref.dtype)
    spread = jnp.concatenate(
        [jnp.broadcast_to(top, (chunk_rows, 128)), jnp.broadcast_to(row_total, (chunk_rows, 128))], axis=0
    )
    stats_out[me] = jnp.transpose(spread)[:8, :]
    copies = []
    for step in range(1, groups):
        target = lax.rem(me + step, groups)
        for source, sent, got in ((out_ref, back_send, back_recv), (stats_out, stat_send, stat_recv)):
            copy = pltpu.make_async_remote_copy(
                src_ref=source.at[me],
                dst_ref=source.at[me],
                send_sem=sent.at[step],
                recv_sem=got.at[step],
                device_id=(target, lane),
                device_id_type=mesh_ids,
            )
            copy.start()
            copies.append(copy)
    for copy in copies:
        copy.wait()


def grp_combine(accum, stats, collective):
    groups = accum.shape[0]
    vmem = pl.BlockSpec(memory_space=pltpu.VMEM)
    sems = pltpu.SemaphoreType.DMA((groups,))
    return pl.pallas_call(
        combine_kernel,
        out_shape=(
            jax.ShapeDtypeStruct(accum.shape, accum.dtype),
            jax.ShapeDtypeStruct(stats.shape, stats.dtype),
        ),
        in_specs=[vmem, vmem],
        out_specs=(vmem, vmem),
        scratch_shapes=[pltpu.VMEM(accum.shape, accum.dtype), pltpu.VMEM(stats.shape, stats.dtype)]
        + [sems] * 8,
        compiler_params=pltpu.CompilerParams(collective_id=collective, has_side_effects=True),
    )(accum, stats)


def back_kernel(
    dq_in, dk_in, dv_in, dq_out, gk_out, gv_out, part_ref, recv_k, recv_v,
    send_sem, recv_sem, back_send, back_recv, kv_send, kv_recv,
):
    groups = dq_out.shape[0]
    sources, block, head_width = recv_k.shape
    me = lax.axis_index("grp")
    lane = lax.axis_index("seq")
    mesh_ids = pl.DeviceIdType.MESH
    barrier = pltpu.get_barrier_semaphore()
    for step in range(1, groups):
        pl.semaphore_signal(
            barrier, inc=1, device_id=(lax.rem(me + step, groups), lane), device_id_type=mesh_ids
        )
    for step in range(1, sources):
        pl.semaphore_signal(
            barrier, inc=1, device_id=(me, lax.rem(lane + step, sources)), device_id_type=mesh_ids
        )
    pl.semaphore_wait(barrier, groups - 1 + sources - 1)
    returns = []
    for step in range(1, sources):
        target = lax.rem(lane + step, sources)
        rows = pl.ds(pl.multiple_of(target * block, block), block)
        for index, (source, landing) in enumerate(((dk_in, recv_k), (dv_in, recv_v))):
            copy = pltpu.make_async_remote_copy(
                src_ref=source.at[rows],
                dst_ref=landing.at[lane],
                send_sem=kv_send.at[index, step],
                recv_sem=kv_recv.at[index, step],
                device_id=(me, target),
                device_id_type=mesh_ids,
            )
            copy.start()
            returns.append(copy)
    copies = []
    for step in range(1, groups):
        target = lax.rem(me + step, groups)
        copy = pltpu.make_async_remote_copy(
            src_ref=dq_in.at[target],
            dst_ref=part_ref.at[me],
            send_sem=send_sem.at[step],
            recv_sem=recv_sem.at[step],
            device_id=(target, lane),
            device_id_type=mesh_ids,
        )
        copy.start()
        copies.append(copy)
    own_rows = pl.ds(pl.multiple_of(lane * block, block), block)
    recv_k[lane] = dk_in[own_rows, :]
    recv_v[lane] = dv_in[own_rows, :]
    part_ref[me] = dq_in[me]
    for copy in copies:
        copy.wait()
    dq_out[me] = jnp.sum(part_ref[...].astype(jnp.float32), axis=0).astype(dq_out.dtype)
    copies = []
    for step in range(1, groups):
        target = lax.rem(me + step, groups)
        copy = pltpu.make_async_remote_copy(
            src_ref=dq_out.at[me],
            dst_ref=dq_out.at[me],
            send_sem=back_send.at[step],
            recv_sem=back_recv.at[step],
            device_id=(target, lane),
            device_id_type=mesh_ids,
        )
        copy.start()
        copies.append(copy)
    for copy in returns:
        copy.wait()
    for head in range(sources // 2):
        cols = pl.ds(head * head_width, head_width)
        for landing, out_ref in ((recv_k, gk_out), (recv_v, gv_out)):
            out_ref[:, cols] = (
                landing[2 * head].astype(jnp.float32) + landing[2 * head + 1].astype(jnp.float32)
            ).astype(out_ref.dtype)
    for copy in copies:
        copy.wait()


def back_exchange(query_grad, key_grad, value_grad, groups, sources, collective):
    head_width = query_grad.shape[-1]
    block = key_grad.shape[0] // sources
    vmem = pl.BlockSpec(memory_space=pltpu.VMEM)
    grad_shape = jax.ShapeDtypeStruct((block, sources // 2 * head_width), key_grad.dtype)
    sems = pltpu.SemaphoreType.DMA((groups,))
    return pl.pallas_call(
        back_kernel,
        out_shape=(jax.ShapeDtypeStruct(query_grad.shape, query_grad.dtype), grad_shape, grad_shape),
        in_specs=[vmem, vmem, vmem],
        out_specs=(vmem, vmem, vmem),
        scratch_shapes=[
            pltpu.VMEM(query_grad.shape, query_grad.dtype),
            pltpu.VMEM((sources, block, head_width), key_grad.dtype),
            pltpu.VMEM((sources, block, head_width), key_grad.dtype),
            sems,
            sems,
            sems,
            sems,
            pltpu.SemaphoreType.DMA((2, sources)),
            pltpu.SemaphoreType.DMA((2, sources)),
        ],
        compiler_params=pltpu.CompilerParams(collective_id=collective, has_side_effects=True),
    )(query_grad, key_grad, value_grad)


def gather_kernel(k_ref, v_ref, k_out, v_out, send_sem, recv_sem, pair_send, pair_recv):
    sources, halves, half, head_width = k_out.shape
    me = lax.axis_index("seq")
    grp_here = lax.axis_index("grp")
    mine = lax.rem(me, 2)
    partner = me + 1 - 2 * mine
    head = me // 2
    mesh_ids = pl.DeviceIdType.MESH
    barrier = pltpu.get_barrier_semaphore()
    for step in range(1, sources):
        pl.semaphore_signal(
            barrier, inc=1, device_id=(grp_here, lax.rem(me + step, sources)), device_id_type=mesh_ids
        )
    pl.semaphore_wait(barrier, sources - 1)
    copies = []
    for step in range(1, sources):
        target = lax.rem(me + step, sources)
        rows = pl.ds(pl.multiple_of(lax.rem(target, 2) * half, half), half)
        cols = pl.ds(pl.multiple_of((target // 2) * head_width, head_width), head_width)
        for index, (source, landing) in enumerate(((k_ref, k_out), (v_ref, v_out))):
            copy = pltpu.make_async_remote_copy(
                src_ref=source.at[rows, cols],
                dst_ref=landing.at[me, lax.rem(target, 2)],
                send_sem=send_sem.at[index, step],
                recv_sem=recv_sem.at[index, step],
                device_id=(grp_here, target),
                device_id_type=mesh_ids,
            )
            copy.start()
            copies.append(copy)
    own_rows = pl.ds(pl.multiple_of(mine * half, half), half)
    own_cols = pl.ds(pl.multiple_of(head * head_width, head_width), head_width)
    k_out[me, mine] = k_ref[own_rows, own_cols]
    v_out[me, mine] = v_ref[own_rows, own_cols]
    forwards = []

    def forward(step, block, sources_of):
        for index, (landing, source) in enumerate(zip((k_out, v_out), sources_of)):
            copy = pltpu.make_async_remote_copy(
                src_ref=source,
                dst_ref=landing.at[block, mine],
                send_sem=pair_send.at[index, step],
                recv_sem=pair_recv.at[index, step],
                device_id=(grp_here, partner),
                device_id_type=mesh_ids,
            )
            copy.start()
            forwards.append(copy)

    forward(0, me, (k_ref.at[own_rows, own_cols], v_ref.at[own_rows, own_cols]))
    for step in range(1, sources):
        for copy in copies[2 * (step - 1) : 2 * step]:
            copy.wait()
        block = lax.rem(me + sources - step, sources)
        forward(step, block, (k_out.at[block, mine], v_out.at[block, mine]))
    for copy in forwards:
        copy.wait()


def seq_gather(scene_keys, scene_values, sources, head_width, collective):
    half = scene_keys.shape[0] // QPARTS
    vmem = pl.BlockSpec(memory_space=pltpu.VMEM)
    out = jax.ShapeDtypeStruct((sources, QPARTS, half, head_width), scene_keys.dtype)
    return pl.pallas_call(
        gather_kernel,
        out_shape=(out, out),
        in_specs=[vmem, vmem],
        out_specs=(vmem, vmem),
        scratch_shapes=[
            pltpu.SemaphoreType.DMA((2, sources)),
            pltpu.SemaphoreType.DMA((2, sources)),
            pltpu.SemaphoreType.DMA((2, sources)),
            pltpu.SemaphoreType.DMA((2, sources)),
        ],
        compiler_params=pltpu.CompilerParams(collective_id=collective, has_side_effects=True),
    )(scene_keys, scene_values)


def scatter_rows(rows, parts, collective):
    return grp_exchange(
        rows.reshape(parts, rows.shape[0] // parts, rows.shape[1]), parts, False, collective
    )


def broadcast_rows(chunk, parts, collective):
    gathered = grp_exchange(chunk, parts, True, collective)
    return gathered.reshape(parts * chunk.shape[0], chunk.shape[1])


def per_device(queries, scene_keys, scene_values, grad_output, tile_list, tile_counts):
    items_here = queries.shape[0]
    head_width = queries.shape[2]
    query_rows = queries.shape[1]
    scene_here = scene_keys.shape[0]
    heads_total = scene_keys.shape[1] // head_width
    seq_devices = lax.axis_size("seq")
    groups = lax.axis_size("grp")
    chunk_rows = query_rows // groups
    group_keys = scene_here * seq_devices
    copies = max(1, QPARTS // items_here)
    heads_here = max(1, items_here // QPARTS)
    softmax_scale = head_width ** (-0.5)
    half_keys = scene_here // QPARTS
    key_halves, value_halves = seq_gather(scene_keys, scene_values, seq_devices, head_width, 4)
    key_group = key_halves.reshape(group_keys, 1, head_width)
    value_group = value_halves.reshape(group_keys, 1, head_width)
    part_accum, stats = forward_item(
        queries[0],
        key_group[:, 0, :],
        value_group[:, 0, :],
        tile_list[0, 0],
        tile_counts[0, 0],
        softmax_scale,
        groups,
    )
    out_rows, out_stats = grp_combine(part_accum, stats, 0)
    attended = out_rows.reshape(1, query_rows, head_width)
    query_grad, key_grad, value_grad = backward_item(
        queries[0],
        key_group[:, 0, :],
        value_group[:, 0, :],
        grad_output[0],
        attended[0],
        out_stats,
        tile_list[0, 0],
        tile_counts[0, 0],
        softmax_scale,
    )
    grad_queries, grad_keys, grad_values = back_exchange(
        query_grad.reshape(groups, chunk_rows, head_width), key_grad, value_grad, groups, seq_devices, 2
    )
    grad_queries = grad_queries.reshape(1, query_rows, head_width)
    return (attended, grad_queries, grad_keys, grad_values)


def solution(mesh):
    in_specs = (
        P("seq", None, None),
        P(("grp", "seq"), None),
        P(("grp", "seq"), None),
        P("seq", None, None),
        P("grp", "seq", None, None),
        P("grp", "seq"),
    )
    out_specs = (
        P("seq", None, None),
        P("seq", None, None),
        P(("grp", "seq"), None),
        P(("grp", "seq"), None),
    )
    return jax.shard_map(
        per_device, mesh=mesh, in_specs=in_specs, out_specs=out_specs, check_vma=False
    )
```

```python
import jax
import jax.numpy as jnp
from jax import lax
from jax.experimental import pallas as pl
from jax.experimental.pallas import tpu as pltpu
from jax.sharding import PartitionSpec as P

QPARTS = 2
QBLK = 512
KBLK = 512


NEG_START = -1e30


LIST_SLOTS = 9


def tile_starts(list_ref, position):
    query_block = jnp.clip(list_ref[position, 0], 0, QPARTS - 1)
    key_block = jnp.clip(list_ref[position, 1], 0, 7)
    return (
        pl.multiple_of(query_block * QBLK, QBLK),
        pl.multiple_of(key_block * KBLK, KBLK),
    )


def forward_kernel(
    softmax_scale, list_ref, count_ref, q_ref, k_ref, v_ref, acc_out, stats_out, max_ref, total_ref, accum_ref
):
    max_ref[...] = jnp.full(max_ref.shape, NEG_START, jnp.float32)
    total_ref[...] = jnp.zeros(total_ref.shape, jnp.float32)
    accum_ref[...] = jnp.zeros(accum_ref.shape, jnp.float32)
    live_tiles = jnp.clip(count_ref[0], 0, LIST_SLOTS)

    def visit(position, carry):
        query_start, key_start = tile_starts(list_ref, position)
        rows = pl.ds(query_start, QBLK)
        keys = pl.ds(key_start, KBLK)
        scores = (
            lax.dot_general(
                q_ref[rows, :], k_ref[keys, :], (((1,), (1,)), ((), ())),
                preferred_element_type=jnp.float32,
            )
            * softmax_scale
        )
        old_max = max_ref[rows, :]
        new_max = jnp.maximum(old_max, jnp.max(scores, axis=1, keepdims=True))
        new_max = new_max.astype(jnp.bfloat16).astype(jnp.float32)
        weights = jnp.exp(scores - new_max[:, :1])
        shrink = jnp.exp(old_max - new_max)
        total_ref[rows, :] = total_ref[rows, :] * shrink + jnp.sum(weights, axis=1, keepdims=True)
        accum_ref[rows, :] = accum_ref[rows, :] * shrink[:, :1] + jnp.dot(
            weights.astype(jnp.bfloat16), v_ref[keys, :], preferred_element_type=jnp.float32
        )
        max_ref[rows, :] = new_max
        return carry

    lax.fori_loop(0, live_tiles, visit, 0)
    groups, chunk_rows = acc_out.shape[0], acc_out.shape[1]
    for g in range(groups):
        rows = pl.ds(g * chunk_rows, chunk_rows)
        acc_out[g] = accum_ref[rows, :].astype(acc_out.dtype)
        stacked = jnp.concatenate([max_ref[rows, :], total_ref[rows, :]], axis=0)
        stats_out[g] = jnp.transpose(stacked)[:8, :]


def forward_item(query_item, key_head, value_head, listing, live_tiles, softmax_scale, groups):
    query_rows, head_width = query_item.shape
    chunk_rows = query_rows // groups
    smem = pl.BlockSpec(memory_space=pltpu.SMEM)
    vmem = pl.BlockSpec(memory_space=pltpu.VMEM)
    rows_f32 = pltpu.VMEM((query_rows, head_width), jnp.float32)
    return pl.pallas_call(
        lambda *refs: forward_kernel(softmax_scale, *refs),
        out_shape=(
            jax.ShapeDtypeStruct((groups, chunk_rows, head_width), jnp.bfloat16),
            jax.ShapeDtypeStruct((groups, 8, 2 * chunk_rows), jnp.float32),
        ),
        in_specs=[smem, smem, vmem, vmem, vmem],
        out_specs=(vmem, vmem),
        scratch_shapes=[rows_f32, rows_f32, rows_f32],
    )(listing, live_tiles.reshape(1), query_item, key_head, value_head)


def backward_kernel(
    softmax_scale, list_ref, count_ref, q_ref, k_ref, v_ref, do_ref, att_ref, stats_ref,
    dq_ref, dk_ref, dv_ref, dq_acc, dk_acc, dv_acc, log_ref, delta_ref,
):
    groups = stats_ref.shape[0]
    chunk_rows = stats_ref.shape[2] // 2
    for g in range(groups):
        rows = pl.ds(g * chunk_rows, chunk_rows)
        columns = jnp.transpose(jnp.broadcast_to(stats_ref[g][0:1, :], (2 * chunk_rows, 2 * chunk_rows)))
        log_ref[rows, :] = columns[:chunk_rows, 0:1] + jnp.log(columns[chunk_rows:, 0:1])
        delta_ref[rows, :] = jnp.sum(
            att_ref[rows, :].astype(jnp.float32) * do_ref[rows, :].astype(jnp.float32),
            axis=1,
            keepdims=True,
        )
    dq_acc[...] = jnp.zeros(dq_acc.shape, jnp.float32)
    dk_acc[...] = jnp.zeros(dk_acc.shape, jnp.float32)
    dv_acc[...] = jnp.zeros(dv_acc.shape, jnp.float32)
    live_tiles = jnp.clip(count_ref[0], 0, LIST_SLOTS)

    def visit(position, carry):
        query_start, key_start = tile_starts(list_ref, position)
        rows = pl.ds(query_start, QBLK)
        keys = pl.ds(key_start, KBLK)
        query_block = q_ref[rows, :]
        grad_block = do_ref[rows, :]
        key_block = k_ref[keys, :]
        value_block = v_ref[keys, :]
        scores = (
            lax.dot_general(
                query_block, key_block, (((1,), (1,)), ((), ())),
                preferred_element_type=jnp.float32,
            )
            * softmax_scale
        )
        probs = jnp.exp(scores - log_ref[rows, :])
        probs_half = probs.astype(jnp.bfloat16)
        dv_acc[keys, :] += lax.dot_general(
            probs_half, grad_block, (((0,), (0,)), ((), ())), preferred_element_type=jnp.float32
        )
        prob_grad = lax.dot_general(
            grad_block, value_block, (((1,), (1,)), ((), ())), preferred_element_type=jnp.float32
        )
        score_grad = (probs * (prob_grad - delta_ref[rows, :])).astype(jnp.bfloat16)
        dq_acc[rows, :] += (
            jnp.dot(score_grad, key_block, preferred_element_type=jnp.float32) * softmax_scale
        )
        dk_acc[keys, :] += (
            lax.dot_general(
                score_grad, query_block, (((0,), (0,)), ((), ())),
                preferred_element_type=jnp.float32,
            )
            * softmax_scale
        )
        return carry

    lax.fori_loop(0, live_tiles, visit, 0)
    dq_ref[...] = dq_acc[...].astype(dq_ref.dtype)
    dk_ref[...] = dk_acc[...].astype(dk_ref.dtype)
    dv_ref[...] = dv_acc[...].astype(dv_ref.dtype)


def backward_item(
    query_item, key_head, value_head, grad_item, attended, stats, listing, live_tiles, softmax_scale,
):
    query_rows, head_width = query_item.shape
    key_rows = key_head.shape[0]
    smem = pl.BlockSpec(memory_space=pltpu.SMEM)
    vmem = pl.BlockSpec(memory_space=pltpu.VMEM)
    return pl.pallas_call(
        lambda *refs: backward_kernel(softmax_scale, *refs),
        out_shape=(
            jax.ShapeDtypeStruct((query_rows, head_width), jnp.bfloat16),
            jax.ShapeDtypeStruct((key_rows, head_width), jnp.bfloat16),
            jax.ShapeDtypeStruct((key_rows, head_width), jnp.bfloat16),
        ),
        in_specs=[smem, smem] + [vmem] * 6,
        out_specs=(vmem, vmem, vmem),
        scratch_shapes=[
            pltpu.VMEM((query_rows, head_width), jnp.float32),
            pltpu.VMEM((key_rows, head_width), jnp.float32),
            pltpu.VMEM((key_rows, head_width), jnp.float32),
            pltpu.VMEM((query_rows, 1), jnp.float32),
            pltpu.VMEM((query_rows, 1), jnp.float32),
        ],
    )(
        listing,
        live_tiles.reshape(1),
        query_item,
        key_head,
        value_head,
        grad_item,
        attended,
        stats,
    )


def exchange_kernel(broadcast, x_ref, y_ref, send_sem, recv_sem):
    groups = y_ref.shape[0]
    me = lax.axis_index("grp")
    lane = lax.axis_index("seq")
    mesh_ids = pl.DeviceIdType.MESH
    barrier = pltpu.get_barrier_semaphore()
    for step in range(1, groups):
        pl.semaphore_signal(
            barrier, inc=1, device_id=(lax.rem(me + step, groups), lane), device_id_type=mesh_ids
        )
    pl.semaphore_wait(barrier, groups - 1)
    copies = []
    for step in range(1, groups):
        target = lax.rem(me + step, groups)
        copy = pltpu.make_async_remote_copy(
            src_ref=x_ref if broadcast else x_ref.at[target],
            dst_ref=y_ref.at[me],
            send_sem=send_sem.at[step],
            recv_sem=recv_sem.at[step],
            device_id=(target, lane),
            device_id_type=mesh_ids,
        )
        copy.start()
        copies.append(copy)
    y_ref[me] = x_ref[...] if broadcast else x_ref[me]
    for copy in copies:
        copy.wait()


def grp_exchange(x, groups, broadcast, collective):
    out_shape = (groups,) + (x.shape if broadcast else x.shape[1:])
    vmem = pl.BlockSpec(memory_space=pltpu.VMEM)
    return pl.pallas_call(
        lambda *refs: exchange_kernel(broadcast, *refs),
        out_shape=jax.ShapeDtypeStruct(out_shape, x.dtype),
        in_specs=[vmem],
        out_specs=vmem,
        scratch_shapes=[pltpu.SemaphoreType.DMA((groups,)), pltpu.SemaphoreType.DMA((groups,))],
        compiler_params=pltpu.CompilerParams(collective_id=collective, has_side_effects=True),
    )(x)


def reduce_kernel(x_ref, y_ref, part_ref, send_sem, recv_sem, back_send, back_recv):
    groups = y_ref.shape[0]
    me = lax.axis_index("grp")
    lane = lax.axis_index("seq")
    mesh_ids = pl.DeviceIdType.MESH
    barrier = pltpu.get_barrier_semaphore()
    for step in range(1, groups):
        pl.semaphore_signal(
            barrier, inc=1, device_id=(lax.rem(me + step, groups), lane), device_id_type=mesh_ids
        )
    pl.semaphore_wait(barrier, groups - 1)
    copies = []
    for step in range(1, groups):
        target = lax.rem(me + step, groups)
        copy = pltpu.make_async_remote_copy(
            src_ref=x_ref.at[target],
            dst_ref=part_ref.at[me],
            send_sem=send_sem.at[step],
            recv_sem=recv_sem.at[step],
            device_id=(target, lane),
            device_id_type=mesh_ids,
        )
        copy.start()
        copies.append(copy)
    part_ref[me] = x_ref[me]
    for copy in copies:
        copy.wait()
    y_ref[me] = jnp.sum(part_ref[...].astype(jnp.float32), axis=0).astype(y_ref.dtype)
    copies = []
    for step in range(1, groups):
        target = lax.rem(me + step, groups)
        copy = pltpu.make_async_remote_copy(
            src_ref=y_ref.at[me],
            dst_ref=y_ref.at[me],
            send_sem=back_send.at[step],
            recv_sem=back_recv.at[step],
            device_id=(target, lane),
            device_id_type=mesh_ids,
        )
        copy.start()
        copies.append(copy)
    for copy in copies:
        copy.wait()


def grp_reduce(x, groups, collective):
    vmem = pl.BlockSpec(memory_space=pltpu.VMEM)
    sems = pltpu.SemaphoreType.DMA((groups,))
    return pl.pallas_call(
        reduce_kernel,
        out_shape=jax.ShapeDtypeStruct(x.shape, x.dtype),
        in_specs=[vmem],
        out_specs=vmem,
        scratch_shapes=[pltpu.VMEM(x.shape, x.dtype), sems, sems, sems, sems],
        compiler_params=pltpu.CompilerParams(collective_id=collective, has_side_effects=True),
    )(x)


def combine_kernel(
    acc_in, stats_in, out_ref, stats_out, acc_part, stats_part,
    send_acc, recv_acc, send_stats, recv_stats, back_send, back_recv, stat_send, stat_recv,
):
    groups, chunk_rows, head_width = out_ref.shape
    me = lax.axis_index("grp")
    lane = lax.axis_index("seq")
    mesh_ids = pl.DeviceIdType.MESH
    barrier = pltpu.get_barrier_semaphore()
    for step in range(1, groups):
        pl.semaphore_signal(
            barrier, inc=1, device_id=(lax.rem(me + step, groups), lane), device_id_type=mesh_ids
        )
    pl.semaphore_wait(barrier, groups - 1)
    copies = []
    for step in range(1, groups):
        target = lax.rem(me + step, groups)
        for source, landing, sent, got in (
            (acc_in, acc_part, send_acc, recv_acc),
            (stats_in, stats_part, send_stats, recv_stats),
        ):
            rows = pl.ds(0, 1) if source is stats_in else pl.ds(0, source.shape[1])
            copy = pltpu.make_async_remote_copy(
                src_ref=source.at[target, rows],
                dst_ref=landing.at[me, rows],
                send_sem=sent.at[step],
                recv_sem=got.at[step],
                device_id=(target, lane),
                device_id_type=mesh_ids,
            )
            copy.start()
            copies.append(copy)
    acc_part[me] = acc_in[me]
    stats_part[me] = stats_in[me]
    for copy in copies:
        copy.wait()
    columns = jnp.transpose(stats_part[...].reshape(groups * 8, 128))
    maxima = [columns[:chunk_rows, 8 * g : 8 * g + 1] for g in range(groups)]
    totals = [columns[chunk_rows:, 8 * g : 8 * g + 1] for g in range(groups)]
    top = maxima[0]
    for g in range(1, groups):
        top = jnp.maximum(top, maxima[g])
    row_total = jnp.zeros_like(top)
    row_accum = jnp.zeros((chunk_rows, head_width), jnp.float32)
    for g in range(groups):
        shrink = jnp.exp(maxima[g] - top)
        row_total = row_total + totals[g] * shrink
        row_accum = row_accum + acc_part[g].astype(jnp.float32) * shrink
    out_ref[me] = (row_accum / row_total).astype(out_ref.dtype)
    spread = jnp.concatenate(
        [jnp.broadcast_to(top, (chunk_rows, 128)), jnp.broadcast_to(row_total, (chunk_rows, 128))], axis=0
    )
    stats_out[me] = jnp.transpose(spread)[:8, :]
    copies = []
    for step in range(1, groups):
        target = lax.rem(me + step, groups)
        for source, sent, got in ((out_ref, back_send, back_recv), (stats_out, stat_send, stat_recv)):
            rows = pl.ds(0, 1) if source is stats_out else pl.ds(0, source.shape[1])
            copy = pltpu.make_async_remote_copy(
                src_ref=source.at[me, rows],
                dst_ref=source.at[me, rows],
                send_sem=sent.at[step],
                recv_sem=got.at[step],
                device_id=(target, lane),
                device_id_type=mesh_ids,
            )
            copy.start()
            copies.append(copy)
    for copy in copies:
        copy.wait()


def grp_combine(accum, stats, collective):
    groups = accum.shape[0]
    vmem = pl.BlockSpec(memory_space=pltpu.VMEM)
    sems = pltpu.SemaphoreType.DMA((groups,))
    return pl.pallas_call(
        combine_kernel,
        out_shape=(
            jax.ShapeDtypeStruct(accum.shape, accum.dtype),
            jax.ShapeDtypeStruct(stats.shape, stats.dtype),
        ),
        in_specs=[vmem, vmem],
        out_specs=(vmem, vmem),
        scratch_shapes=[pltpu.VMEM(accum.shape, accum.dtype), pltpu.VMEM(stats.shape, stats.dtype)]
        + [sems] * 8,
        compiler_params=pltpu.CompilerParams(collective_id=collective, has_side_effects=True),
    )(accum, stats)


def back_kernel(
    dq_in, dk_in, dv_in, dq_out, gk_out, gv_out, part_ref, recv_k, recv_v,
    send_sem, recv_sem, back_send, back_recv, kv_send, kv_recv,
):
    groups = dq_out.shape[0]
    sources, block, head_width = recv_k.shape
    me = lax.axis_index("grp")
    lane = lax.axis_index("seq")
    mesh_ids = pl.DeviceIdType.MESH
    barrier = pltpu.get_barrier_semaphore()
    for step in range(1, groups):
        pl.semaphore_signal(
            barrier, inc=1, device_id=(lax.rem(me + step, groups), lane), device_id_type=mesh_ids
        )
    for step in range(1, sources):
        pl.semaphore_signal(
            barrier, inc=1, device_id=(me, lax.rem(lane + step, sources)), device_id_type=mesh_ids
        )
    pl.semaphore_wait(barrier, groups - 1 + sources - 1)
    returns = []
    for step in range(1, sources):
        target = lax.rem(lane + step, sources)
        rows = pl.ds(pl.multiple_of(target * block, block), block)
        for index, (source, landing) in enumerate(((dk_in, recv_k), (dv_in, recv_v))):
            copy = pltpu.make_async_remote_copy(
                src_ref=source.at[rows],
                dst_ref=landing.at[lane],
                send_sem=kv_send.at[index, step],
                recv_sem=kv_recv.at[index, step],
                device_id=(me, target),
                device_id_type=mesh_ids,
            )
            copy.start()
            returns.append(copy)
    copies = []
    for step in range(1, groups):
        target = lax.rem(me + step, groups)
        copy = pltpu.make_async_remote_copy(
            src_ref=dq_in.at[target],
            dst_ref=part_ref.at[me],
            send_sem=send_sem.at[step],
            recv_sem=recv_sem.at[step],
            device_id=(target, lane),
            device_id_type=mesh_ids,
        )
        copy.start()
        copies.append(copy)
    own_rows = pl.ds(pl.multiple_of(lane * block, block), block)
    recv_k[lane] = dk_in[own_rows, :]
    recv_v[lane] = dv_in[own_rows, :]
    part_ref[me] = dq_in[me]
    for copy in copies:
        copy.wait()
    dq_out[me] = jnp.sum(part_ref[...].astype(jnp.float32), axis=0).astype(dq_out.dtype)
    copies = []
    for step in range(1, groups):
        target = lax.rem(me + step, groups)
        copy = pltpu.make_async_remote_copy(
            src_ref=dq_out.at[me],
            dst_ref=dq_out.at[me],
            send_sem=back_send.at[step],
            recv_sem=back_recv.at[step],
            device_id=(target, lane),
            device_id_type=mesh_ids,
        )
        copy.start()
        copies.append(copy)
    for copy in returns:
        copy.wait()
    for head in range(sources // 2):
        cols = pl.ds(head * head_width, head_width)
        for landing, out_ref in ((recv_k, gk_out), (recv_v, gv_out)):
            out_ref[:, cols] = (
                landing[2 * head].astype(jnp.float32) + landing[2 * head + 1].astype(jnp.float32)
            ).astype(out_ref.dtype)
    for copy in copies:
        copy.wait()


def back_exchange(query_grad, key_grad, value_grad, groups, sources, collective):
    head_width = query_grad.shape[-1]
    block = key_grad.shape[0] // sources
    vmem = pl.BlockSpec(memory_space=pltpu.VMEM)
    grad_shape = jax.ShapeDtypeStruct((block, sources // 2 * head_width), key_grad.dtype)
    sems = pltpu.SemaphoreType.DMA((groups,))
    return pl.pallas_call(
        back_kernel,
        out_shape=(jax.ShapeDtypeStruct(query_grad.shape, query_grad.dtype), grad_shape, grad_shape),
        in_specs=[vmem, vmem, vmem],
        out_specs=(vmem, vmem, vmem),
        scratch_shapes=[
            pltpu.VMEM(query_grad.shape, query_grad.dtype),
            pltpu.VMEM((sources, block, head_width), key_grad.dtype),
            pltpu.VMEM((sources, block, head_width), key_grad.dtype),
            sems,
            sems,
            sems,
            sems,
            pltpu.SemaphoreType.DMA((2, sources)),
            pltpu.SemaphoreType.DMA((2, sources)),
        ],
        compiler_params=pltpu.CompilerParams(collective_id=collective, has_side_effects=True),
    )(query_grad, key_grad, value_grad)


def gather_kernel(k_ref, v_ref, k_out, v_out, send_sem, recv_sem, pair_send, pair_recv):
    sources, halves, half, head_width = k_out.shape
    me = lax.axis_index("seq")
    grp_here = lax.axis_index("grp")
    mine = lax.rem(me, 2)
    partner = me + 1 - 2 * mine
    head = me // 2
    mesh_ids = pl.DeviceIdType.MESH
    barrier = pltpu.get_barrier_semaphore()
    for step in range(1, sources):
        pl.semaphore_signal(
            barrier, inc=1, device_id=(grp_here, lax.rem(me + step, sources)), device_id_type=mesh_ids
        )
    pl.semaphore_wait(barrier, sources - 1)
    copies = []
    for step in range(1, sources):
        target = lax.rem(me + step, sources)
        rows = pl.ds(pl.multiple_of(lax.rem(target, 2) * half, half), half)
        cols = pl.ds(pl.multiple_of((target // 2) * head_width, head_width), head_width)
        for index, (source, landing) in enumerate(((k_ref, k_out), (v_ref, v_out))):
            copy = pltpu.make_async_remote_copy(
                src_ref=source.at[rows, cols],
                dst_ref=landing.at[me, lax.rem(target, 2)],
                send_sem=send_sem.at[index, step],
                recv_sem=recv_sem.at[index, step],
                device_id=(grp_here, target),
                device_id_type=mesh_ids,
            )
            copy.start()
            copies.append(copy)
    own_rows = pl.ds(pl.multiple_of(mine * half, half), half)
    own_cols = pl.ds(pl.multiple_of(head * head_width, head_width), head_width)
    k_out[me, mine] = k_ref[own_rows, own_cols]
    v_out[me, mine] = v_ref[own_rows, own_cols]
    forwards = []

    def forward(step, block, sources_of):
        for index, (landing, source) in enumerate(zip((k_out, v_out), sources_of)):
            copy = pltpu.make_async_remote_copy(
                src_ref=source,
                dst_ref=landing.at[block, mine],
                send_sem=pair_send.at[index, step],
                recv_sem=pair_recv.at[index, step],
                device_id=(grp_here, partner),
                device_id_type=mesh_ids,
            )
            copy.start()
            forwards.append(copy)

    forward(0, me, (k_ref.at[own_rows, own_cols], v_ref.at[own_rows, own_cols]))
    for step in range(1, sources):
        for copy in copies[2 * (step - 1) : 2 * step]:
            copy.wait()
        block = lax.rem(me + sources - step, sources)
        forward(step, block, (k_out.at[block, mine], v_out.at[block, mine]))
    for copy in forwards:
        copy.wait()


def seq_gather(scene_keys, scene_values, sources, head_width, collective):
    half = scene_keys.shape[0] // QPARTS
    vmem = pl.BlockSpec(memory_space=pltpu.VMEM)
    out = jax.ShapeDtypeStruct((sources, QPARTS, half, head_width), scene_keys.dtype)
    return pl.pallas_call(
        gather_kernel,
        out_shape=(out, out),
        in_specs=[vmem, vmem],
        out_specs=(vmem, vmem),
        scratch_shapes=[
            pltpu.SemaphoreType.DMA((2, sources)),
            pltpu.SemaphoreType.DMA((2, sources)),
            pltpu.SemaphoreType.DMA((2, sources)),
            pltpu.SemaphoreType.DMA((2, sources)),
        ],
        compiler_params=pltpu.CompilerParams(collective_id=collective, has_side_effects=True),
    )(scene_keys, scene_values)


def scatter_rows(rows, parts, collective):
    return grp_exchange(
        rows.reshape(parts, rows.shape[0] // parts, rows.shape[1]), parts, False, collective
    )


def broadcast_rows(chunk, parts, collective):
    gathered = grp_exchange(chunk, parts, True, collective)
    return gathered.reshape(parts * chunk.shape[0], chunk.shape[1])


def per_device(queries, scene_keys, scene_values, grad_output, tile_list, tile_counts):
    items_here = queries.shape[0]
    head_width = queries.shape[2]
    query_rows = queries.shape[1]
    scene_here = scene_keys.shape[0]
    heads_total = scene_keys.shape[1] // head_width
    seq_devices = lax.axis_size("seq")
    groups = lax.axis_size("grp")
    chunk_rows = query_rows // groups
    group_keys = scene_here * seq_devices
    copies = max(1, QPARTS // items_here)
    heads_here = max(1, items_here // QPARTS)
    softmax_scale = head_width ** (-0.5)
    half_keys = scene_here // QPARTS
    key_halves, value_halves = seq_gather(scene_keys, scene_values, seq_devices, head_width, 4)
    key_group = key_halves.reshape(group_keys, 1, head_width)
    value_group = value_halves.reshape(group_keys, 1, head_width)
    part_accum, stats = forward_item(
        queries[0],
        key_group[:, 0, :],
        value_group[:, 0, :],
        tile_list[0, 0],
        tile_counts[0, 0],
        softmax_scale,
        groups,
    )
    out_rows, out_stats = grp_combine(part_accum, stats, 0)
    attended = out_rows.reshape(1, query_rows, head_width)
    query_grad, key_grad, value_grad = backward_item(
        queries[0],
        key_group[:, 0, :],
        value_group[:, 0, :],
        grad_output[0],
        attended[0],
        out_stats,
        tile_list[0, 0],
        tile_counts[0, 0],
        softmax_scale,
    )
    grad_queries, grad_keys, grad_values = back_exchange(
        query_grad.reshape(groups, chunk_rows, head_width), key_grad, value_grad, groups, seq_devices, 2
    )
    grad_queries = grad_queries.reshape(1, query_rows, head_width)
    return (attended, grad_queries, grad_keys, grad_values)


def solution(mesh):
    in_specs = (
        P("seq", None, None),
        P(("grp", "seq"), None),
        P(("grp", "seq"), None),
        P("seq", None, None),
        P("grp", "seq", None, None),
        P("grp", "seq"),
    )
    out_specs = (
        P("seq", None, None),
        P("seq", None, None),
        P(("grp", "seq"), None),
        P(("grp", "seq"), None),
    )
    return jax.shard_map(
        per_device, mesh=mesh, in_specs=in_specs, out_specs=out_specs, check_vma=False
    )
```
